32 devices in a mesh: gx: 4 (over y, x), gy: 8 (over z, core).
Axes of the slice: x: 2, y: 2, z: 4, core: 2. Of those that a mesh axis runs over, the one named last changes fastest.
Arguments:
- inputs: bfloat16 [32, 32, 32, 256], P(None, 'gx', 'gy'), may hold values from -6 to 6
- pre_act: bfloat16 [32, 32, 32, 256], P(None, 'gx', 'gy'), may hold values from -8 to 8
- grad_out: bfloat16 [32, 32, 32, 256], P(None, 'gx', 'gy'), may hold values from -6 to 6
- point_weight: float32 [32, 32], replicated, may hold values from -1 to 1
- mode_weight: float32 [32, 32, 2, 16, 1024], P('gx', 'gy'), may hold values from -12 to 12
Outputs:
- input_grad: float32 [32, 32, 32, 256], P(None, 'gx', 'gy')
- point_grad: float32 [32, 32], replicated
- bias_grad: float32 [32], replicated
- mode_grad: float32 [32, 32, 2, 16, 1024], P('gx', 'gy')
The draws below stay inside these ranges and needn't reach their ends.
All inputs are finite; a program needn't handle non-finite values.
Results may differ from the reference program's by a relative error of at most 0.0003.
Values sent between devices are 32-bit elements; how exact they have to be, the bound alone decides.
No kernel may reach another device: no remote copies, remote signals or barrier semaphores. Data moves between devices by JAX's collectives and lax.ppermute only.
A program may use at most 64 MiB of HBM per device.

```python
import math
import jax
import jax.numpy as jnp
from jax import lax

C = 32
KX = 32
KY = 32
KZ = 16
Z = 256
X = 32
Y = 32


def levels(stream_key, shape, cuts, least, high):
    factor_of, own = 1.0, jax.random.fold_in(stream_key, 6)
    for position, blocks in cuts:
        draws = jnp.exp(jax.random.uniform(jax.random.fold_in(own, position), (blocks,), jnp.float32, least / len(cuts), high / len(cuts)))
        factor_of = factor_of * jnp.repeat(draws, shape[position] // blocks).reshape([-1 if axis == position else 1 for axis in range(len(shape))])
    return factor_of


def centred(key, extent, width, bound, shards=(), kind=jnp.bfloat16):
    result = jax.random.normal(key, extent, jnp.float32) * width
    if len(shards) > 0:
        result = levels(key, extent, shards, -0.22, 0.18) * result
    return jnp.clip(result, min=-bound, max=bound).astype(kind)


def setup_inputs(seed: int = 0) -> dict:
    seeds = jax.random.split(jax.random.key(seed), 6)
    return {
        "inputs": centred(seeds[0], (C, X, Y, Z), 1.0, 6.0, ((1, 4), (2, 8))),
        "pre_act": centred(seeds[1], (C, X, Y, Z), 1.5, 8.0, ((1, 4), (2, 8))),
        "grad_out": centred(seeds[2], (C, X, Y, Z), 1.0, 6.0, ((1, 4), (2, 8))),
        "point_weight": centred(seeds[3], (C, C), C ** -0.5, 1.0, (), jnp.float32),
        "mode_weight": centred(seeds[4], (KX, KY, 2, KZ, C * C), 2.0, 12.0, ((0, 4), (1, 8)), jnp.float32),
    }


HIGHEST_PRECISION = lax.Precision.HIGHEST
ROOT_HALF = 0.7071067811865476
NORMAL_PEAK = 0.3989422804014327

def gelu_slope(pre_act):
    value = pre_act.astype(jnp.float32)
    return 0.5 * (1.0 + jax.scipy.special.erf(value * ROOT_HALF)) + value * jnp.exp(-0.5 * value * value) * NORMAL_PEAK

def phases(length, modes, wrapped, index, first, count):
    if wrapped:
        frequency = jnp.where(index < modes // 2, index, index + (length - modes))
    else:
        frequency = index
    places = first + jnp.arange(count, dtype=jnp.int32)
    turns = frequency[:, None] * places[None, :] % length
    angle = turns.astype(jnp.float32) * (2.0 * math.pi / length)
    return (jnp.cos(angle), jnp.sin(angle))

def transform(cos_table, sin_table, data, sign):
    real_part = data[..., 0, :]
    imag_part = data[..., 1, :]

    def apply(table, values):
        return jnp.tensordot(table, values, axes=1, precision=HIGHEST_PRECISION)
    if sign < 0:
        out_real = apply(cos_table, real_part) + apply(sin_table, imag_part)
        out_imag = apply(cos_table, imag_part) - apply(sin_table, real_part)
    else:
        out_real = apply(cos_table, real_part) - apply(sin_table, imag_part)
        out_imag = apply(cos_table, imag_part) + apply(sin_table, real_part)
    return jnp.stack([out_real, out_imag], axis=-2)

def depth_forward(field, kz_count):
    channels = field.shape[0]
    depth = field.shape[-1]
    cos_z, sin_z = phases(depth, kz_count, False, jnp.arange(kz_count, dtype=jnp.int32), 0, depth)
    real_part = jnp.einsum('cabz,kz->abkc', field, cos_z, precision=HIGHEST_PRECISION)
    imag_part = -jnp.einsum('cabz,kz->abkc', field, sin_z, precision=HIGHEST_PRECISION)
    lead = real_part.shape[:2]
    return jnp.stack([real_part.reshape(lead + (kz_count * channels,)), imag_part.reshape(lead + (kz_count * channels,))], axis=2)

def depth_inverse(spectrum, kz_count, channels, depth):
    lead = spectrum.shape[:2]
    split = spectrum.reshape(lead + (2, kz_count, channels))
    cos_z, sin_z = phases(depth, kz_count, False, jnp.arange(kz_count, dtype=jnp.int32), 0, depth)
    return jnp.einsum('abkc,kz->cabz', split[:, :, 0], cos_z, precision=HIGHEST_PRECISION) - jnp.einsum('abkc,kz->cabz', split[:, :, 1], sin_z, precision=HIGHEST_PRECISION)

def mode_work(spectrum_in, spectrum_grad, weight, cells):
    rows_a, rows_b, _, kz_count, _ = weight.shape
    channels = spectrum_in.shape[-1] // kz_count
    factor = jnp.where(jnp.arange(kz_count, dtype=jnp.int32) == 0, 1.0, 2.0).astype(jnp.float32) / cells
    shape = (rows_a, rows_b, 2, kz_count, channels)
    given = spectrum_in.reshape(shape)
    scaled = spectrum_grad.reshape(shape) * factor[:, None]
    mixing = weight.reshape(shape + (channels,))
    in_real = given[:, :, 0]
    in_imag = given[:, :, 1]
    grad_real = scaled[:, :, 0]
    grad_imag = scaled[:, :, 1]
    mix_real = mixing[:, :, 0]
    mix_imag = mixing[:, :, 1]

    def outer(left, right):
        return jnp.einsum('abki,abko->abkio', left, right, precision=HIGHEST_PRECISION)

    def mixed(values, matrix):
        return jnp.einsum('abko,abkio->abki', values, matrix, precision=HIGHEST_PRECISION)
    result_real = outer(in_real, grad_real) + outer(in_imag, grad_imag)
    result_imag = outer(in_real, grad_imag) - outer(in_imag, grad_real)
    mode_grad = jnp.stack([result_real, result_imag], axis=2).reshape(rows_a, rows_b, 2, kz_count, channels * channels)
    back_real = mixed(grad_real, mix_real) + mixed(grad_imag, mix_imag)
    back_imag = mixed(grad_imag, mix_real) - mixed(grad_real, mix_imag)
    back_spectrum = jnp.stack([back_real, back_imag], axis=2).reshape(rows_a, rows_b, 2, kz_count * channels)
    return (mode_grad, back_spectrum)

def reference(inputs, pre_act, grad_out, point_weight, mode_weight):
    cells = X * Y * Z
    scale = 1.0 / math.sqrt(cells)

    def plane_terms(place):
        field_in = lax.dynamic_slice_in_dim(inputs, place, 1, 1).astype(jnp.float32)
        pre_plane = lax.dynamic_slice_in_dim(pre_act, place, 1, 1)
        grad_plane = lax.dynamic_slice_in_dim(grad_out, place, 1, 1)
        pre_grad = grad_plane.astype(jnp.float32) * gelu_slope(pre_plane)
        weight_sum = jnp.einsum('iabz,oabz->io', field_in, pre_grad, precision=HIGHEST_PRECISION)
        bias_sum = lax.optimization_barrier(jnp.sum(pre_grad, axis=(1, 2, 3)))
        both = jnp.stack([depth_forward(field_in, KZ), depth_forward(pre_grad, KZ)], axis=2)
        return (weight_sum, bias_sum, both[0])
    weight_sums, bias_sums, spectra = lax.map(plane_terms, jnp.arange(X, dtype=jnp.int32))
    cos_y, sin_y = phases(Y, KY, True, jnp.arange(KY, dtype=jnp.int32), 0, Y)
    cos_x, sin_x = phases(X, KX, True, jnp.arange(KX, dtype=jnp.int32), 0, X)
    along_y = transform(cos_y, sin_y, jnp.swapaxes(spectra, 0, 1), -1)
    owned = transform(cos_x, sin_x, jnp.swapaxes(along_y, 0, 1), -1)
    mode_grad, back_spectrum = mode_work(owned[:, :, 0], owned[:, :, 1], mode_weight, cells)
    near = transform(cos_x.T, sin_x.T, back_spectrum, 1)
    spread = jnp.swapaxes(transform(cos_y.T, sin_y.T, jnp.swapaxes(near, 0, 1), 1), 0, 1)

    def plane_grad(place):
        pre_plane = lax.dynamic_slice_in_dim(pre_act, place, 1, 1)
        grad_plane = lax.dynamic_slice_in_dim(grad_out, place, 1, 1)
        pre_grad = grad_plane.astype(jnp.float32) * gelu_slope(pre_plane)
        local = jnp.einsum('io,oabz->iabz', point_weight, pre_grad, precision=HIGHEST_PRECISION)
        layer = lax.dynamic_slice_in_dim(spread, place, 1, 0)
        return (local + depth_inverse(layer, KZ, C, Z))[:, 0]
    input_grad = jnp.swapaxes(lax.map(plane_grad, jnp.arange(X, dtype=jnp.int32)), 0, 1)
    point_grad = lax.optimization_barrier(jnp.sum(weight_sums, axis=0)) * scale
    bias_grad = lax.optimization_barrier(jnp.sum(bias_sums, axis=0)) * scale
    return (input_grad, point_grad, bias_grad, mode_grad)
```

```python
import math

import jax
import jax.numpy as jnp
import numpy as np
from jax import lax
from jax.experimental import pallas as pl
from jax.experimental.pallas import tpu as pltpu
from jax.sharding import PartitionSpec as P

HIGHEST_PRECISION = lax.Precision.HIGHEST
ROOT_HALF = 0.7071067811865476
NORMAL_PEAK = 0.3989422804014327


def gelu_slope(pre_act):
    value = pre_act.astype(jnp.float32)
    return (
        0.5 * (1.0 + jax.scipy.special.erf(value * ROOT_HALF))
        + value * jnp.exp(-0.5 * value * value) * NORMAL_PEAK
    )


def phases(length, modes, wrapped, index, first, count):
    if wrapped:
        frequency = jnp.where(index < modes // 2, index, index + (length - modes))
    else:
        frequency = index
    places = first + jnp.arange(count, dtype=jnp.int32)
    turns = frequency[:, None] * places[None, :] % length
    angle = turns.astype(jnp.float32) * (2.0 * math.pi / length)
    return (jnp.cos(angle), jnp.sin(angle))


def transform(cos_table, sin_table, data, sign):
    real_part = data[..., 0, :]
    imag_part = data[..., 1, :]

    def apply(table, values):
        return jnp.tensordot(table, values, axes=1, precision=HIGHEST_PRECISION)

    if sign < 0:
        out_real = apply(cos_table, real_part) + apply(sin_table, imag_part)
        out_imag = apply(cos_table, imag_part) - apply(sin_table, real_part)
    else:
        out_real = apply(cos_table, real_part) - apply(sin_table, imag_part)
        out_imag = apply(cos_table, imag_part) + apply(sin_table, real_part)
    return jnp.stack([out_real, out_imag], axis=-2)


def depth_forward(field, kz_count):
    channels = field.shape[0]
    depth = field.shape[-1]
    cos_z, sin_z = phases(depth, kz_count, False, jnp.arange(kz_count, dtype=jnp.int32), 0, depth)
    real_part = jnp.einsum("cabz,kz->abkc", field, cos_z, precision=HIGHEST_PRECISION)
    imag_part = -jnp.einsum("cabz,kz->abkc", field, sin_z, precision=HIGHEST_PRECISION)
    lead = real_part.shape[:2]
    return jnp.stack(
        [
            real_part.reshape(lead + (kz_count * channels,)),
            imag_part.reshape(lead + (kz_count * channels,)),
        ],
        axis=2,
    )


def depth_inverse(spectrum, kz_count, channels, depth):
    lead = spectrum.shape[:2]
    split = spectrum.reshape(lead + (2, kz_count, channels))
    cos_z, sin_z = phases(depth, kz_count, False, jnp.arange(kz_count, dtype=jnp.int32), 0, depth)
    return jnp.einsum(
        "abkc,kz->cabz", split[:, :, 0], cos_z, precision=HIGHEST_PRECISION
    ) - jnp.einsum("abkc,kz->cabz", split[:, :, 1], sin_z, precision=HIGHEST_PRECISION)


def mode_work(spectrum_in, spectrum_grad, weight, cells):
    rows_a, rows_b, _, kz_count, _ = weight.shape
    channels = spectrum_in.shape[-1] // kz_count
    factor = (
        jnp.where(jnp.arange(kz_count, dtype=jnp.int32) == 0, 1.0, 2.0).astype(jnp.float32) / cells
    )
    shape = (rows_a, rows_b, 2, kz_count, channels)
    given = spectrum_in.reshape(shape)
    scaled = spectrum_grad.reshape(shape) * factor[:, None]
    mixing = weight.reshape(shape + (channels,))
    in_real = given[:, :, 0]
    in_imag = given[:, :, 1]
    grad_real = scaled[:, :, 0]
    grad_imag = scaled[:, :, 1]
    mix_real = mixing[:, :, 0]
    mix_imag = mixing[:, :, 1]

    def outer(left, right):
        return jnp.einsum("abki,abko->abkio", left, right, precision=HIGHEST_PRECISION)

    def mixed(values, matrix):
        return jnp.einsum("abko,abkio->abki", values, matrix, precision=HIGHEST_PRECISION)

    result_real = outer(in_real, grad_real) + outer(in_imag, grad_imag)
    result_imag = outer(in_real, grad_imag) - outer(in_imag, grad_real)
    mode_grad = jnp.stack([result_real, result_imag], axis=2).reshape(
        rows_a, rows_b, 2, kz_count, channels * channels
    )
    back_real = mixed(grad_real, mix_real) + mixed(grad_imag, mix_imag)
    back_imag = mixed(grad_imag, mix_real) - mixed(grad_real, mix_imag)
    back_spectrum = jnp.stack([back_real, back_imag], axis=2).reshape(
        rows_a, rows_b, 2, kz_count * channels
    )
    return (mode_grad, back_spectrum)


def joined_rows(main, extra):
    count = main.shape[0]
    return jnp.concatenate([main.reshape(count, -1), extra.reshape(count, -1)], axis=1)


def split_rows(result, main_shape, extra_shape):
    main_size = 1
    for item in main_shape[1:]:
        main_size = main_size * item
    main = result[:, :main_size].reshape(main_shape)
    extra = result[:, main_size:].reshape(extra_shape)
    return (main, extra)


def partial_sums(inputs, pre_act, grad_out, point_weight, mode_weight):
    channels, x_local, y_local, depth = inputs.shape
    kx_local, ky_local, _, kz_count, _ = mode_weight.shape
    x_devices = lax.axis_size("gx")
    y_devices = lax.axis_size("gy")
    x_length = x_local * x_devices
    y_length = y_local * y_devices
    kx_count = kx_local * x_devices
    ky_count = ky_local * y_devices
    cells = x_length * y_length * depth
    scale = 1.0 / math.sqrt(cells)
    x_offset = lax.axis_index("gx") * x_local
    y_offset = lax.axis_index("gy") * y_local
    width = kz_count * channels
    pair_width = 2 * width
    stat_count = channels * channels + channels
    mode_count = kx_count * ky_count
    field_in = inputs.astype(jnp.float32)
    pre_grad = grad_out.astype(jnp.float32) * gelu_slope(pre_act)
    weight_sum = jnp.einsum("ixyz,oxyz->io", field_in, pre_grad, precision=HIGHEST_PRECISION)
    bias_sum = jnp.sum(pre_grad, axis=(1, 2, 3))
    extra_cols = (stat_count + mode_count - 1) // mode_count
    stat_flat = jnp.concatenate([weight_sum.reshape(-1), bias_sum])
    grid = jnp.pad(stat_flat, (0, mode_count * extra_cols - stat_count)).reshape(
        kx_count, ky_count, extra_cols
    )
    spectra = jnp.stack(
        [depth_forward(field_in, kz_count), depth_forward(pre_grad, kz_count)], axis=2
    )
    along_y = jnp.swapaxes(spectra, 0, 1)
    grid_y = jnp.swapaxes(grid, 0, 1)
    cos_y, sin_y = phases(
        y_length,
        ky_count,
        True,
        jnp.arange(lax.axis_size("gy") * ky_local, dtype=jnp.int32),
        y_offset,
        y_local,
    )
    partial_y, extra_y = split_rows(
        lax.psum_scatter(
            joined_rows(transform(cos_y, sin_y, along_y, -1), grid_y),
            "gy",
            scatter_dimension=0,
            tiled=True,
        ),
        (ky_local, x_local, 2, 2, width),
        (ky_local, kx_count, extra_cols),
    )
    along_x = jnp.swapaxes(partial_y, 0, 1)
    extra_along = jnp.swapaxes(extra_y, 0, 1)
    cos_x, sin_x = phases(
        x_length,
        kx_count,
        True,
        jnp.arange(lax.axis_size("gx") * kx_local, dtype=jnp.int32),
        x_offset,
        x_local,
    )
    owned, owned_extra = split_rows(
        lax.psum_scatter(
            joined_rows(transform(cos_x, sin_x, along_x, -1), extra_along),
            "gx",
            scatter_dimension=0,
            tiled=True,
        ),
        (kx_local, ky_local, 2, 2, width),
        (kx_local, ky_local, extra_cols),
    )
    mode_grad, back_spectrum = mode_work(owned[:, :, 0], owned[:, :, 1], mode_weight, cells)
    back_joined = jnp.concatenate(
        [back_spectrum.reshape(kx_local, ky_local, pair_width), owned_extra], axis=2
    )
    piece = lax.all_gather(back_joined, "gx", axis=0, tiled=True)
    kx_index = jnp.arange(piece.shape[0], dtype=jnp.int32)
    cos_x, sin_x = phases(x_length, kx_count, True, kx_index, x_offset, x_local)
    main = piece[:, :, :pair_width].reshape(piece.shape[0], piece.shape[1], 2, width)
    near = transform(cos_x.T, sin_x.T, main, 1)
    near_stats = piece[:, :, pair_width:]
    side_cols = (kx_count * extra_cols + x_local - 1) // x_local
    side_flat = jnp.swapaxes(near_stats, 0, 1).reshape(ky_local, kx_count * extra_cols)
    side = jnp.swapaxes(side_flat.reshape(ky_local, x_local, side_cols), 0, 1)
    near_joined = jnp.concatenate([near.reshape(x_local, ky_local, pair_width), side], axis=2)
    piece = lax.all_gather(near_joined, "gy", axis=1, tiled=True)
    ky_index = jnp.arange(piece.shape[1], dtype=jnp.int32)
    cos_y, sin_y = phases(y_length, ky_count, True, ky_index, y_offset, y_local)
    main = piece[:, :, :pair_width].reshape(piece.shape[0], piece.shape[1], 2, width)
    moved = jnp.swapaxes(transform(cos_y.T, sin_y.T, jnp.swapaxes(main, 0, 1), 1), 0, 1)
    far_stats = piece[:, :, pair_width:]
    stats_rows = jnp.swapaxes(far_stats, 0, 1).reshape(ky_count, x_local * side_cols)
    stats_grid = jnp.swapaxes(stats_rows.reshape(ky_count, kx_count, extra_cols), 0, 1)
    stat_values = stats_grid.reshape(-1)[:stat_count]
    point_grad = stat_values[: channels * channels].reshape(channels, channels)
    bias_grad = stat_values[channels * channels :]
    local = jnp.einsum("io,oxyz->ixyz", point_weight, pre_grad, precision=HIGHEST_PRECISION)
    input_grad = local + depth_inverse(moved, kz_count, channels, depth)
    return (input_grad, point_grad * scale, bias_grad * scale, mode_grad)


LANES = 128
SUBLANES = 8
HL = 8
BF16 = jnp.bfloat16
F32 = jnp.float32


def split_table(table):
    high = table.astype(np.float32).astype(BF16)
    low = (table - high.astype(np.float64)).astype(np.float32).astype(BF16)
    return (high, low)


def split(values):
    high = values.astype(BF16)
    return (high, (values - high.astype(F32)).astype(BF16))


def dot(left, right):
    return jnp.dot(left, right, preferred_element_type=F32)


def dot_rows(left, right):
    return lax.dot_general(left, right, (((1,), (1,)), ((), ())), preferred_element_type=F32)


def product(left, right, multiply=dot):
    return (
        multiply(left[0], right[0]) + multiply(left[0], right[1]) + multiply(left[1], right[0])
    )


def iota(shape, axis):
    return lax.broadcasted_iota(jnp.int32, shape, axis)


def wave(length, modes):
    index = np.arange(modes)
    frequency = np.where(index < modes // 2, index, index + (length - modes))
    turns = frequency[:, None] * np.arange(length)[None, :] % length
    angle = turns * (2.0 * math.pi / length)
    return (np.cos(angle), np.sin(angle))


def depth_table(depth, kz_count, x_local):
    h = np.arange(kz_count)
    angle = (h[None, :] * np.arange(LANES)[:, None] % depth) * (2.0 * math.pi / depth)
    both = np.stack([np.cos(angle), -np.sin(angle)], axis=1)
    both = both.reshape(LANES, 2, kz_count // HL, 1, HL).transpose(0, 2, 3, 1, 4)
    return np.broadcast_to(both, (LANES, kz_count // HL, x_local, 2, HL)).reshape(LANES, -1)


def x_table(x_devices, x_local, kx_local):
    cos_x, sin_x = wave(x_devices * x_local, x_devices * kx_local)
    mix = np.array([[cos_x, -sin_x], [sin_x, cos_x]])
    mix = mix.reshape(2, 2, x_devices, kx_local, x_devices, x_local)
    full = np.einsum("pqakbx,hj->bxphaqkj", mix, np.eye(HL))
    size = x_devices * x_local * 2 * HL
    return full.reshape(size, -1)


def y_table(y_devices, y_local, ky_local, hh_count):
    pair = wave(y_devices * y_local, y_devices * ky_local)
    shape = (y_devices, ky_local, y_devices, y_local)
    parts = [
        np.einsum("akby,fg,hi->akgibfhy", t.reshape(shape), np.eye(2), np.eye(hh_count)).reshape(
            y_devices * ky_local * 2 * hh_count, -1
        )
        for t in pair
    ]
    return np.concatenate(parts, axis=1)


def y_inverse_table(y_devices, y_local, ky_local, hh_count):
    pair = wave(y_devices * y_local, y_devices * ky_local)
    shape = (y_devices, ky_local, y_devices, y_local)
    parts = [
        np.einsum("akby,hi->biyakh", t.reshape(shape), np.eye(hh_count)).reshape(
            y_devices * y_local * hh_count, -1
        )
        for t in pair
    ]
    return np.concatenate(parts, axis=1)


def spread_table(channels):
    left = np.repeat(np.eye(channels), channels, axis=1)
    right = np.tile(np.eye(channels), (1, LANES // channels))
    one = np.zeros((2 * channels, channels * channels + LANES))
    one[:channels, : channels * channels] = left
    one[channels:, channels * channels :] = right
    return np.concatenate([one, one], axis=0).astype(BF16)


def slot_mask(y_local):
    shape = (SUBLANES, LANES)
    return (iota(shape, 0) < y_local) & (iota(shape, 1) % (2 * HL) == HL)


def grid_kernel(in_ref, pre_ref, out_grad_ref, hi_ref, lo_ref, s_ref, ghi_ref, glo_ref):
    channels, x_local = in_ref.shape[:2]
    y_local = SUBLANES // 2
    rows = channels * SUBLANES
    table_hi = hi_ref[...].astype(F32)
    table_lo = lo_ref[...].astype(F32)
    lane_x = iota(table_hi.shape, 1) % LANES // (2 * HL)
    fields, highs, lows, tables_hi, tables_lo = [], [], [], [], []
    for x in range(x_local):
        fields.append(in_ref[:, x].astype(F32).reshape(rows, LANES).astype(BF16))
        pre_grad = out_grad_ref[:, x].astype(F32) * gelu_slope(pre_ref[:, x])
        high, low = split(pre_grad.reshape(rows, LANES))
        ghi_ref[x] = high
        glo_ref[x] = low
        highs.append(high)
        lows.append(low)
        tables_hi.append(jnp.where(lane_x == x, table_hi, 0.0).astype(BF16))
        tables_lo.append(jnp.where(lane_x == x, table_lo, 0.0).astype(BF16))
    field = jnp.concatenate(fields, axis=1)
    high = jnp.concatenate(highs, axis=1)
    low = jnp.concatenate(lows, axis=1)
    table = (jnp.concatenate(tables_hi, axis=0), jnp.concatenate(tables_lo, axis=0))
    raw_in = dot(field, table[0]) + dot(field, table[1])
    raw_grad = product((high, low), table)

    tile = (channels, SUBLANES, LANES)
    sign = jnp.where(iota(tile, 2) % 2 == 0, 1.0, -1.0)
    upper = iota(tile, 1) < y_local

    def joined(raw):
        even = raw[:, :LANES].reshape(tile)
        odd = raw[:, LANES:].reshape(tile)
        return jnp.where(
            upper,
            even + sign * pltpu.roll(even, y_local, 1),
            pltpu.roll(odd, y_local, 1) + sign * odd,
        )

    wide = (channels, SUBLANES, rows)
    row, col = iota(wide, 1), iota(wide, 2)
    gram = dot_rows(field, high) + dot_rows(field, low)
    trace = jnp.where(row == col % SUBLANES, gram.reshape(wide), 0.0)
    trace = jnp.sum(trace, axis=1, keepdims=True)
    at_row = row == col // SUBLANES // x_local
    weight_rows = split(jnp.where(at_row, trace, 0.0).reshape(rows, rows))
    flat = (rows, LANES)
    place = jnp.where(
        iota(flat, 1) == iota(flat, 0) // SUBLANES % x_local * (2 * HL) + HL, 1.0, 0.0
    ).astype(BF16)
    weight_slots = dot(weight_rows[0], place) + dot(weight_rows[1], place)
    ones = jnp.ones((2 * SUBLANES, field.shape[1]), BF16)
    bias = (dot_rows(ones, high) + dot_rows(ones, low))[:SUBLANES]
    bias_rows = split(jnp.where(at_row[0], bias, 0.0))
    bias_slots = dot(bias_rows[0], place) + dot(bias_rows[1], place)
    s_ref[:, 0] = joined(raw_in) + weight_slots.reshape(tile)
    s_ref[:, 1] = joined(raw_grad) + bias_slots[None]


def plane_kernel(r_ref, txh_ref, txl_ref, tyh_ref, tyl_ref, s_ref, stat_ref):
    x_devices, y_devices = s_ref.shape[:2]
    y_local = SUBLANES // 2
    stat_ref[...] = jnp.sum(r_ref[...], axis=0)
    values = jnp.where(slot_mask(y_local), 0.0, r_ref[...])
    values = values.reshape(x_devices, -1, LANES)
    wide = jnp.concatenate([values[g] for g in range(x_devices)], axis=1)
    along_x = product(split(wide), (txh_ref[...], txl_ref[...]))
    lane = iota((along_x.shape[0], LANES), 1)
    sign = jnp.where(lane < LANES // 2, 1.0, -1.0)
    turned = [
        sign * pltpu.roll(along_x[:, g * LANES : (g + 1) * LANES], LANES // 2, 1)
        for g in range(x_devices)
    ]
    both = jnp.concatenate([along_x, jnp.concatenate(turned, axis=1)], axis=0)
    along_y = product((tyh_ref[...], tyl_ref[...]), split(both))
    for g in range(x_devices):
        s_ref[g] = along_y[:, g * LANES : (g + 1) * LANES].reshape(s_ref.shape[1:])


def mode_kernel(cells, r_ref, spread_ref, sum_ref, weight_ref, grad_ref, s_ref):
    channels = sum_ref.shape[0]
    kx_local = weight_ref.shape[0]
    ky = pl.program_id(0)
    half = LANES // 2
    stacked = [
        r_ref[pl.ds(ky * 4 + f * 2 + hh, channels, stride=r_ref.shape[0] // channels), :]
        for hh in range(2)
        for f in range(2)
    ]
    modes = jnp.concatenate(stacked, axis=0).T
    row, lane = iota(modes.shape, 0), iota(modes.shape, 1)
    first = (row % HL == 0) & (lane < half)
    factor = jnp.where(
        lane // channels % 2 == 1, jnp.where(first, 1.0 / cells, 2.0 / cells), 1.0
    )
    modes = modes * factor
    low = modes - modes.astype(BF16).astype(F32)
    left = jnp.concatenate(
        [
            jnp.where(lane < half, modes, pltpu.roll(low, half, 1)),
            jnp.where(lane < half, pltpu.roll(modes, half, 1), low),
        ],
        axis=0,
    ).astype(BF16)
    spread = dot(left, spread_ref[...])
    count = kx_local * HL
    size = channels * channels
    for hh in range(2):
        real = spread[hh * 2 * count : hh * 2 * count + count]
        imag = spread[hh * 2 * count + count : (hh + 1) * 2 * count]
        in_real, in_imag = real[:, :size], imag[:, :size]
        repeat = size // LANES
        grad_real = jnp.concatenate([real[:, size:]] * repeat, axis=1)
        grad_imag = jnp.concatenate([imag[:, size:]] * repeat, axis=1)
        rows = pl.ds(hh * HL, HL)
        tile = (kx_local, HL, size)
        grad_ref[:, 0, 0, rows, :] = (in_real * grad_real + in_imag * grad_imag).reshape(tile)
        grad_ref[:, 0, 1, rows, :] = (in_real * grad_imag - in_imag * grad_real).reshape(tile)
        mix_real = weight_ref[:, 0, 0, rows, :].reshape(count, size)
        mix_imag = weight_ref[:, 0, 1, rows, :].reshape(count, size)
        terms = jnp.concatenate(
            [
                grad_real * mix_real + grad_imag * mix_imag,
                grad_imag * mix_real - grad_real * mix_imag,
            ],
            axis=0,
        )
        high, lower = split(terms)
        back = dot_rows(sum_ref[...], high) + dot_rows(sum_ref[...], lower)
        s_ref[pl.ds(ky * 2 + hh, channels, stride=SUBLANES), :] = back


def inverse_kernel(r_ref, stat_ref, tyh_ref, tyl_ref, txh_ref, txl_ref, s_ref):
    x_devices, y_devices = s_ref.shape[:2]
    y_local = SUBLANES // 2
    values = r_ref[...].reshape(x_devices, y_devices * SUBLANES, LANES)
    lane = iota(values.shape[1:], 1)
    sign = jnp.where(lane < LANES // 2, -1.0, 1.0)
    wide = jnp.concatenate([values[g] for g in range(x_devices)], axis=1)
    turned = [sign * pltpu.roll(values[g], LANES // 2, 1) for g in range(x_devices)]
    both = jnp.concatenate([wide, jnp.concatenate(turned, axis=1)], axis=0)
    along_y = product((tyh_ref[...], tyl_ref[...]), split(both))
    along_x = product(split(along_y), (txh_ref[...], txl_ref[...]), dot_rows)
    slots = slot_mask(y_local)
    for g in range(x_devices):
        block = along_x[:, g * LANES : (g + 1) * LANES].reshape(s_ref.shape[1:])
        s_ref[g] = jnp.where(slots, stat_ref[0], block)


def result_kernel(
    scale, r_ref, stat_ref, hi_ref, lo_ref, kw_ref, ghi_ref, glo_ref, grad_ref, point_ref, bias_ref
):
    channels, x_block = grad_ref.shape[:2]
    y_local = SUBLANES // 2
    x_local = LANES // (2 * HL)
    step = pl.program_id(0)
    rows = channels * SUBLANES
    tile = (channels, SUBLANES, LANES)
    values = r_ref[...].reshape(tile)
    turned = pltpu.roll(values, y_local, 1)
    sign = jnp.where(iota(tile, 2) % 2 == 0, 1.0, -1.0)
    upper = iota(tile, 1) < y_local
    left = jnp.concatenate(
        [
            jnp.where(upper, values, sign * turned).reshape(rows, LANES),
            jnp.where(upper, turned, sign * values).reshape(rows, LANES),
        ],
        axis=1,
    )
    high, low = split(left)
    kw_high, kw_low = split(kw_ref[...])
    left = jnp.concatenate([high, low, high, kw_high, kw_high, kw_low], axis=1)
    table_hi = hi_ref[...].astype(F32)
    table_lo = lo_ref[...].astype(F32)
    row_x = iota(table_hi.shape, 0) % LANES // (2 * HL)
    for k in range(x_block):
        keep = row_x == step * x_block + k
        t_hi = jnp.where(keep, table_hi, 0.0).astype(BF16)
        t_lo = jnp.where(keep, table_lo, 0.0).astype(BF16)
        right = jnp.concatenate([t_hi, t_hi, t_lo, ghi_ref[k], glo_ref[k], ghi_ref[k]], axis=0)
        grad_ref[:, k] = dot(left, right).reshape(tile)

    @pl.when(step == 0)
    def _():
        flat = (LANES, channels)
        lane, out = iota(flat, 0), iota(flat, 1)
        point = jnp.zeros(point_ref.shape, F32)
        bias = jnp.zeros(bias_ref.shape, F32)
        for y in range(y_local):
            place = (lane == out % x_local * (2 * HL) + HL) & (out // x_local == y)
            place = jnp.where(place, 1.0, 0.0)
            taken = r_ref[pl.ds(y, channels, stride=SUBLANES), :]
            point += jnp.dot(
                taken, place, precision=HIGHEST_PRECISION, preferred_element_type=F32
            )
            taken = jnp.broadcast_to(stat_ref[1, pl.ds(y, 1), :], (SUBLANES, LANES))
            bias += jnp.dot(
                taken, place, precision=HIGHEST_PRECISION, preferred_element_type=F32
            )
        point_ref[...] = point * scale
        bias_ref[...] = bias * scale


def call(kernel, out_shape, name, **options):
    params = pltpu.CompilerParams(vmem_limit_bytes=56 << 20)
    return pl.pallas_call(
        kernel, out_shape=out_shape, name=name, compiler_params=params, **options
    )


def whole(shape):
    zeros = (0,) * len(shape)
    return pl.BlockSpec(shape, lambda *_: zeros)


def to_tiles(array):
    lead, (rows, depth) = array.shape[:-2], array.shape[-2:]
    split_up = array.reshape(lead + (rows, depth // LANES, LANES))
    return jnp.swapaxes(split_up, -3, -2).reshape(lead + (SUBLANES, LANES))


def from_tiles(array, rows, depth):
    lead = array.shape[:-2]
    split_up = array.reshape(lead + (depth // LANES, rows, LANES))
    return jnp.swapaxes(split_up, -3, -2).reshape(lead + (rows, depth))


def transposed(inputs, pre_act, grad_out, point_weight, mode_weight):
    channels, x_local, y_local, depth = inputs.shape
    kx_local, ky_local, _, kz_count, pairs = mode_weight.shape
    x_devices = lax.axis_size("gx")
    y_devices = lax.axis_size("gy")
    devices = x_devices * y_devices
    hh_count = kz_count // HL
    cells = x_local * x_devices * y_local * y_devices * depth
    scale = 1.0 / math.sqrt(cells)
    axes = ("gx", "gy")
    rows = channels * SUBLANES

    def struct(shape, kind=F32):
        return jax.ShapeDtypeStruct(shape, kind)

    def exchange(chunks):
        return lax.all_to_all(chunks, axes, 0, 0)

    z_high, z_low = split_table(depth_table(depth, kz_count, x_local))
    tx = split_table(x_table(x_devices, x_local, kx_local))
    ty = split_table(y_table(y_devices, y_local, ky_local, hh_count))
    tyi = split_table(y_inverse_table(y_devices, y_local, ky_local, hh_count))
    spread = spread_table(channels)
    summed = np.repeat(np.eye(channels), channels, axis=1).astype(BF16)

    chunks, g_high, g_low = call(
        grid_kernel,
        (
            struct((channels, 2, SUBLANES, LANES)),
            struct((x_local, rows, LANES), BF16),
            struct((x_local, rows, LANES), BF16),
        ),
        "grid",
    )(to_tiles(inputs), to_tiles(pre_act), to_tiles(grad_out), z_high, z_low)
    planes = exchange(chunks)
    mode_rows = ky_local * 2 * hh_count
    chunks, stats = call(
        plane_kernel,
        (struct((x_devices, y_devices, mode_rows, LANES)), struct((2, SUBLANES, LANES))),
        "plane",
    )(planes, *tx, *ty)
    modes = exchange(chunks.reshape(devices, mode_rows, LANES))
    block = (kx_local, 1, 2, kz_count, pairs)
    block_spec = pl.BlockSpec(block, lambda k: (0, k, 0, 0, 0))
    mode_grad, chunks = call(
        lambda *refs: mode_kernel(cells, *refs),
        (struct(mode_weight.shape), struct((devices * SUBLANES, LANES))),
        "mode",
        grid=(ky_local,),
        in_specs=[
            whole((devices * mode_rows, LANES)),
            whole(spread.shape),
            whole(summed.shape),
            block_spec,
        ],
        out_specs=(block_spec, whole((devices * SUBLANES, LANES))),
    )(modes.reshape(devices * mode_rows, LANES), spread, summed, mode_weight)
    back = exchange(chunks.reshape(devices, SUBLANES, LANES))
    chunks = call(
        inverse_kernel, struct((x_devices, y_devices, SUBLANES, LANES)), "inverse"
    )(back, stats, *tyi, *tx)
    near = exchange(chunks.reshape(devices, SUBLANES, LANES))
    kron = (
        point_weight[:, None, :, None] * jnp.eye(SUBLANES, dtype=F32)[None, :, None, :]
    ).reshape(rows, rows)
    x_block = max(x_local // 4, 1)
    g_spec = pl.BlockSpec((x_block, rows, LANES), lambda k: (k, 0, 0))
    grad, point_grad, bias_grad = call(
        lambda *refs: result_kernel(scale, *refs),
        (
            struct((channels, x_local, SUBLANES, LANES)),
            struct((channels, channels)),
            struct((SUBLANES, channels)),
        ),
        "result",
        grid=(x_local // x_block,),
        in_specs=[
            whole((rows, LANES)),
            whole((2, SUBLANES, LANES)),
            whole((2 * LANES, LANES)),
            whole((2 * LANES, LANES)),
            whole((rows, rows)),
            g_spec,
            g_spec,
        ],
        out_specs=(
            pl.BlockSpec((channels, x_block, SUBLANES, LANES), lambda k: (0, k, 0, 0)),
            whole((channels, channels)),
            whole((SUBLANES, channels)),
        ),
    )(near.reshape(rows, LANES), stats, z_high.T, z_low.T, kron, g_high, g_low)
    return (from_tiles(grad, y_local, depth), point_grad, bias_grad[0], mode_grad)


def one_channel_each(inputs, mode_weight):
    channels, x_local, y_local, depth = inputs.shape
    kx_local, ky_local, _, kz_count, _ = mode_weight.shape
    return (
        channels == lax.axis_size("gx") * lax.axis_size("gy")
        and LANES % channels == 0
        and depth == 2 * LANES
        and y_local * 2 == SUBLANES
        and kz_count == 2 * HL
        and ky_local * 2 == SUBLANES
        and x_local * 2 * HL == LANES
        and kx_local == x_local
        and x_local * y_local == channels
    )


def shards(inputs, pre_act, grad_out, point_weight, mode_weight):
    plan = transposed if one_channel_each(inputs, mode_weight) else partial_sums
    return plan(inputs, pre_act, grad_out, point_weight, mode_weight)


def solution(mesh):
    return jax.shard_map(
        shards,
        mesh=mesh,
        in_specs=(
            P(None, "gx", "gy", None),
            P(None, "gx", "gy", None),
            P(None, "gx", "gy", None),
            P(),
            P("gx", "gy", None, None, None),
        ),
        out_specs=(P(None, "gx", "gy", None), P(), P(), P("gx", "gy", None, None, None)),
        check_vma=False,
    )
```

```python
import functools
import math

import jax
import jax.numpy as jnp
import numpy as np
from jax import lax
from jax.experimental import pallas as pl
from jax.experimental.pallas import tpu as pltpu
from jax.sharding import PartitionSpec as P

HIGHEST_PRECISION = lax.Precision.HIGHEST
ROOT_HALF = 0.7071067811865476
NORMAL_PEAK = 0.3989422804014327


def gelu_slope(pre_act):
    value = pre_act.astype(jnp.float32)
    return (
        0.5 * (1.0 + jax.scipy.special.erf(value * ROOT_HALF))
        + value * jnp.exp(-0.5 * value * value) * NORMAL_PEAK
    )


def phases(length, modes, wrapped, index, first, count):
    if wrapped:
        frequency = jnp.where(index < modes // 2, index, index + (length - modes))
    else:
        frequency = index
    places = first + jnp.arange(count, dtype=jnp.int32)
    turns = frequency[:, None] * places[None, :] % length
    angle = turns.astype(jnp.float32) * (2.0 * math.pi / length)
    return (jnp.cos(angle), jnp.sin(angle))


def transform(cos_table, sin_table, data, sign):
    real_part = data[..., 0, :]
    imag_part = data[..., 1, :]

    def apply(table, values):
        return jnp.tensordot(table, values, axes=1, precision=HIGHEST_PRECISION)

    if sign < 0:
        out_real = apply(cos_table, real_part) + apply(sin_table, imag_part)
        out_imag = apply(cos_table, imag_part) - apply(sin_table, real_part)
    else:
        out_real = apply(cos_table, real_part) - apply(sin_table, imag_part)
        out_imag = apply(cos_table, imag_part) + apply(sin_table, real_part)
    return jnp.stack([out_real, out_imag], axis=-2)


def depth_forward(field, kz_count):
    channels = field.shape[0]
    depth = field.shape[-1]
    cos_z, sin_z = phases(depth, kz_count, False, jnp.arange(kz_count, dtype=jnp.int32), 0, depth)
    real_part = jnp.einsum("cabz,kz->abkc", field, cos_z, precision=HIGHEST_PRECISION)
    imag_part = -jnp.einsum("cabz,kz->abkc", field, sin_z, precision=HIGHEST_PRECISION)
    lead = real_part.shape[:2]
    return jnp.stack(
        [
            real_part.reshape(lead + (kz_count * channels,)),
            imag_part.reshape(lead + (kz_count * channels,)),
        ],
        axis=2,
    )


def depth_inverse(spectrum, kz_count, channels, depth):
    lead = spectrum.shape[:2]
    split = spectrum.reshape(lead + (2, kz_count, channels))
    cos_z, sin_z = phases(depth, kz_count, False, jnp.arange(kz_count, dtype=jnp.int32), 0, depth)
    return jnp.einsum(
        "abkc,kz->cabz", split[:, :, 0], cos_z, precision=HIGHEST_PRECISION
    ) - jnp.einsum("abkc,kz->cabz", split[:, :, 1], sin_z, precision=HIGHEST_PRECISION)


def mode_work(spectrum_in, spectrum_grad, weight, cells):
    rows_a, rows_b, _, kz_count, _ = weight.shape
    channels = spectrum_in.shape[-1] // kz_count
    factor = (
        jnp.where(jnp.arange(kz_count, dtype=jnp.int32) == 0, 1.0, 2.0).astype(jnp.float32) / cells
    )
    shape = (rows_a, rows_b, 2, kz_count, channels)
    given = spectrum_in.reshape(shape)
    scaled = spectrum_grad.reshape(shape) * factor[:, None]
    mixing = weight.reshape(shape + (channels,))
    in_real = given[:, :, 0]
    in_imag = given[:, :, 1]
    grad_real = scaled[:, :, 0]
    grad_imag = scaled[:, :, 1]
    mix_real = mixing[:, :, 0]
    mix_imag = mixing[:, :, 1]

    def outer(left, right):
        return jnp.einsum("abki,abko->abkio", left, right, precision=HIGHEST_PRECISION)

    def mixed(values, matrix):
        return jnp.einsum("abko,abkio->abki", values, matrix, precision=HIGHEST_PRECISION)

    result_real = outer(in_real, grad_real) + outer(in_imag, grad_imag)
    result_imag = outer(in_real, grad_imag) - outer(in_imag, grad_real)
    mode_grad = jnp.stack([result_real, result_imag], axis=2).reshape(
        rows_a, rows_b, 2, kz_count, channels * channels
    )
    back_real = mixed(grad_real, mix_real) + mixed(grad_imag, mix_imag)
    back_imag = mixed(grad_imag, mix_real) - mixed(grad_real, mix_imag)
    back_spectrum = jnp.stack([back_real, back_imag], axis=2).reshape(
        rows_a, rows_b, 2, kz_count * channels
    )
    return (mode_grad, back_spectrum)


def joined_rows(main, extra):
    count = main.shape[0]
    return jnp.concatenate([main.reshape(count, -1), extra.reshape(count, -1)], axis=1)


def split_rows(result, main_shape, extra_shape):
    main_size = 1
    for item in main_shape[1:]:
        main_size = main_size * item
    main = result[:, :main_size].reshape(main_shape)
    extra = result[:, main_size:].reshape(extra_shape)
    return (main, extra)


def partial_sums(inputs, pre_act, grad_out, point_weight, mode_weight):
    channels, x_local, y_local, depth = inputs.shape
    kx_local, ky_local, _, kz_count, _ = mode_weight.shape
    x_devices = lax.axis_size("gx")
    y_devices = lax.axis_size("gy")
    x_length = x_local * x_devices
    y_length = y_local * y_devices
    kx_count = kx_local * x_devices
    ky_count = ky_local * y_devices
    cells = x_length * y_length * depth
    scale = 1.0 / math.sqrt(cells)
    x_offset = lax.axis_index("gx") * x_local
    y_offset = lax.axis_index("gy") * y_local
    width = kz_count * channels
    pair_width = 2 * width
    stat_count = channels * channels + channels
    mode_count = kx_count * ky_count
    field_in = inputs.astype(jnp.float32)
    pre_grad = grad_out.astype(jnp.float32) * gelu_slope(pre_act)
    weight_sum = jnp.einsum("ixyz,oxyz->io", field_in, pre_grad, precision=HIGHEST_PRECISION)
    bias_sum = jnp.sum(pre_grad, axis=(1, 2, 3))
    extra_cols = (stat_count + mode_count - 1) // mode_count
    stat_flat = jnp.concatenate([weight_sum.reshape(-1), bias_sum])
    grid = jnp.pad(stat_flat, (0, mode_count * extra_cols - stat_count)).reshape(
        kx_count, ky_count, extra_cols
    )
    spectra = jnp.stack(
        [depth_forward(field_in, kz_count), depth_forward(pre_grad, kz_count)], axis=2
    )
    along_y = jnp.swapaxes(spectra, 0, 1)
    grid_y = jnp.swapaxes(grid, 0, 1)
    cos_y, sin_y = phases(
        y_length,
        ky_count,
        True,
        jnp.arange(lax.axis_size("gy") * ky_local, dtype=jnp.int32),
        y_offset,
        y_local,
    )
    partial_y, extra_y = split_rows(
        lax.psum_scatter(
            joined_rows(transform(cos_y, sin_y, along_y, -1), grid_y),
            "gy",
            scatter_dimension=0,
            tiled=True,
        ),
        (ky_local, x_local, 2, 2, width),
        (ky_local, kx_count, extra_cols),
    )
    along_x = jnp.swapaxes(partial_y, 0, 1)
    extra_along = jnp.swapaxes(extra_y, 0, 1)
    cos_x, sin_x = phases(
        x_length,
        kx_count,
        True,
        jnp.arange(lax.axis_size("gx") * kx_local, dtype=jnp.int32),
        x_offset,
        x_local,
    )
    owned, owned_extra = split_rows(
        lax.psum_scatter(
            joined_rows(transform(cos_x, sin_x, along_x, -1), extra_along),
            "gx",
            scatter_dimension=0,
            tiled=True,
        ),
        (kx_local, ky_local, 2, 2, width),
        (kx_local, ky_local, extra_cols),
    )
    mode_grad, back_spectrum = mode_work(owned[:, :, 0], owned[:, :, 1], mode_weight, cells)
    back_joined = jnp.concatenate(
        [back_spectrum.reshape(kx_local, ky_local, pair_width), owned_extra], axis=2
    )
    piece = lax.all_gather(back_joined, "gx", axis=0, tiled=True)
    kx_index = jnp.arange(piece.shape[0], dtype=jnp.int32)
    cos_x, sin_x = phases(x_length, kx_count, True, kx_index, x_offset, x_local)
    main = piece[:, :, :pair_width].reshape(piece.shape[0], piece.shape[1], 2, width)
    near = transform(cos_x.T, sin_x.T, main, 1)
    near_stats = piece[:, :, pair_width:]
    side_cols = (kx_count * extra_cols + x_local - 1) // x_local
    side_flat = jnp.swapaxes(near_stats, 0, 1).reshape(ky_local, kx_count * extra_cols)
    side = jnp.swapaxes(side_flat.reshape(ky_local, x_local, side_cols), 0, 1)
    near_joined = jnp.concatenate([near.reshape(x_local, ky_local, pair_width), side], axis=2)
    piece = lax.all_gather(near_joined, "gy", axis=1, tiled=True)
    ky_index = jnp.arange(piece.shape[1], dtype=jnp.int32)
    cos_y, sin_y = phases(y_length, ky_count, True, ky_index, y_offset, y_local)
    main = piece[:, :, :pair_width].reshape(piece.shape[0], piece.shape[1], 2, width)
    moved = jnp.swapaxes(transform(cos_y.T, sin_y.T, jnp.swapaxes(main, 0, 1), 1), 0, 1)
    far_stats = piece[:, :, pair_width:]
    stats_rows = jnp.swapaxes(far_stats, 0, 1).reshape(ky_count, x_local * side_cols)
    stats_grid = jnp.swapaxes(stats_rows.reshape(ky_count, kx_count, extra_cols), 0, 1)
    stat_values = stats_grid.reshape(-1)[:stat_count]
    point_grad = stat_values[: channels * channels].reshape(channels, channels)
    bias_grad = stat_values[channels * channels :]
    local = jnp.einsum("io,oxyz->ixyz", point_weight, pre_grad, precision=HIGHEST_PRECISION)
    input_grad = local + depth_inverse(moved, kz_count, channels, depth)
    return (input_grad, point_grad * scale, bias_grad * scale, mode_grad)


LANES = 128
SUBLANES = 8
HL = 8
BF16 = jnp.bfloat16
F32 = jnp.float32


def split_table(table):
    high = table.astype(np.float32).astype(BF16)
    low = (table - high.astype(np.float64)).astype(np.float32).astype(BF16)
    return (high, low)


def split(values):
    high = values.astype(BF16)
    return (high, (values - high.astype(F32)).astype(BF16))


def dot(left, right):
    return jnp.dot(left, right, preferred_element_type=F32)


def dot_rows(left, right):
    return lax.dot_general(left, right, (((1,), (1,)), ((), ())), preferred_element_type=F32)


def product(left, right, multiply=dot):
    return (
        multiply(left[0], right[0]) + multiply(left[0], right[1]) + multiply(left[1], right[0])
    )


def iota(shape, axis):
    return lax.broadcasted_iota(jnp.int32, shape, axis)


def wave(length, modes):
    index = np.arange(modes)
    frequency = np.where(index < modes // 2, index, index + (length - modes))
    turns = frequency[:, None] * np.arange(length)[None, :] % length
    angle = turns * (2.0 * math.pi / length)
    return (np.cos(angle), np.sin(angle))


def depth_table(depth, kz_count, x_local):
    h = np.arange(kz_count)
    angle = (h[None, :] * np.arange(LANES)[:, None] % depth) * (2.0 * math.pi / depth)
    both = np.stack([np.cos(angle), -np.sin(angle)], axis=1)
    both = both.reshape(LANES, 2, kz_count // HL, 1, HL).transpose(0, 2, 3, 1, 4)
    return np.broadcast_to(both, (LANES, kz_count // HL, x_local, 2, HL)).reshape(LANES, -1)


def x_table(x_devices, x_local, kx_local):
    cos_x, sin_x = wave(x_devices * x_local, x_devices * kx_local)
    mix = np.array([[cos_x, -sin_x], [sin_x, cos_x]])
    mix = mix.reshape(2, 2, x_devices, kx_local, x_devices, x_local)
    full = np.einsum("pqakbx,hj->bxphaqkj", mix, np.eye(HL))
    size = x_devices * x_local * 2 * HL
    return full.reshape(size, -1)


def y_table(y_devices, y_local, ky_local, hh_count):
    pair = wave(y_devices * y_local, y_devices * ky_local)
    shape = (y_devices, ky_local, y_devices, y_local)
    parts = [
        np.einsum("akby,fg,hi->akgibfhy", t.reshape(shape), np.eye(2), np.eye(hh_count)).reshape(
            y_devices * ky_local * 2 * hh_count, -1
        )
        for t in pair
    ]
    return np.concatenate(parts, axis=1)


def y_inverse_table(y_devices, y_local, ky_local, hh_count):
    pair = wave(y_devices * y_local, y_devices * ky_local)
    shape = (y_devices, ky_local, y_devices, y_local)
    parts = [
        np.einsum("akby,hi->biyakh", t.reshape(shape), np.eye(hh_count)).reshape(
            y_devices * y_local * hh_count, -1
        )
        for t in pair
    ]
    return np.concatenate(parts, axis=1)


def spread_table(channels):
    left = np.repeat(np.eye(channels), channels, axis=1)
    right = np.tile(np.eye(channels), (1, LANES // channels))
    one = np.zeros((2 * channels, channels * channels + LANES))
    one[:channels, : channels * channels] = left
    one[channels:, channels * channels :] = right
    return np.concatenate([one, one], axis=0).astype(BF16)


def slot_mask(y_local):
    shape = (SUBLANES, LANES)
    return (iota(shape, 0) < y_local) & (iota(shape, 1) % (2 * HL) == HL)


def grid_kernel(count, *refs):
    in_hbm, pre_hbm, out_grad_hbm, hi_hbm, lo_hbm = refs[:5]
    later_hbm, refs = refs[5 : 5 + count], refs[5 + count :]
    s_ref, ghi_ref, glo_ref = refs[:3]
    later, refs = refs[3 : 3 + count], refs[3 + count :]
    in_ref, pre_ref, out_grad_ref, hi_ref, lo_ref, near_sems, far_sems = refs
    channels, x_local = in_ref.shape[:2]
    y_local = SUBLANES // 2
    rows = channels * SUBLANES
    step = max(x_local // 4, 1)
    parts = {}
    for x in range(0, x_local, step):
        at = (slice(None), pl.ds(x, step))
        for index, pair in enumerate(((pre_hbm, pre_ref), (out_grad_hbm, out_grad_ref))):
            sem = near_sems.at[2 * (x // step) + index]
            parts[x, index] = pltpu.make_async_copy(pair[0].at[at], pair[1].at[at], sem)
            parts[x, index].start()
    whole_copies = [(in_hbm, in_ref), (hi_hbm, hi_ref), (lo_hbm, lo_ref)]
    whole_copies = whole_copies + list(zip(later_hbm, later))
    whole_copies = [
        pltpu.make_async_copy(source, target, far_sems.at[index])
        for index, (source, target) in enumerate(whole_copies)
    ]
    for copy in whole_copies:
        copy.start()
    fields, highs, lows, tables_hi, tables_lo = [], [], [], [], []
    for x in range(x_local):
        if x % step == 0:
            parts[x, 0].wait()
            parts[x, 1].wait()
        pre_grad = out_grad_ref[:, x].astype(F32) * gelu_slope(pre_ref[:, x])
        high, low = split(pre_grad.reshape(rows, LANES))
        ghi_ref[x] = high
        glo_ref[x] = low
        highs.append(high)
        lows.append(low)
    for copy in whole_copies[:3]:
        copy.wait()
    table_hi = hi_ref[...].astype(F32)
    table_lo = lo_ref[...].astype(F32)
    lane_x = iota(table_hi.shape, 1) % LANES // (2 * HL)
    for x in range(x_local):
        fields.append(in_ref[:, x].astype(F32).reshape(rows, LANES).astype(BF16))
        tables_hi.append(jnp.where(lane_x == x, table_hi, 0.0).astype(BF16))
        tables_lo.append(jnp.where(lane_x == x, table_lo, 0.0).astype(BF16))
    field = jnp.concatenate(fields, axis=1)
    high = jnp.concatenate(highs, axis=1)
    low = jnp.concatenate(lows, axis=1)
    table = (jnp.concatenate(tables_hi, axis=0), jnp.concatenate(tables_lo, axis=0))
    raw_in = dot(field, table[0]) + dot(field, table[1])
    raw_grad = product((high, low), table)

    tile = (channels, SUBLANES, LANES)
    sign = jnp.where(iota(tile, 2) % 2 == 0, 1.0, -1.0)
    upper = iota(tile, 1) < y_local

    def joined(raw):
        even = raw[:, :LANES].reshape(tile)
        odd = raw[:, LANES:].reshape(tile)
        return jnp.where(
            upper,
            even + sign * pltpu.roll(even, y_local, 1),
            pltpu.roll(odd, y_local, 1) + sign * odd,
        )

    wide = (channels, SUBLANES, rows)
    row, col = iota(wide, 1), iota(wide, 2)
    gram = dot_rows(field, high) + dot_rows(field, low)
    trace = jnp.where(row == col % SUBLANES, gram.reshape(wide), 0.0)
    trace = jnp.sum(trace, axis=1, keepdims=True)
    at_row = row == col // SUBLANES // x_local
    weight_rows = split(jnp.where(at_row, trace, 0.0).reshape(rows, rows))
    flat = (rows, LANES)
    place = jnp.where(
        iota(flat, 1) == iota(flat, 0) // SUBLANES % x_local * (2 * HL) + HL, 1.0, 0.0
    ).astype(BF16)
    weight_slots = dot(weight_rows[0], place) + dot(weight_rows[1], place)
    ones = jnp.ones((2 * SUBLANES, field.shape[1]), BF16)
    bias = (dot_rows(ones, high) + dot_rows(ones, low))[:SUBLANES]
    bias_rows = split(jnp.where(at_row[0], bias, 0.0))
    bias_slots = dot(bias_rows[0], place) + dot(bias_rows[1], place)
    s_ref[:, 0] = joined(raw_in) + weight_slots.reshape(tile)
    s_ref[:, 1] = joined(raw_grad) + bias_slots[None]
    for copy in whole_copies[3:]:
        copy.wait()


def slot_place(channels, x_local, y):
    lane, out = iota((LANES, channels), 0), iota((LANES, channels), 1)
    place = (lane == out % x_local * (2 * HL) + HL) & (out // x_local == y)
    return jnp.where(place, 1.0, 0.0)


def from_slots(taken, place):
    return jnp.dot(taken, place, precision=HIGHEST_PRECISION, preferred_element_type=F32)


def plane_kernel(
    scale, r_ref, txh_ref, txl_ref, tyh_ref, tyl_ref, s_ref, stat_ref, bias_ref
):
    x_devices, y_devices = s_ref.shape[:2]
    y_local = SUBLANES // 2
    stats = jnp.sum(r_ref[...], axis=0)
    stat_ref[...] = stats[0]
    channels = bias_ref.shape[1]
    bias = jnp.zeros((SUBLANES, channels), F32)
    for y in range(y_local):
        row = jnp.where(iota((SUBLANES, LANES), 0) == y, stats[1], 0.0)
        bias += from_slots(row, slot_place(channels, channels // y_local, y))
    bias_ref[...] = jnp.sum(bias, axis=0, keepdims=True) * scale
    values = jnp.where(slot_mask(y_local), 0.0, r_ref[...])
    values = values.reshape(x_devices, -1, LANES)
    wide = jnp.concatenate([values[g] for g in range(x_devices)], axis=1)
    along_x = product(split(wide), (txh_ref[...], txl_ref[...]))
    lane = iota((along_x.shape[0], LANES), 1)
    sign = jnp.where(lane < LANES // 2, 1.0, -1.0)
    turned = [
        sign * pltpu.roll(along_x[:, g * LANES : (g + 1) * LANES], LANES // 2, 1)
        for g in range(x_devices)
    ]
    both = jnp.concatenate([along_x, jnp.concatenate(turned, axis=1)], axis=0)
    along_y = product((tyh_ref[...], tyl_ref[...]), split(both))
    for g in range(x_devices):
        s_ref[g] = along_y[:, g * LANES : (g + 1) * LANES].reshape(s_ref.shape[1:])


def mode_rows(r_ref, picks, channels):
    stride = r_ref.shape[0] // channels
    taken = [r_ref[pl.ds(pick, channels, stride=stride), :] for pick in picks]
    return jnp.concatenate(taken, axis=0).T


def repeated(values, times):
    return jnp.concatenate([values] * times, axis=1)


def back_kernel(cells, channels, r_ref, weight_ref, s_ref):
    size = channels * channels
    kx_local, ky_local = weight_ref.shape[:2]
    shape = (channels, size)
    sums = jnp.where(iota(shape, 0) == iota(shape, 1) // channels, 1.0, 0.0).astype(BF16)
    count = kx_local * HL
    times = size // LANES
    group = LANES // channels // 2
    for start in range(0, ky_local, group):
        places = [(ky, hh) for ky in range(start, start + group) for hh in range(2)]
        modes = mode_rows(r_ref, [ky * 4 + 2 + hh for ky, hh in places], channels)
        row, lane = iota(modes.shape, 0), iota(modes.shape, 1)
        first = (row % HL == 0) & (lane // channels % 2 == 0)
        modes = modes * jnp.where(first, 1.0 / cells, 2.0 / cells)
        for index, (ky, hh) in enumerate(places):
            grad = jnp.where(lane // channels == index, modes, 0.0)
            shift = channels
            while shift < LANES:
                grad = grad + pltpu.roll(grad, shift, 1)
                shift = shift * 2
            grad_real, grad_imag = repeated(grad[:count], times), repeated(grad[count:], times)
            rows = slice(hh * HL, (hh + 1) * HL)
            mix_real = weight_ref[:, ky, 0, rows, :].reshape(count, size)
            mix_imag = weight_ref[:, ky, 1, rows, :].reshape(count, size)
            terms = jnp.concatenate(
                [
                    grad_real * mix_real + grad_imag * mix_imag,
                    grad_imag * mix_real - grad_real * mix_imag,
                ],
                axis=0,
            )
            high, low = split(terms)
            back = dot_rows(sums, high) + dot_rows(sums, low)
            s_ref[pl.ds(ky * 2 + hh, channels, stride=SUBLANES), :] = back


def outer_kernel(cells, r_ref, spread_ref, grad_ref):
    kx_local = grad_ref.shape[0]
    size = grad_ref.shape[-1]
    channels = spread_ref.shape[0] // 4
    ky = pl.program_id(0)
    half = LANES // 2
    modes = mode_rows(r_ref, [ky * 4 + f * 2 + hh for hh in range(2) for f in range(2)], channels)
    row, lane = iota(modes.shape, 0), iota(modes.shape, 1)
    first = (row % HL == 0) & (lane < half)
    factor = jnp.where(
        lane // channels % 2 == 1, jnp.where(first, 1.0 / cells, 2.0 / cells), 1.0
    )
    modes = modes * factor
    low = modes - modes.astype(BF16).astype(F32)
    left = jnp.concatenate(
        [
            jnp.where(lane < half, modes, pltpu.roll(low, half, 1)),
            jnp.where(lane < half, pltpu.roll(modes, half, 1), low),
        ],
        axis=0,
    ).astype(BF16)
    spread = dot(left, spread_ref[...])
    count = kx_local * HL
    for hh in range(2):
        real = spread[hh * 2 * count : hh * 2 * count + count]
        imag = spread[hh * 2 * count + count : (hh + 1) * 2 * count]
        in_real, in_imag = real[:, :size], imag[:, :size]
        times = size // LANES
        grad_real, grad_imag = repeated(real[:, size:], times), repeated(imag[:, size:], times)
        rows = pl.ds(hh * HL, HL)
        tile = (kx_local, HL, size)
        grad_ref[:, 0, 0, rows, :] = (in_real * grad_real + in_imag * grad_imag).reshape(tile)
        grad_ref[:, 0, 1, rows, :] = (in_real * grad_imag - in_imag * grad_real).reshape(tile)


def local_kernel(weight_ref, ghi_ref, glo_ref, local_ref):
    channels, x_local = local_ref.shape[:2]
    rows = channels * SUBLANES
    spread = jnp.where(
        iota((rows, channels), 0) // SUBLANES == iota((rows, channels), 1), 1.0, 0.0
    )
    tall = jnp.dot(
        spread, weight_ref[...], precision=HIGHEST_PRECISION, preferred_element_type=F32
    )
    square = lax.dot_general(
        tall,
        spread,
        (((1,), (1,)), ((), ())),
        precision=HIGHEST_PRECISION,
        preferred_element_type=F32,
    )
    same = iota(square.shape, 0) % SUBLANES == iota(square.shape, 1) % SUBLANES
    high, low = split(jnp.where(same, square, 0.0))
    left = jnp.concatenate([high, high, low], axis=1)
    for x in range(x_local):
        right = jnp.concatenate([ghi_ref[x], glo_ref[x], ghi_ref[x]], axis=0)
        local_ref[:, x] = dot(left, right).reshape(channels, SUBLANES, LANES)


def inverse_kernel(r_ref, stat_ref, tyh_ref, tyl_ref, txh_ref, txl_ref, s_ref):
    x_devices, y_devices = s_ref.shape[:2]
    y_local = SUBLANES // 2
    values = r_ref[...].reshape(x_devices, y_devices * SUBLANES, LANES)
    lane = iota(values.shape[1:], 1)
    sign = jnp.where(lane < LANES // 2, -1.0, 1.0)
    wide = jnp.concatenate([values[g] for g in range(x_devices)], axis=1)
    turned = [sign * pltpu.roll(values[g], LANES // 2, 1) for g in range(x_devices)]
    both = jnp.concatenate([wide, jnp.concatenate(turned, axis=1)], axis=0)
    along_y = product((tyh_ref[...], tyl_ref[...]), split(both))
    along_x = product(split(along_y), (txh_ref[...], txl_ref[...]), dot_rows)
    slots = slot_mask(y_local)
    for g in range(x_devices):
        block = along_x[:, g * LANES : (g + 1) * LANES].reshape(s_ref.shape[1:])
        s_ref[g] = jnp.where(slots, stat_ref[...], block)


def result_kernel(scale, r_ref, hi_ref, lo_ref, local_ref, grad_ref, point_ref, left_ref):
    channels, x_block = grad_ref.shape[:2]
    y_local = SUBLANES // 2
    x_local = LANES // (2 * HL)
    step = pl.program_id(0)
    rows = channels * SUBLANES
    tile = (channels, SUBLANES, LANES)

    @pl.when(step == 0)
    def _():
        values = r_ref[...].reshape(tile)
        turned = pltpu.roll(values, y_local, 1)
        sign = jnp.where(iota(tile, 2) % 2 == 0, 1.0, -1.0)
        upper = iota(tile, 1) < y_local
        left = jnp.concatenate(
            [
                jnp.where(upper, values, sign * turned).reshape(rows, LANES),
                jnp.where(upper, turned, sign * values).reshape(rows, LANES),
            ],
            axis=1,
        )
        high, low = split(left)
        left_ref[...] = jnp.concatenate([high, low, high], axis=1)
        point = jnp.zeros(point_ref.shape, F32)
        for y in range(y_local):
            taken = r_ref[pl.ds(y, channels, stride=SUBLANES), :]
            point += from_slots(taken, slot_place(channels, x_local, y))
        point_ref[...] = point * scale

    table_hi = hi_ref[...].astype(F32)
    table_lo = lo_ref[...].astype(F32)
    row_x = iota(table_hi.shape, 0) % LANES // (2 * HL)
    for k in range(x_block):
        x = step * x_block + k
        t_hi = jnp.where(row_x == x, table_hi, 0.0).astype(BF16)
        t_lo = jnp.where(row_x == x, table_lo, 0.0).astype(BF16)
        right = jnp.concatenate([t_hi, t_hi, t_lo], axis=0)
        grad_ref[:, k] = dot(left_ref[...], right).reshape(tile) + local_ref[:, x]


def call(kernel, out_shape, name, vmem=16, **options):
    params = pltpu.CompilerParams(vmem_limit_bytes=vmem << 20)
    return pl.pallas_call(
        kernel, out_shape=out_shape, name=name, compiler_params=params, **options
    )


def held(count):
    return [pl.BlockSpec(memory_space=pltpu.VMEM)] * count


def to_tiles(array):
    lead, (rows, depth) = array.shape[:-2], array.shape[-2:]
    split_up = array.reshape(lead + (rows, depth // LANES, LANES))
    return jnp.swapaxes(split_up, -3, -2).reshape(lead + (SUBLANES, LANES))


def from_tiles(array, rows, depth):
    lead = array.shape[:-2]
    split_up = array.reshape(lead + (depth // LANES, rows, LANES))
    return jnp.swapaxes(split_up, -3, -2).reshape(lead + (rows, depth))


def transposed(inputs, pre_act, grad_out, point_weight, mode_weight):
    channels, x_local, y_local, depth = inputs.shape
    kx_local, ky_local, _, kz_count, pairs = mode_weight.shape
    x_devices = lax.axis_size("gx")
    y_devices = lax.axis_size("gy")
    devices = x_devices * y_devices
    hh_count = kz_count // HL
    cells = x_local * x_devices * y_local * y_devices * depth
    scale = 1.0 / math.sqrt(cells)
    axes = ("gx", "gy")
    rows = channels * SUBLANES

    def struct(shape, kind=F32):
        return jax.ShapeDtypeStruct(shape, kind)

    def exchange(chunks):
        return lax.all_to_all(chunks, axes, 0, 0)

    z_high, z_low = split_table(depth_table(depth, kz_count, x_local))
    tx = split_table(x_table(x_devices, x_local, kx_local))
    ty = split_table(y_table(y_devices, y_local, ky_local, hh_count))
    tyi = split_table(y_inverse_table(y_devices, y_local, ky_local, hh_count))
    spread = spread_table(channels)

    field_shape = (channels, x_local, SUBLANES, LANES)
    later = (*tx, *ty, *tyi, z_high.T, z_low.T, mode_weight)
    chunks, g_high, g_low, *later = call(
        functools.partial(grid_kernel, len(later)),
        (
            struct((channels, 2, SUBLANES, LANES)),
            struct((x_local, rows, LANES), BF16),
            struct((x_local, rows, LANES), BF16),
            *(struct(array.shape, array.dtype) for array in later),
        ),
        "grid",
        vmem=24,
        in_specs=[pl.BlockSpec(memory_space=pltpu.HBM)] * (5 + len(later)),
        out_specs=held(3 + len(later)),
        scratch_shapes=[
            *([pltpu.VMEM(field_shape, BF16)] * 3),
            *([pltpu.VMEM(z_high.shape, BF16)] * 2),
            pltpu.SemaphoreType.DMA((2 * x_local,)),
            pltpu.SemaphoreType.DMA((3 + len(later),)),
        ],
    )(
        *(
            pltpu.with_memory_space_constraint(array, pltpu.HBM)
            for array in (
                to_tiles(inputs),
                to_tiles(pre_act),
                to_tiles(grad_out),
                z_high,
                z_low,
                *later,
            )
        )
    )
    tx, ty, tyi, z_turned, mode_weight = later[:2], later[2:4], later[4:6], later[6:8], later[8]
    planes = exchange(chunks)
    local = call(
        local_kernel,
        struct((channels, x_local, SUBLANES, LANES)),
        "local",
        in_specs=held(3),
        out_specs=held(1)[0],
    )(point_weight, g_high, g_low)
    mode_rows_count = ky_local * 2 * hh_count
    chunks, stats, bias_grad = call(
        functools.partial(plane_kernel, scale),
        (
            struct((x_devices, y_devices, mode_rows_count, LANES)),
            struct((SUBLANES, LANES)),
            struct((1, channels)),
        ),
        "plane",
        in_specs=held(5),
        out_specs=held(3),
    )(planes, *tx, *ty)
    modes = exchange(chunks.reshape(devices, mode_rows_count, LANES))
    modes = modes.reshape(devices * mode_rows_count, LANES)
    chunks = call(
        functools.partial(back_kernel, cells, channels),
        struct((devices * SUBLANES, LANES)),
        "back",
        in_specs=held(2),
        out_specs=held(1)[0],
    )(modes, mode_weight)
    back = exchange(chunks.reshape(devices, SUBLANES, LANES))
    block = (kx_local, 1, 2, kz_count, pairs)
    mode_grad = call(
        functools.partial(outer_kernel, cells),
        struct(mode_weight.shape),
        "outer",
        grid=(ky_local,),
        in_specs=held(2),
        out_specs=pl.BlockSpec(block, lambda k: (0, k, 0, 0, 0)),
    )(modes, spread)
    chunks = call(
        inverse_kernel,
        struct((x_devices, y_devices, SUBLANES, LANES)),
        "inverse",
        in_specs=held(6),
        out_specs=held(1)[0],
    )(back, stats, *tyi, *tx)
    near = exchange(chunks.reshape(devices, SUBLANES, LANES))
    x_block = max(x_local // 4, 1)
    tile_spec = pl.BlockSpec((channels, x_block, SUBLANES, LANES), lambda k: (0, k, 0, 0))
    grad, point_grad = call(
        functools.partial(result_kernel, scale),
        (
            struct((channels, x_local, SUBLANES, LANES)),
            struct((channels, channels)),
        ),
        "result",
        grid=(x_local // x_block,),
        in_specs=held(4),
        out_specs=(tile_spec, pl.BlockSpec((channels, channels), lambda k: (0, 0))),
        scratch_shapes=[pltpu.VMEM((rows, 6 * LANES), BF16)],
    )(near.reshape(rows, LANES), *z_turned, local)
    return (from_tiles(grad, y_local, depth), point_grad, bias_grad[0], mode_grad)


def one_channel_each(inputs, mode_weight):
    channels, x_local, y_local, depth = inputs.shape
    kx_local, ky_local, _, kz_count, _ = mode_weight.shape
    return (
        channels == lax.axis_size("gx") * lax.axis_size("gy")
        and LANES % channels == 0
        and depth == 2 * LANES
        and y_local * 2 == SUBLANES
        and kz_count == 2 * HL
        and ky_local * 2 == SUBLANES
        and x_local * 2 * HL == LANES
        and kx_local == x_local
        and x_local * y_local == channels
    )


def shards(inputs, pre_act, grad_out, point_weight, mode_weight):
    plan = transposed if one_channel_each(inputs, mode_weight) else partial_sums
    return plan(inputs, pre_act, grad_out, point_weight, mode_weight)


def solution(mesh):
    return jax.shard_map(
        shards,
        mesh=mesh,
        in_specs=(
            P(None, "gx", "gy", None),
            P(None, "gx", "gy", None),
            P(None, "gx", "gy", None),
            P(),
            P("gx", "gy", None, None, None),
        ),
        out_specs=(P(None, "gx", "gy", None), P(), P(), P("gx", "gy", None, None, None)),
        check_vma=False,
    )
```

```python
import functools
import math

import jax
import jax.numpy as jnp
import numpy as np
from jax import lax
from jax.experimental import pallas as pl
from jax.experimental.pallas import tpu as pltpu
from jax.sharding import PartitionSpec as P

HIGHEST_PRECISION = lax.Precision.HIGHEST
ROOT_HALF = 0.7071067811865476
NORMAL_PEAK = 0.3989422804014327


def gelu_slope(pre_act):
    value = pre_act.astype(jnp.float32)
    return (
        0.5 * (1.0 + jax.scipy.special.erf(value * ROOT_HALF))
        + value * jnp.exp(-0.5 * value * value) * NORMAL_PEAK
    )


def phases(length, modes, wrapped, index, first, count):
    if wrapped:
        frequency = jnp.where(index < modes // 2, index, index + (length - modes))
    else:
        frequency = index
    places = first + jnp.arange(count, dtype=jnp.int32)
    turns = frequency[:, None] * places[None, :] % length
    angle = turns.astype(jnp.float32) * (2.0 * math.pi / length)
    return (jnp.cos(angle), jnp.sin(angle))


def transform(cos_table, sin_table, data, sign):
    real_part = data[..., 0, :]
    imag_part = data[..., 1, :]

    def apply(table, values):
        return jnp.tensordot(table, values, axes=1, precision=HIGHEST_PRECISION)

    if sign < 0:
        out_real = apply(cos_table, real_part) + apply(sin_table, imag_part)
        out_imag = apply(cos_table, imag_part) - apply(sin_table, real_part)
    else:
        out_real = apply(cos_table, real_part) - apply(sin_table, imag_part)
        out_imag = apply(cos_table, imag_part) + apply(sin_table, real_part)
    return jnp.stack([out_real, out_imag], axis=-2)


def depth_forward(field, kz_count):
    channels = field.shape[0]
    depth = field.shape[-1]
    cos_z, sin_z = phases(depth, kz_count, False, jnp.arange(kz_count, dtype=jnp.int32), 0, depth)
    real_part = jnp.einsum("cabz,kz->abkc", field, cos_z, precision=HIGHEST_PRECISION)
    imag_part = -jnp.einsum("cabz,kz->abkc", field, sin_z, precision=HIGHEST_PRECISION)
    lead = real_part.shape[:2]
    return jnp.stack(
        [
            real_part.reshape(lead + (kz_count * channels,)),
            imag_part.reshape(lead + (kz_count * channels,)),
        ],
        axis=2,
    )


def depth_inverse(spectrum, kz_count, channels, depth):
    lead = spectrum.shape[:2]
    split = spectrum.reshape(lead + (2, kz_count, channels))
    cos_z, sin_z = phases(depth, kz_count, False, jnp.arange(kz_count, dtype=jnp.int32), 0, depth)
    return jnp.einsum(
        "abkc,kz->cabz", split[:, :, 0], cos_z, precision=HIGHEST_PRECISION
    ) - jnp.einsum("abkc,kz->cabz", split[:, :, 1], sin_z, precision=HIGHEST_PRECISION)


def mode_work(spectrum_in, spectrum_grad, weight, cells):
    rows_a, rows_b, _, kz_count, _ = weight.shape
    channels = spectrum_in.shape[-1] // kz_count
    factor = (
        jnp.where(jnp.arange(kz_count, dtype=jnp.int32) == 0, 1.0, 2.0).astype(jnp.float32) / cells
    )
    shape = (rows_a, rows_b, 2, kz_count, channels)
    given = spectrum_in.reshape(shape)
    scaled = spectrum_grad.reshape(shape) * factor[:, None]
    mixing = weight.reshape(shape + (channels,))
    in_real = given[:, :, 0]
    in_imag = given[:, :, 1]
    grad_real = scaled[:, :, 0]
    grad_imag = scaled[:, :, 1]
    mix_real = mixing[:, :, 0]
    mix_imag = mixing[:, :, 1]

    def outer(left, right):
        return jnp.einsum("abki,abko->abkio", left, right, precision=HIGHEST_PRECISION)

    def mixed(values, matrix):
        return jnp.einsum("abko,abkio->abki", values, matrix, precision=HIGHEST_PRECISION)

    result_real = outer(in_real, grad_real) + outer(in_imag, grad_imag)
    result_imag = outer(in_real, grad_imag) - outer(in_imag, grad_real)
    mode_grad = jnp.stack([result_real, result_imag], axis=2).reshape(
        rows_a, rows_b, 2, kz_count, channels * channels
    )
    back_real = mixed(grad_real, mix_real) + mixed(grad_imag, mix_imag)
    back_imag = mixed(grad_imag, mix_real) - mixed(grad_real, mix_imag)
    back_spectrum = jnp.stack([back_real, back_imag], axis=2).reshape(
        rows_a, rows_b, 2, kz_count * channels
    )
    return (mode_grad, back_spectrum)


def joined_rows(main, extra):
    count = main.shape[0]
    return jnp.concatenate([main.reshape(count, -1), extra.reshape(count, -1)], axis=1)


def split_rows(result, main_shape, extra_shape):
    main_size = 1
    for item in main_shape[1:]:
        main_size = main_size * item
    main = result[:, :main_size].reshape(main_shape)
    extra = result[:, main_size:].reshape(extra_shape)
    return (main, extra)


def partial_sums(inputs, pre_act, grad_out, point_weight, mode_weight):
    channels, x_local, y_local, depth = inputs.shape
    kx_local, ky_local, _, kz_count, _ = mode_weight.shape
    x_devices = lax.axis_size("gx")
    y_devices = lax.axis_size("gy")
    x_length = x_local * x_devices
    y_length = y_local * y_devices
    kx_count = kx_local * x_devices
    ky_count = ky_local * y_devices
    cells = x_length * y_length * depth
    scale = 1.0 / math.sqrt(cells)
    x_offset = lax.axis_index("gx") * x_local
    y_offset = lax.axis_index("gy") * y_local
    width = kz_count * channels
    pair_width = 2 * width
    stat_count = channels * channels + channels
    mode_count = kx_count * ky_count
    field_in = inputs.astype(jnp.float32)
    pre_grad = grad_out.astype(jnp.float32) * gelu_slope(pre_act)
    weight_sum = jnp.einsum("ixyz,oxyz->io", field_in, pre_grad, precision=HIGHEST_PRECISION)
    bias_sum = jnp.sum(pre_grad, axis=(1, 2, 3))
    extra_cols = (stat_count + mode_count - 1) // mode_count
    stat_flat = jnp.concatenate([weight_sum.reshape(-1), bias_sum])
    grid = jnp.pad(stat_flat, (0, mode_count * extra_cols - stat_count)).reshape(
        kx_count, ky_count, extra_cols
    )
    spectra = jnp.stack(
        [depth_forward(field_in, kz_count), depth_forward(pre_grad, kz_count)], axis=2
    )
    along_y = jnp.swapaxes(spectra, 0, 1)
    grid_y = jnp.swapaxes(grid, 0, 1)
    cos_y, sin_y = phases(
        y_length,
        ky_count,
        True,
        jnp.arange(lax.axis_size("gy") * ky_local, dtype=jnp.int32),
        y_offset,
        y_local,
    )
    partial_y, extra_y = split_rows(
        lax.psum_scatter(
            joined_rows(transform(cos_y, sin_y, along_y, -1), grid_y),
            "gy",
            scatter_dimension=0,
            tiled=True,
        ),
        (ky_local, x_local, 2, 2, width),
        (ky_local, kx_count, extra_cols),
    )
    along_x = jnp.swapaxes(partial_y, 0, 1)
    extra_along = jnp.swapaxes(extra_y, 0, 1)
    cos_x, sin_x = phases(
        x_length,
        kx_count,
        True,
        jnp.arange(lax.axis_size("gx") * kx_local, dtype=jnp.int32),
        x_offset,
        x_local,
    )
    owned, owned_extra = split_rows(
        lax.psum_scatter(
            joined_rows(transform(cos_x, sin_x, along_x, -1), extra_along),
            "gx",
            scatter_dimension=0,
            tiled=True,
        ),
        (kx_local, ky_local, 2, 2, width),
        (kx_local, ky_local, extra_cols),
    )
    mode_grad, back_spectrum = mode_work(owned[:, :, 0], owned[:, :, 1], mode_weight, cells)
    back_joined = jnp.concatenate(
        [back_spectrum.reshape(kx_local, ky_local, pair_width), owned_extra], axis=2
    )
    piece = lax.all_gather(back_joined, "gx", axis=0, tiled=True)
    kx_index = jnp.arange(piece.shape[0], dtype=jnp.int32)
    cos_x, sin_x = phases(x_length, kx_count, True, kx_index, x_offset, x_local)
    main = piece[:, :, :pair_width].reshape(piece.shape[0], piece.shape[1], 2, width)
    near = transform(cos_x.T, sin_x.T, main, 1)
    near_stats = piece[:, :, pair_width:]
    side_cols = (kx_count * extra_cols + x_local - 1) // x_local
    side_flat = jnp.swapaxes(near_stats, 0, 1).reshape(ky_local, kx_count * extra_cols)
    side = jnp.swapaxes(side_flat.reshape(ky_local, x_local, side_cols), 0, 1)
    near_joined = jnp.concatenate([near.reshape(x_local, ky_local, pair_width), side], axis=2)
    piece = lax.all_gather(near_joined, "gy", axis=1, tiled=True)
    ky_index = jnp.arange(piece.shape[1], dtype=jnp.int32)
    cos_y, sin_y = phases(y_length, ky_count, True, ky_index, y_offset, y_local)
    main = piece[:, :, :pair_width].reshape(piece.shape[0], piece.shape[1], 2, width)
    moved = jnp.swapaxes(transform(cos_y.T, sin_y.T, jnp.swapaxes(main, 0, 1), 1), 0, 1)
    far_stats = piece[:, :, pair_width:]
    stats_rows = jnp.swapaxes(far_stats, 0, 1).reshape(ky_count, x_local * side_cols)
    stats_grid = jnp.swapaxes(stats_rows.reshape(ky_count, kx_count, extra_cols), 0, 1)
    stat_values = stats_grid.reshape(-1)[:stat_count]
    point_grad = stat_values[: channels * channels].reshape(channels, channels)
    bias_grad = stat_values[channels * channels :]
    local = jnp.einsum("io,oxyz->ixyz", point_weight, pre_grad, precision=HIGHEST_PRECISION)
    input_grad = local + depth_inverse(moved, kz_count, channels, depth)
    return (input_grad, point_grad * scale, bias_grad * scale, mode_grad)


LANES = 128
SUBLANES = 8
HL = 8
BF16 = jnp.bfloat16
F32 = jnp.float32


def split_table(table):
    high = table.astype(np.float32).astype(BF16)
    low = (table - high.astype(np.float64)).astype(np.float32).astype(BF16)
    return (high, low)


def split(values):
    high = values.astype(BF16)
    return (high, (values - high.astype(F32)).astype(BF16))


def dot(left, right):
    return jnp.dot(left, right, preferred_element_type=F32)


def dot_rows(left, right):
    return lax.dot_general(left, right, (((1,), (1,)), ((), ())), preferred_element_type=F32)


def product(left, right):
    left = jnp.concatenate([left[0], left[1], left[0]], axis=1)
    return dot(left, jnp.concatenate([right[0], right[0], right[1]], axis=0))


def product_rows(left, right):
    left = jnp.concatenate([left[0], left[1], left[0]], axis=1)
    return dot_rows(left, jnp.concatenate([right[0], right[0], right[1]], axis=1))


def iota(shape, axis):
    return lax.broadcasted_iota(jnp.int32, shape, axis)


def wave(length, modes):
    index = np.arange(modes)
    frequency = np.where(index < modes // 2, index, index + (length - modes))
    turns = frequency[:, None] * np.arange(length)[None, :] % length
    angle = turns * (2.0 * math.pi / length)
    return (np.cos(angle), np.sin(angle))


def depth_table(depth, kz_count, x_local):
    h = np.arange(kz_count)
    angle = (h[None, :] * np.arange(LANES)[:, None] % depth) * (2.0 * math.pi / depth)
    both = np.stack([np.cos(angle), -np.sin(angle)], axis=1)
    both = both.reshape(LANES, 2, kz_count // HL, 1, HL).transpose(0, 2, 3, 1, 4)
    return np.broadcast_to(both, (LANES, kz_count // HL, x_local, 2, HL)).reshape(LANES, -1)


def x_table(x_devices, x_local, kx_local):
    cos_x, sin_x = wave(x_devices * x_local, x_devices * kx_local)
    mix = np.array([[cos_x, -sin_x], [sin_x, cos_x]])
    mix = mix.reshape(2, 2, x_devices, kx_local, x_devices, x_local)
    full = np.einsum("pqakbx,hj->bxphaqkj", mix, np.eye(HL))
    size = x_devices * x_local * 2 * HL
    return full.reshape(size, -1)


def y_table(y_devices, y_local, ky_local, hh_count):
    pair = wave(y_devices * y_local, y_devices * ky_local)
    shape = (y_devices, ky_local, y_devices, y_local)
    parts = [
        np.einsum("akby,fg,hi->akgibfhy", t.reshape(shape), np.eye(2), np.eye(hh_count)).reshape(
            y_devices * ky_local * 2 * hh_count, -1
        )
        for t in pair
    ]
    return np.concatenate(parts, axis=1)


def y_inverse_table(y_devices, y_local, ky_local, hh_count):
    pair = wave(y_devices * y_local, y_devices * ky_local)
    shape = (y_devices, ky_local, y_devices, y_local)
    parts = [
        np.einsum("akby,hi->biyakh", t.reshape(shape), np.eye(hh_count)).reshape(
            y_devices * y_local * hh_count, -1
        )
        for t in pair
    ]
    return np.concatenate(parts, axis=1)


def spread_table(channels):
    left = np.repeat(np.eye(channels), channels, axis=1)
    right = np.tile(np.eye(channels), (1, LANES // channels))
    one = np.zeros((2 * channels, channels * channels + LANES))
    one[:channels, : channels * channels] = left
    one[channels:, channels * channels :] = right
    return np.concatenate([one, one], axis=0).astype(BF16)


def slot_mask(y_local):
    shape = (SUBLANES, LANES)
    return (iota(shape, 0) < y_local) & (iota(shape, 1) % (2 * HL) == HL)


def only_x(table, x):
    group = 2 * HL
    zeros = jnp.zeros((LANES, table.shape[1]), table.dtype)
    blocks = []
    for start in range(0, table.shape[0], LANES):
        at = start + x * group
        blocks += [zeros[: x * group], table[at : at + group], zeros[(x + 1) * group :]]
    return jnp.concatenate([block for block in blocks if block.shape[0] > 0], axis=0)


def grid_kernel(count, *refs):
    fields_hbm, refs = refs[:3], refs[3:]
    later_hbm, refs = refs[:count], refs[count:]
    s_ref, ghi_ref, glo_ref = refs[:3]
    later, refs = refs[3 : 3 + count], refs[3 + count :]
    in_ref, pre_ref, out_grad_ref, near_sems, far_sems = refs
    hi_ref, lo_ref = later[:2]
    channels, x_local = in_ref.shape[:2]
    y_local = SUBLANES // 2
    rows = channels * SUBLANES
    group = max(x_local // 4, 1)
    parts = []
    later_copies = [
        pltpu.make_async_copy(source, target, far_sems.at[index])
        for index, (source, target) in enumerate(zip(later_hbm, later))
    ]
    for x in range(0, x_local, group):
        at = (slice(None), pl.ds(x, group))
        copies = [
            pltpu.make_async_copy(source.at[at], target.at[at], near_sems.at[index, x // group])
            for index, (source, target) in enumerate(
                zip(fields_hbm, (in_ref, pre_ref, out_grad_ref))
            )
        ]
        parts.append(copies)
        for copy in copies:
            copy.start()
        if x == 0:
            for copy in later_copies[:2]:
                copy.start()
    for copy in later_copies[2:]:
        copy.start()
    raw, gram = 0.0, 0.0
    ones = jnp.ones((2 * SUBLANES, 2 * group * LANES), BF16)
    for first in range(0, x_local, group):
        for copy in parts[first // group]:
            copy.wait()
        fields, highs, lows = [], [], []
        for x in range(first, first + group):
            pre_grad = out_grad_ref[:, x].astype(F32) * gelu_slope(pre_ref[:, x])
            high, low = split(pre_grad.reshape(rows, LANES))
            ghi_ref[x] = high
            glo_ref[x] = low
            highs.append(high)
            lows.append(low)
            fields.append(in_ref[:, x].reshape(rows, LANES))
        if first == 0:
            for copy in later_copies[:2]:
                copy.wait()
        tables = [
            only_x(ref[...], x) for ref in (hi_ref, lo_ref) for x in range(first, first + group)
        ]
        table = jnp.concatenate(tables, axis=1)
        field = jnp.concatenate(fields * 2, axis=1)
        high = jnp.concatenate(highs * 2, axis=1)
        low = jnp.concatenate(lows * 2, axis=1)
        raw += dot_rows(jnp.concatenate([field, high, low], axis=0), table)
        both = jnp.concatenate(highs + lows, axis=1)
        gram += dot_rows(jnp.concatenate([field, ones], axis=0), both)
    raw_in, raw_grad = raw[:rows], raw[rows : 2 * rows] + raw[2 * rows :]
    gram, bias = gram[:rows], gram[rows : rows + SUBLANES]

    tile = (channels, SUBLANES, LANES)
    sign = jnp.where(iota(tile, 2) % 2 == 0, 1.0, -1.0)
    upper = iota(tile, 1) < y_local

    def joined(raw):
        even = raw[:, :LANES].reshape(tile)
        odd = raw[:, LANES:].reshape(tile)
        return jnp.where(
            upper,
            even + sign * pltpu.roll(even, y_local, 1),
            pltpu.roll(odd, y_local, 1) + sign * odd,
        )

    wide = (channels, SUBLANES, rows)
    row, col = iota(wide, 1), iota(wide, 2)
    trace = jnp.where(row == col % SUBLANES, gram.reshape(wide), 0.0)
    trace = jnp.sum(trace, axis=1, keepdims=True)
    at_row = row == col // SUBLANES // x_local
    weight_rows = split(jnp.where(at_row, trace, 0.0).reshape(rows, rows))
    flat = (rows, LANES)
    place = jnp.where(
        iota(flat, 1) == iota(flat, 0) // SUBLANES % x_local * (2 * HL) + HL, 1.0, 0.0
    ).astype(BF16)
    weight_slots = dot(weight_rows[0], place) + dot(weight_rows[1], place)
    bias_rows = split(jnp.where(at_row[0], bias, 0.0))
    bias_slots = dot(bias_rows[0], place) + dot(bias_rows[1], place)
    s_ref[:, 0] = joined(raw_in) + weight_slots.reshape(tile)
    s_ref[:, 1] = joined(raw_grad) + bias_slots[None]
    for copy in later_copies[2:]:
        copy.wait()


def slot_place(channels, x_local, y):
    lane, out = iota((LANES, channels), 0), iota((LANES, channels), 1)
    place = (lane == out % x_local * (2 * HL) + HL) & (out // x_local == y)
    return jnp.where(place, 1.0, 0.0)


def from_slots(taken, place):
    return jnp.dot(taken, place, precision=HIGHEST_PRECISION, preferred_element_type=F32)


def plane_kernel(r_ref, txh_ref, txl_ref, tyh_ref, tyl_ref, s_ref, stat_ref):
    x_devices, y_devices = s_ref.shape[:2]
    y_local = SUBLANES // 2
    stat_ref[...] = jnp.sum(r_ref[...], axis=0)
    values = jnp.where(slot_mask(y_local), 0.0, r_ref[...])
    values = values.reshape(x_devices, -1, LANES)
    wide = jnp.concatenate([values[g] for g in range(x_devices)], axis=1)
    along_x = product(split(wide), (txh_ref[...], txl_ref[...]))
    lane = iota((along_x.shape[0], LANES), 1)
    sign = jnp.where(lane < LANES // 2, 1.0, -1.0)
    turned = [
        sign * pltpu.roll(along_x[:, g * LANES : (g + 1) * LANES], LANES // 2, 1)
        for g in range(x_devices)
    ]
    both = jnp.concatenate([along_x, jnp.concatenate(turned, axis=1)], axis=0)
    along_y = product((tyh_ref[...], tyl_ref[...]), split(both))
    for g in range(x_devices):
        s_ref[g] = along_y[:, g * LANES : (g + 1) * LANES].reshape(s_ref.shape[1:])


def mode_rows(r_ref, picks, channels):
    stride = r_ref.shape[0] // channels
    taken = [r_ref[pl.ds(pick, channels, stride=stride), :] for pick in picks]
    return jnp.concatenate(taken, axis=0).T


def repeated(values, times):
    return jnp.concatenate([values] * times, axis=1)


def back_kernel(cells, channels, r_ref, weight_ref, s_ref):
    size = channels * channels
    kx_local, ky_local = weight_ref.shape[:2]
    count = kx_local * HL
    width = SUBLANES * channels
    shape = (2 * SUBLANES, 2 * width)
    sums = iota(shape, 0) == iota(shape, 1) % width // channels
    sums = jnp.where(sums, 1.0, 0.0).astype(BF16)
    group = LANES // channels // 2
    for start in range(0, ky_local, group):
        places = [(ky, hh) for ky in range(start, start + group) for hh in range(2)]
        modes = mode_rows(r_ref, [ky * 4 + 2 + hh for ky, hh in places], channels)
        row, lane = iota(modes.shape, 0), iota(modes.shape, 1)
        first = (row % HL == 0) & (lane // channels % 2 == 0)
        modes = modes * jnp.where(first, 1.0 / cells, 2.0 / cells)
        for index, (ky, hh) in enumerate(places):
            grad = jnp.where(lane // channels == index, modes, 0.0)
            shift = channels
            while shift < LANES:
                grad = grad + pltpu.roll(grad, shift, 1)
                shift = shift * 2
            grad_real = repeated(grad[:count], width // LANES)
            grad_imag = repeated(grad[count:], width // LANES)
            rows = slice(hh * HL, (hh + 1) * HL)
            for block in range(size // width):
                at = slice(block * width, (block + 1) * width)
                mix_real = weight_ref[:, ky, 0, rows, at].reshape(count, width)
                mix_imag = weight_ref[:, ky, 1, rows, at].reshape(count, width)
                terms = jnp.concatenate(
                    [
                        grad_real * mix_real + grad_imag * mix_imag,
                        grad_imag * mix_real - grad_real * mix_imag,
                    ],
                    axis=0,
                )
                back = dot_rows(sums, jnp.concatenate(split(terms), axis=1))
                at = block * SUBLANES * SUBLANES + ky * 2 + hh
                s_ref[pl.ds(at, SUBLANES, stride=SUBLANES), :] = back[:SUBLANES]


def outer_kernel(cells, r_ref, spread_ref, grad_ref):
    kx_local = grad_ref.shape[0]
    size = grad_ref.shape[-1]
    channels = spread_ref.shape[0] // 4
    ky = pl.program_id(0)
    half = LANES // 2
    modes = mode_rows(r_ref, [ky * 4 + f * 2 + hh for hh in range(2) for f in range(2)], channels)
    row, lane = iota(modes.shape, 0), iota(modes.shape, 1)
    first = (row % HL == 0) & (lane < half)
    factor = jnp.where(
        lane // channels % 2 == 1, jnp.where(first, 1.0 / cells, 2.0 / cells), 1.0
    )
    modes = modes * factor
    low = modes - modes.astype(BF16).astype(F32)
    left = jnp.concatenate(
        [
            jnp.where(lane < half, modes, pltpu.roll(low, half, 1)),
            jnp.where(lane < half, pltpu.roll(modes, half, 1), low),
        ],
        axis=0,
    ).astype(BF16)
    spread = dot(left, spread_ref[...])
    count = kx_local * HL
    for hh in range(2):
        real = spread[hh * 2 * count : hh * 2 * count + count]
        imag = spread[hh * 2 * count + count : (hh + 1) * 2 * count]
        in_real, in_imag = real[:, :size], imag[:, :size]
        times = size // LANES
        grad_real, grad_imag = repeated(real[:, size:], times), repeated(imag[:, size:], times)
        rows = pl.ds(hh * HL, HL)
        tile = (kx_local, HL, size)
        grad_ref[:, 0, 0, rows, :] = (in_real * grad_real + in_imag * grad_imag).reshape(tile)
        grad_ref[:, 0, 1, rows, :] = (in_real * grad_imag - in_imag * grad_real).reshape(tile)


def local_kernel(scale, weight_ref, ghi_ref, glo_ref, stat_ref, local_ref, bias_ref):
    channels, x_local = local_ref.shape[:2]
    rows = channels * SUBLANES
    bias = jnp.zeros((SUBLANES, channels), F32)
    for y in range(SUBLANES // 2):
        row = jnp.where(iota((SUBLANES, LANES), 0) == y, stat_ref[1], 0.0)
        bias += from_slots(row, slot_place(channels, x_local, y))
    bias_ref[...] = jnp.sum(bias, axis=0, keepdims=True) * scale
    spread = jnp.where(
        iota((rows, channels), 0) // SUBLANES == iota((rows, channels), 1), 1.0, 0.0
    )
    tall = jnp.dot(
        spread, weight_ref[...], precision=HIGHEST_PRECISION, preferred_element_type=F32
    )
    square = lax.dot_general(
        tall,
        spread,
        (((1,), (1,)), ((), ())),
        precision=HIGHEST_PRECISION,
        preferred_element_type=F32,
    )
    same = iota(square.shape, 0) % SUBLANES == iota(square.shape, 1) % SUBLANES
    high, low = split(jnp.where(same, square, 0.0))
    left = jnp.concatenate([high, high, low], axis=1)
    for x in range(x_local):
        right = jnp.concatenate([ghi_ref[x], glo_ref[x], ghi_ref[x]], axis=0)
        local_ref[:, x] = dot(left, right).reshape(channels, SUBLANES, LANES)


def inverse_kernel(r_ref, stat_ref, tyh_ref, tyl_ref, txh_ref, txl_ref, s_ref):
    x_devices, y_devices = s_ref.shape[:2]
    y_local = SUBLANES // 2
    values = r_ref[...].reshape(x_devices, y_devices * SUBLANES, LANES)
    lane = iota(values.shape[1:], 1)
    sign = jnp.where(lane < LANES // 2, -1.0, 1.0)
    wide = jnp.concatenate([values[g] for g in range(x_devices)], axis=1)
    turned = [sign * pltpu.roll(values[g], LANES // 2, 1) for g in range(x_devices)]
    both = jnp.concatenate([wide, jnp.concatenate(turned, axis=1)], axis=0)
    along_y = product((tyh_ref[...], tyl_ref[...]), split(both))
    along_x = product_rows(split(along_y), (txh_ref[...], txl_ref[...]))
    slots = slot_mask(y_local)
    for g in range(x_devices):
        block = along_x[:, g * LANES : (g + 1) * LANES].reshape(s_ref.shape[1:])
        s_ref[g] = jnp.where(slots, stat_ref[0], block)


def result_kernel(scale, r_ref, hi_ref, lo_ref, local_ref, grad_hbm, point_ref, grad_ref, sems):
    channels, x_local = grad_ref.shape[:2]
    y_local = SUBLANES // 2
    rows = channels * SUBLANES
    tile = (channels, SUBLANES, LANES)
    values = r_ref[...].reshape(tile)
    turned = pltpu.roll(values, y_local, 1)
    sign = jnp.where(iota(tile, 2) % 2 == 0, 1.0, -1.0)
    upper = iota(tile, 1) < y_local
    left = jnp.concatenate(
        [
            jnp.where(upper, values, sign * turned).reshape(rows, LANES),
            jnp.where(upper, turned, sign * values).reshape(rows, LANES),
        ],
        axis=1,
    )
    high, low = split(left)
    left = jnp.concatenate([high, low, high], axis=1)
    group = max(x_local // 4, 1)
    copies = []
    for first in range(0, x_local, group):
        places = range(first, first + group)
        t_hi = jnp.concatenate([only_x(hi_ref[...], x) for x in places], axis=1)
        t_lo = jnp.concatenate([only_x(lo_ref[...], x) for x in places], axis=1)
        block = dot(left, jnp.concatenate([t_hi, t_hi, t_lo], axis=0))
        for x in places:
            part = block[:, (x - first) * LANES : (x - first + 1) * LANES]
            grad_ref[:, x] = part.reshape(tile) + local_ref[:, x]
        at = (slice(None), pl.ds(first, group))
        sem = sems.at[first // group]
        copies.append(pltpu.make_async_copy(grad_ref.at[at], grad_hbm.at[at], sem))
        copies[-1].start()
    point = jnp.zeros(point_ref.shape, F32)
    for y in range(y_local):
        taken = r_ref[pl.ds(y, channels, stride=SUBLANES), :]
        point += from_slots(taken, slot_place(channels, x_local, y))
    point_ref[...] = point * scale
    for copy in copies:
        copy.wait()


def call(kernel, out_shape, name, vmem=16, **options):
    params = pltpu.CompilerParams(vmem_limit_bytes=vmem << 20)
    return pl.pallas_call(
        kernel, out_shape=out_shape, name=name, compiler_params=params, **options
    )


def held(count):
    return [pl.BlockSpec(memory_space=pltpu.VMEM)] * count


def to_tiles(array):
    lead, (rows, depth) = array.shape[:-2], array.shape[-2:]
    split_up = array.reshape(lead + (rows, depth // LANES, LANES))
    return jnp.swapaxes(split_up, -3, -2).reshape(lead + (SUBLANES, LANES))


def from_tiles(array, rows, depth):
    lead = array.shape[:-2]
    split_up = array.reshape(lead + (depth // LANES, rows, LANES))
    return jnp.swapaxes(split_up, -3, -2).reshape(lead + (rows, depth))


def transposed(inputs, pre_act, grad_out, point_weight, mode_weight):
    channels, x_local, y_local, depth = inputs.shape
    kx_local, ky_local, _, kz_count, pairs = mode_weight.shape
    x_devices = lax.axis_size("gx")
    y_devices = lax.axis_size("gy")
    devices = x_devices * y_devices
    hh_count = kz_count // HL
    cells = x_local * x_devices * y_local * y_devices * depth
    scale = 1.0 / math.sqrt(cells)
    axes = ("gx", "gy")
    rows = channels * SUBLANES

    def struct(shape, kind=F32):
        return jax.ShapeDtypeStruct(shape, kind)

    def exchange(chunks):
        return lax.all_to_all(chunks, axes, 0, 0)

    z_high, z_low = split_table(depth_table(depth, kz_count, x_local))
    tx = split_table(x_table(x_devices, x_local, kx_local))
    ty = split_table(y_table(y_devices, y_local, ky_local, hh_count))
    tyi = split_table(y_inverse_table(y_devices, y_local, ky_local, hh_count))
    spread = spread_table(channels)

    field_shape = (channels, x_local, SUBLANES, LANES)
    later = (z_high.T, z_low.T, *tx, *ty, *tyi, mode_weight)
    chunks, g_high, g_low, *later = call(
        functools.partial(grid_kernel, len(later)),
        (
            struct((channels, 2, SUBLANES, LANES)),
            struct((x_local, rows, LANES), BF16),
            struct((x_local, rows, LANES), BF16),
            *(struct(array.shape, array.dtype) for array in later),
        ),
        "grid",
        vmem=24,
        in_specs=[pl.BlockSpec(memory_space=pltpu.HBM)] * (3 + len(later)),
        out_specs=held(3 + len(later)),
        scratch_shapes=[
            *([pltpu.VMEM(field_shape, BF16)] * 3),
            pltpu.SemaphoreType.DMA((3, x_local)),
            pltpu.SemaphoreType.DMA((len(later),)),
        ],
    )(
        *(
            pltpu.with_memory_space_constraint(array, pltpu.HBM)
            for array in (
                to_tiles(inputs),
                to_tiles(pre_act),
                to_tiles(grad_out),
                *later,
            )
        )
    )
    z_turned, tx, ty, tyi, mode_weight = later[:2], later[2:4], later[4:6], later[6:8], later[8]
    planes = exchange(chunks)
    mode_rows_count = ky_local * 2 * hh_count
    chunks, stats = call(
        plane_kernel,
        (
            struct((x_devices, y_devices, mode_rows_count, LANES)),
            struct((2, SUBLANES, LANES)),
        ),
        "plane",
        in_specs=held(5),
        out_specs=held(2),
    )(planes, *tx, *ty)
    local, bias_grad = call(
        functools.partial(local_kernel, scale),
        (struct(field_shape), struct((1, channels))),
        "local",
        in_specs=held(4),
        out_specs=held(2),
    )(point_weight, g_high, g_low, stats)
    modes = exchange(chunks.reshape(devices, mode_rows_count, LANES))
    modes = modes.reshape(devices * mode_rows_count, LANES)
    chunks = call(
        functools.partial(back_kernel, cells, channels),
        struct((devices * SUBLANES, LANES)),
        "back",
        in_specs=held(2),
        out_specs=held(1)[0],
    )(modes, mode_weight)
    back = exchange(chunks.reshape(devices, SUBLANES, LANES))
    block = (kx_local, 1, 2, kz_count, pairs)
    mode_grad = call(
        functools.partial(outer_kernel, cells),
        struct(mode_weight.shape),
        "outer",
        grid=(ky_local,),
        in_specs=held(2),
        out_specs=pl.BlockSpec(block, lambda k: (0, k, 0, 0, 0)),
    )(modes, spread)
    chunks = call(
        inverse_kernel,
        struct((x_devices, y_devices, SUBLANES, LANES)),
        "inverse",
        in_specs=held(6),
        out_specs=held(1)[0],
    )(back, stats, *tyi, *tx)
    near = exchange(chunks.reshape(devices, SUBLANES, LANES))
    grad, point_grad = call(
        functools.partial(result_kernel, scale),
        (struct(field_shape), struct((channels, channels))),
        "result",
        in_specs=held(4),
        out_specs=(pl.BlockSpec(memory_space=pltpu.HBM), held(1)[0]),
        scratch_shapes=[pltpu.VMEM(field_shape, F32), pltpu.SemaphoreType.DMA((x_local,))],
    )(near.reshape(rows, LANES), *z_turned, local)
    return (from_tiles(grad, y_local, depth), point_grad, bias_grad[0], mode_grad)


def one_channel_each(inputs, mode_weight):
    channels, x_local, y_local, depth = inputs.shape
    kx_local, ky_local, _, kz_count, _ = mode_weight.shape
    return (
        channels == lax.axis_size("gx") * lax.axis_size("gy")
        and LANES % channels == 0
        and depth == 2 * LANES
        and y_local * 2 == SUBLANES
        and kz_count == 2 * HL
        and ky_local * 2 == SUBLANES
        and x_local * 2 * HL == LANES
        and kx_local == x_local
        and x_local * y_local == channels
    )


def shards(inputs, pre_act, grad_out, point_weight, mode_weight):
    plan = transposed if one_channel_each(inputs, mode_weight) else partial_sums
    return plan(inputs, pre_act, grad_out, point_weight, mode_weight)


def solution(mesh):
    return jax.shard_map(
        shards,
        mesh=mesh,
        in_specs=(
            P(None, "gx", "gy", None),
            P(None, "gx", "gy", None),
            P(None, "gx", "gy", None),
            P(),
            P("gx", "gy", None, None, None),
        ),
        out_specs=(P(None, "gx", "gy", None), P(), P(), P("gx", "gy", None, None, None)),
        check_vma=False,
    )
```

```python
import functools
import math

import jax
import jax.numpy as jnp
import numpy as np
from jax import lax
from jax.experimental import pallas as pl
from jax.experimental.pallas import tpu as pltpu
from jax.sharding import PartitionSpec as P

HIGHEST_PRECISION = lax.Precision.HIGHEST
ROOT_HALF = 0.7071067811865476
NORMAL_PEAK = 0.3989422804014327


def gelu_slope(pre_act):
    value = pre_act.astype(jnp.float32)
    return (
        0.5 * (1.0 + jax.scipy.special.erf(value * ROOT_HALF))
        + value * jnp.exp(-0.5 * value * value) * NORMAL_PEAK
    )


def phases(length, modes, wrapped, index, first, count):
    if wrapped:
        frequency = jnp.where(index < modes // 2, index, index + (length - modes))
    else:
        frequency = index
    places = first + jnp.arange(count, dtype=jnp.int32)
    turns = frequency[:, None] * places[None, :] % length
    angle = turns.astype(jnp.float32) * (2.0 * math.pi / length)
    return (jnp.cos(angle), jnp.sin(angle))


def transform(cos_table, sin_table, data, sign):
    real_part = data[..., 0, :]
    imag_part = data[..., 1, :]

    def apply(table, values):
        return jnp.tensordot(table, values, axes=1, precision=HIGHEST_PRECISION)

    if sign < 0:
        out_real = apply(cos_table, real_part) + apply(sin_table, imag_part)
        out_imag = apply(cos_table, imag_part) - apply(sin_table, real_part)
    else:
        out_real = apply(cos_table, real_part) - apply(sin_table, imag_part)
        out_imag = apply(cos_table, imag_part) + apply(sin_table, real_part)
    return jnp.stack([out_real, out_imag], axis=-2)


def depth_forward(field, kz_count):
    channels = field.shape[0]
    depth = field.shape[-1]
    cos_z, sin_z = phases(depth, kz_count, False, jnp.arange(kz_count, dtype=jnp.int32), 0, depth)
    real_part = jnp.einsum("cabz,kz->abkc", field, cos_z, precision=HIGHEST_PRECISION)
    imag_part = -jnp.einsum("cabz,kz->abkc", field, sin_z, precision=HIGHEST_PRECISION)
    lead = real_part.shape[:2]
    return jnp.stack(
        [
            real_part.reshape(lead + (kz_count * channels,)),
            imag_part.reshape(lead + (kz_count * channels,)),
        ],
        axis=2,
    )


def depth_inverse(spectrum, kz_count, channels, depth):
    lead = spectrum.shape[:2]
    split = spectrum.reshape(lead + (2, kz_count, channels))
    cos_z, sin_z = phases(depth, kz_count, False, jnp.arange(kz_count, dtype=jnp.int32), 0, depth)
    return jnp.einsum(
        "abkc,kz->cabz", split[:, :, 0], cos_z, precision=HIGHEST_PRECISION
    ) - jnp.einsum("abkc,kz->cabz", split[:, :, 1], sin_z, precision=HIGHEST_PRECISION)


def mode_work(spectrum_in, spectrum_grad, weight, cells):
    rows_a, rows_b, _, kz_count, _ = weight.shape
    channels = spectrum_in.shape[-1] // kz_count
    factor = (
        jnp.where(jnp.arange(kz_count, dtype=jnp.int32) == 0, 1.0, 2.0).astype(jnp.float32) / cells
    )
    shape = (rows_a, rows_b, 2, kz_count, channels)
    given = spectrum_in.reshape(shape)
    scaled = spectrum_grad.reshape(shape) * factor[:, None]
    mixing = weight.reshape(shape + (channels,))
    in_real = given[:, :, 0]
    in_imag = given[:, :, 1]
    grad_real = scaled[:, :, 0]
    grad_imag = scaled[:, :, 1]
    mix_real = mixing[:, :, 0]
    mix_imag = mixing[:, :, 1]

    def outer(left, right):
        return jnp.einsum("abki,abko->abkio", left, right, precision=HIGHEST_PRECISION)

    def mixed(values, matrix):
        return jnp.einsum("abko,abkio->abki", values, matrix, precision=HIGHEST_PRECISION)

    result_real = outer(in_real, grad_real) + outer(in_imag, grad_imag)
    result_imag = outer(in_real, grad_imag) - outer(in_imag, grad_real)
    mode_grad = jnp.stack([result_real, result_imag], axis=2).reshape(
        rows_a, rows_b, 2, kz_count, channels * channels
    )
    back_real = mixed(grad_real, mix_real) + mixed(grad_imag, mix_imag)
    back_imag = mixed(grad_imag, mix_real) - mixed(grad_real, mix_imag)
    back_spectrum = jnp.stack([back_real, back_imag], axis=2).reshape(
        rows_a, rows_b, 2, kz_count * channels
    )
    return (mode_grad, back_spectrum)


def joined_rows(main, extra):
    count = main.shape[0]
    return jnp.concatenate([main.reshape(count, -1), extra.reshape(count, -1)], axis=1)


def split_rows(result, main_shape, extra_shape):
    main_size = 1
    for item in main_shape[1:]:
        main_size = main_size * item
    main = result[:, :main_size].reshape(main_shape)
    extra = result[:, main_size:].reshape(extra_shape)
    return (main, extra)


def partial_sums(inputs, pre_act, grad_out, point_weight, mode_weight):
    channels, x_local, y_local, depth = inputs.shape
    kx_local, ky_local, _, kz_count, _ = mode_weight.shape
    x_devices = lax.axis_size("gx")
    y_devices = lax.axis_size("gy")
    x_length = x_local * x_devices
    y_length = y_local * y_devices
    kx_count = kx_local * x_devices
    ky_count = ky_local * y_devices
    cells = x_length * y_length * depth
    scale = 1.0 / math.sqrt(cells)
    x_offset = lax.axis_index("gx") * x_local
    y_offset = lax.axis_index("gy") * y_local
    width = kz_count * channels
    pair_width = 2 * width
    stat_count = channels * channels + channels
    mode_count = kx_count * ky_count
    field_in = inputs.astype(jnp.float32)
    pre_grad = grad_out.astype(jnp.float32) * gelu_slope(pre_act)
    weight_sum = jnp.einsum("ixyz,oxyz->io", field_in, pre_grad, precision=HIGHEST_PRECISION)
    bias_sum = jnp.sum(pre_grad, axis=(1, 2, 3))
    extra_cols = (stat_count + mode_count - 1) // mode_count
    stat_flat = jnp.concatenate([weight_sum.reshape(-1), bias_sum])
    grid = jnp.pad(stat_flat, (0, mode_count * extra_cols - stat_count)).reshape(
        kx_count, ky_count, extra_cols
    )
    spectra = jnp.stack(
        [depth_forward(field_in, kz_count), depth_forward(pre_grad, kz_count)], axis=2
    )
    along_y = jnp.swapaxes(spectra, 0, 1)
    grid_y = jnp.swapaxes(grid, 0, 1)
    cos_y, sin_y = phases(
        y_length,
        ky_count,
        True,
        jnp.arange(lax.axis_size("gy") * ky_local, dtype=jnp.int32),
        y_offset,
        y_local,
    )
    partial_y, extra_y = split_rows(
        lax.psum_scatter(
            joined_rows(transform(cos_y, sin_y, along_y, -1), grid_y),
            "gy",
            scatter_dimension=0,
            tiled=True,
        ),
        (ky_local, x_local, 2, 2, width),
        (ky_local, kx_count, extra_cols),
    )
    along_x = jnp.swapaxes(partial_y, 0, 1)
    extra_along = jnp.swapaxes(extra_y, 0, 1)
    cos_x, sin_x = phases(
        x_length,
        kx_count,
        True,
        jnp.arange(lax.axis_size("gx") * kx_local, dtype=jnp.int32),
        x_offset,
        x_local,
    )
    owned, owned_extra = split_rows(
        lax.psum_scatter(
            joined_rows(transform(cos_x, sin_x, along_x, -1), extra_along),
            "gx",
            scatter_dimension=0,
            tiled=True,
        ),
        (kx_local, ky_local, 2, 2, width),
        (kx_local, ky_local, extra_cols),
    )
    mode_grad, back_spectrum = mode_work(owned[:, :, 0], owned[:, :, 1], mode_weight, cells)
    back_joined = jnp.concatenate(
        [back_spectrum.reshape(kx_local, ky_local, pair_width), owned_extra], axis=2
    )
    piece = lax.all_gather(back_joined, "gx", axis=0, tiled=True)
    kx_index = jnp.arange(piece.shape[0], dtype=jnp.int32)
    cos_x, sin_x = phases(x_length, kx_count, True, kx_index, x_offset, x_local)
    main = piece[:, :, :pair_width].reshape(piece.shape[0], piece.shape[1], 2, width)
    near = transform(cos_x.T, sin_x.T, main, 1)
    near_stats = piece[:, :, pair_width:]
    side_cols = (kx_count * extra_cols + x_local - 1) // x_local
    side_flat = jnp.swapaxes(near_stats, 0, 1).reshape(ky_local, kx_count * extra_cols)
    side = jnp.swapaxes(side_flat.reshape(ky_local, x_local, side_cols), 0, 1)
    near_joined = jnp.concatenate([near.reshape(x_local, ky_local, pair_width), side], axis=2)
    piece = lax.all_gather(near_joined, "gy", axis=1, tiled=True)
    ky_index = jnp.arange(piece.shape[1], dtype=jnp.int32)
    cos_y, sin_y = phases(y_length, ky_count, True, ky_index, y_offset, y_local)
    main = piece[:, :, :pair_width].reshape(piece.shape[0], piece.shape[1], 2, width)
    moved = jnp.swapaxes(transform(cos_y.T, sin_y.T, jnp.swapaxes(main, 0, 1), 1), 0, 1)
    far_stats = piece[:, :, pair_width:]
    stats_rows = jnp.swapaxes(far_stats, 0, 1).reshape(ky_count, x_local * side_cols)
    stats_grid = jnp.swapaxes(stats_rows.reshape(ky_count, kx_count, extra_cols), 0, 1)
    stat_values = stats_grid.reshape(-1)[:stat_count]
    point_grad = stat_values[: channels * channels].reshape(channels, channels)
    bias_grad = stat_values[channels * channels :]
    local = jnp.einsum("io,oxyz->ixyz", point_weight, pre_grad, precision=HIGHEST_PRECISION)
    input_grad = local + depth_inverse(moved, kz_count, channels, depth)
    return (input_grad, point_grad * scale, bias_grad * scale, mode_grad)


LANES = 128
SUBLANES = 8
HL = 8
BF16 = jnp.bfloat16
F32 = jnp.float32


def split_table(table):
    high = table.astype(np.float32).astype(BF16)
    low = (table - high.astype(np.float64)).astype(np.float32).astype(BF16)
    return (high, low)


def split(values):
    high = values.astype(BF16)
    return (high, (values - high.astype(F32)).astype(BF16))


def dot(left, right):
    return jnp.dot(left, right, preferred_element_type=F32)


def dot_rows(left, right):
    return lax.dot_general(left, right, (((1,), (1,)), ((), ())), preferred_element_type=F32)


def product(left, right):
    left = jnp.concatenate([left[0], left[1], left[0]], axis=1)
    return dot(left, jnp.concatenate([right[0], right[0], right[1]], axis=0))


def product_rows(left, right):
    left = jnp.concatenate([left[0], left[1], left[0]], axis=1)
    return dot_rows(left, jnp.concatenate([right[0], right[0], right[1]], axis=1))


def iota(shape, axis):
    return lax.broadcasted_iota(jnp.int32, shape, axis)


def wave(length, modes):
    index = np.arange(modes)
    frequency = np.where(index < modes // 2, index, index + (length - modes))
    turns = frequency[:, None] * np.arange(length)[None, :] % length
    angle = turns * (2.0 * math.pi / length)
    return (np.cos(angle), np.sin(angle))


def depth_table(depth, kz_count, x_local):
    h = np.arange(kz_count)
    angle = (h[None, :] * np.arange(LANES)[:, None] % depth) * (2.0 * math.pi / depth)
    both = np.stack([np.cos(angle), -np.sin(angle)], axis=1)
    both = both.reshape(LANES, 2, kz_count // HL, 1, HL).transpose(0, 2, 3, 1, 4)
    return np.broadcast_to(both, (LANES, kz_count // HL, x_local, 2, HL)).reshape(LANES, -1)


def x_table(x_devices, x_local, kx_local):
    cos_x, sin_x = wave(x_devices * x_local, x_devices * kx_local)
    mix = np.array([[cos_x, -sin_x], [sin_x, cos_x]])
    mix = mix.reshape(2, 2, x_devices, kx_local, x_devices, x_local)
    full = np.einsum("pqakbx,hj->bxphaqkj", mix, np.eye(HL))
    size = x_devices * x_local * 2 * HL
    return full.reshape(size, -1)


def y_table(y_devices, y_local, ky_local, hh_count):
    pair = wave(y_devices * y_local, y_devices * ky_local)
    shape = (y_devices, ky_local, y_devices, y_local)
    parts = [
        np.einsum("akby,fg,hi->akgibfhy", t.reshape(shape), np.eye(2), np.eye(hh_count)).reshape(
            y_devices * ky_local * 2 * hh_count, -1
        )
        for t in pair
    ]
    return np.concatenate(parts, axis=1)


def y_inverse_table(y_devices, y_local, ky_local, hh_count):
    pair = wave(y_devices * y_local, y_devices * ky_local)
    shape = (y_devices, ky_local, y_devices, y_local)
    parts = [
        np.einsum("akby,hi->biyakh", t.reshape(shape), np.eye(hh_count)).reshape(
            y_devices * y_local * hh_count, -1
        )
        for t in pair
    ]
    return np.concatenate(parts, axis=1)


def spread_table(channels):
    left = np.repeat(np.eye(channels), channels, axis=1)
    right = np.tile(np.eye(channels), (1, LANES // channels))
    one = np.zeros((2 * channels, channels * channels + LANES))
    one[:channels, : channels * channels] = left
    one[channels:, channels * channels :] = right
    return np.concatenate([one, one], axis=0).astype(BF16)


def slot_mask(y_local):
    shape = (SUBLANES, LANES)
    return (iota(shape, 0) < y_local) & (iota(shape, 1) % (2 * HL) == HL)


def only_x(table, x):
    group = 2 * HL
    zeros = jnp.zeros((LANES, table.shape[1]), table.dtype)
    blocks = []
    for start in range(0, table.shape[0], LANES):
        at = start + x * group
        blocks += [zeros[: x * group], table[at : at + group], zeros[(x + 1) * group :]]
    return jnp.concatenate([block for block in blocks if block.shape[0] > 0], axis=0)


def grid_kernel(count, *refs):
    fields_hbm, refs = refs[:3], refs[3:]
    later_hbm, refs = refs[:count], refs[count:]
    s_ref, ghi_ref, glo_ref = refs[:3]
    later, refs = refs[3 : 3 + count], refs[3 + count :]
    in_ref, pre_ref, out_grad_ref, near_sems, far_sems = refs
    hi_ref, lo_ref = later[:2]
    channels, x_local = in_ref.shape[:2]
    y_local = SUBLANES // 2
    rows = channels * SUBLANES
    group = max(x_local // 4, 1)
    parts = []
    later_copies = [
        pltpu.make_async_copy(source, target, far_sems.at[index])
        for index, (source, target) in enumerate(zip(later_hbm, later))
    ]
    for x in range(0, x_local, group):
        at = (slice(None), pl.ds(x, group))
        copies = [
            pltpu.make_async_copy(source.at[at], target.at[at], near_sems.at[index, x // group])
            for index, (source, target) in enumerate(
                zip(fields_hbm, (in_ref, pre_ref, out_grad_ref))
            )
        ]
        parts.append(copies)
        for copy in copies:
            copy.start()
        if x == 0:
            for copy in later_copies[:2]:
                copy.start()
    for copy in later_copies[2:]:
        copy.start()
    raw, gram = 0.0, 0.0
    ones = jnp.ones((2 * SUBLANES, 2 * group * LANES), BF16)
    for first in range(0, x_local, group):
        for copy in parts[first // group]:
            copy.wait()
        fields, highs, lows = [], [], []
        for x in range(first, first + group):
            pre_grad = out_grad_ref[:, x].astype(F32) * gelu_slope(pre_ref[:, x])
            high, low = split(pre_grad.reshape(rows, LANES))
            ghi_ref[x] = high
            glo_ref[x] = low
            highs.append(high)
            lows.append(low)
            fields.append(in_ref[:, x].reshape(rows, LANES))
        if first == 0:
            for copy in later_copies[:2]:
                copy.wait()
        tables = [
            only_x(ref[...], x) for ref in (hi_ref, lo_ref) for x in range(first, first + group)
        ]
        table = jnp.concatenate(tables, axis=1)
        field = jnp.concatenate(fields * 2, axis=1)
        high = jnp.concatenate(highs * 2, axis=1)
        low = jnp.concatenate(lows * 2, axis=1)
        raw += dot_rows(jnp.concatenate([field, high, low], axis=0), table)
        both = jnp.concatenate(highs + lows, axis=1)
        gram += dot_rows(jnp.concatenate([field, ones], axis=0), both)
    raw_in, raw_grad = raw[:rows], raw[rows : 2 * rows] + raw[2 * rows :]
    gram, bias = gram[:rows], gram[rows : rows + SUBLANES]

    tile = (channels, SUBLANES, LANES)
    sign = jnp.where(iota(tile, 2) % 2 == 0, 1.0, -1.0)
    upper = iota(tile, 1) < y_local

    def joined(raw):
        even = raw[:, :LANES].reshape(tile)
        odd = raw[:, LANES:].reshape(tile)
        return jnp.where(
            upper,
            even + sign * pltpu.roll(even, y_local, 1),
            pltpu.roll(odd, y_local, 1) + sign * odd,
        )

    wide = (channels, SUBLANES, rows)
    row, col = iota(wide, 1), iota(wide, 2)
    trace = jnp.where(row == col % SUBLANES, gram.reshape(wide), 0.0)
    trace = jnp.sum(trace, axis=1, keepdims=True)
    at_row = row == col // SUBLANES // x_local
    weight_rows = split(jnp.where(at_row, trace, 0.0).reshape(rows, rows))
    flat = (rows, LANES)
    place = jnp.where(
        iota(flat, 1) == iota(flat, 0) // SUBLANES % x_local * (2 * HL) + HL, 1.0, 0.0
    ).astype(BF16)
    weight_slots = dot(weight_rows[0], place) + dot(weight_rows[1], place)
    bias_rows = split(jnp.where(at_row[0], bias, 0.0))
    bias_slots = dot(bias_rows[0], place) + dot(bias_rows[1], place)
    s_ref[:, 0] = joined(raw_in) + weight_slots.reshape(tile)
    s_ref[:, 1] = joined(raw_grad) + bias_slots[None]
    for copy in later_copies[2:]:
        copy.wait()


def slot_place(channels, x_local, y):
    lane, out = iota((LANES, channels), 0), iota((LANES, channels), 1)
    place = (lane == out % x_local * (2 * HL) + HL) & (out // x_local == y)
    return jnp.where(place, 1.0, 0.0)


def from_slots(taken, place):
    high = taken.astype(BF16)
    middle, low = split(taken - high.astype(F32))
    place = place.astype(BF16)
    return dot(
        jnp.concatenate([high, middle, low], axis=1), jnp.concatenate([place] * 3, axis=0)
    )


def plane_kernel(r_ref, txh_ref, txl_ref, tyh_ref, tyl_ref, s_ref, stat_ref):
    x_devices, y_devices = s_ref.shape[:2]
    y_local = SUBLANES // 2
    stat_ref[...] = jnp.sum(r_ref[...], axis=0)
    values = jnp.where(slot_mask(y_local), 0.0, r_ref[...])
    values = values.reshape(x_devices, -1, LANES)
    wide = jnp.concatenate([values[g] for g in range(x_devices)], axis=1)
    along_x = product(split(wide), (txh_ref[...], txl_ref[...]))
    lane = iota((along_x.shape[0], LANES), 1)
    sign = jnp.where(lane < LANES // 2, 1.0, -1.0)
    turned = [
        sign * pltpu.roll(along_x[:, g * LANES : (g + 1) * LANES], LANES // 2, 1)
        for g in range(x_devices)
    ]
    both = jnp.concatenate([along_x, jnp.concatenate(turned, axis=1)], axis=0)
    along_y = product((tyh_ref[...], tyl_ref[...]), split(both))
    for g in range(x_devices):
        s_ref[g] = along_y[:, g * LANES : (g + 1) * LANES].reshape(s_ref.shape[1:])


def mode_rows(r_ref, picks, channels):
    stride = r_ref.shape[0] // channels
    taken = [r_ref[pl.ds(pick, channels, stride=stride), :] for pick in picks]
    return jnp.concatenate(taken, axis=0).T


def repeated(values, times):
    return jnp.concatenate([values] * times, axis=1)


def back_kernel(cells, channels, r_ref, weight_ref, s_ref):
    size = channels * channels
    kx_local, ky_local = weight_ref.shape[:2]
    count = kx_local * HL
    width = SUBLANES * channels
    shape = (2 * SUBLANES, 2 * width)
    sums = iota(shape, 0) == iota(shape, 1) % width // channels
    sums = jnp.where(sums, 1.0, 0.0).astype(BF16)
    group = LANES // channels // 2
    for start in range(0, ky_local, group):
        places = [(ky, hh) for ky in range(start, start + group) for hh in range(2)]
        modes = mode_rows(r_ref, [ky * 4 + 2 + hh for ky, hh in places], channels)
        row, lane = iota(modes.shape, 0), iota(modes.shape, 1)
        first = (row % HL == 0) & (lane // channels % 2 == 0)
        modes = modes * jnp.where(first, 1.0 / cells, 2.0 / cells)
        for index, (ky, hh) in enumerate(places):
            grad = jnp.where(lane // channels == index, modes, 0.0)
            shift = channels
            while shift < LANES:
                grad = grad + pltpu.roll(grad, shift, 1)
                shift = shift * 2
            grad_real = repeated(grad[:count], width // LANES)
            grad_imag = repeated(grad[count:], width // LANES)
            rows = slice(hh * HL, (hh + 1) * HL)
            for block in range(size // width):
                at = slice(block * width, (block + 1) * width)
                mix_real = weight_ref[:, ky, 0, rows, at].reshape(count, width)
                mix_imag = weight_ref[:, ky, 1, rows, at].reshape(count, width)
                terms = jnp.concatenate(
                    [
                        grad_real * mix_real + grad_imag * mix_imag,
                        grad_imag * mix_real - grad_real * mix_imag,
                    ],
                    axis=0,
                )
                back = dot_rows(sums, jnp.concatenate(split(terms), axis=1))
                at = block * SUBLANES * SUBLANES + ky * 2 + hh
                s_ref[pl.ds(at, SUBLANES, stride=SUBLANES), :] = back[:SUBLANES]


def outer_kernel(cells, r_ref, spread_ref, grad_ref):
    kx_local = grad_ref.shape[0]
    size = grad_ref.shape[-1]
    channels = spread_ref.shape[0] // 4
    ky = pl.program_id(0)
    half = LANES // 2
    modes = mode_rows(r_ref, [ky * 4 + f * 2 + hh for hh in range(2) for f in range(2)], channels)
    row, lane = iota(modes.shape, 0), iota(modes.shape, 1)
    first = (row % HL == 0) & (lane < half)
    factor = jnp.where(
        lane // channels % 2 == 1, jnp.where(first, 1.0 / cells, 2.0 / cells), 1.0
    )
    modes = modes * factor
    low = modes - modes.astype(BF16).astype(F32)
    left = jnp.concatenate(
        [
            jnp.where(lane < half, modes, pltpu.roll(low, half, 1)),
            jnp.where(lane < half, pltpu.roll(modes, half, 1), low),
        ],
        axis=0,
    ).astype(BF16)
    spread = dot(left, spread_ref[...])
    count = kx_local * HL
    for hh in range(2):
        real = spread[hh * 2 * count : hh * 2 * count + count]
        imag = spread[hh * 2 * count + count : (hh + 1) * 2 * count]
        in_real, in_imag = real[:, :size], imag[:, :size]
        times = size // LANES
        grad_real, grad_imag = repeated(real[:, size:], times), repeated(imag[:, size:], times)
        rows = pl.ds(hh * HL, HL)
        tile = (kx_local, HL, size)
        grad_ref[:, 0, 0, rows, :] = (in_real * grad_real + in_imag * grad_imag).reshape(tile)
        grad_ref[:, 0, 1, rows, :] = (in_real * grad_imag - in_imag * grad_real).reshape(tile)


def local_kernel(scale, weight_ref, ghi_ref, glo_ref, stat_ref, local_ref, bias_ref):
    channels, x_local = local_ref.shape[:2]
    rows = channels * SUBLANES
    bias = jnp.zeros((SUBLANES, channels), F32)
    for y in range(SUBLANES // 2):
        row = jnp.where(iota((SUBLANES, LANES), 0) == y, stat_ref[1], 0.0)
        bias += from_slots(row, slot_place(channels, x_local, y))
    bias_ref[...] = jnp.sum(bias, axis=0, keepdims=True) * scale
    spread = jnp.where(
        iota((rows, channels), 0) // SUBLANES == iota((rows, channels), 1), 1.0, 0.0
    )
    tall = jnp.dot(
        spread, weight_ref[...], precision=HIGHEST_PRECISION, preferred_element_type=F32
    )
    square = lax.dot_general(
        tall,
        spread,
        (((1,), (1,)), ((), ())),
        precision=HIGHEST_PRECISION,
        preferred_element_type=F32,
    )
    same = iota(square.shape, 0) % SUBLANES == iota(square.shape, 1) % SUBLANES
    high, low = split(jnp.where(same, square, 0.0))
    left = jnp.concatenate([high, high, low], axis=1)
    for x in range(x_local):
        right = jnp.concatenate([ghi_ref[x], glo_ref[x], ghi_ref[x]], axis=0)
        local_ref[:, x] = dot(left, right).reshape(channels, SUBLANES, LANES)


def inverse_kernel(r_ref, stat_ref, tyh_ref, tyl_ref, txh_ref, txl_ref, s_ref):
    x_devices, y_devices = s_ref.shape[:2]
    y_local = SUBLANES // 2
    values = r_ref[...].reshape(x_devices, y_devices * SUBLANES, LANES)
    lane = iota(values.shape[1:], 1)
    sign = jnp.where(lane < LANES // 2, -1.0, 1.0)
    wide = jnp.concatenate([values[g] for g in range(x_devices)], axis=1)
    turned = [sign * pltpu.roll(values[g], LANES // 2, 1) for g in range(x_devices)]
    both = jnp.concatenate([wide, jnp.concatenate(turned, axis=1)], axis=0)
    along_y = product((tyh_ref[...], tyl_ref[...]), split(both))
    along_x = product_rows(split(along_y), (txh_ref[...], txl_ref[...]))
    slots = slot_mask(y_local)
    for g in range(x_devices):
        block = along_x[:, g * LANES : (g + 1) * LANES].reshape(s_ref.shape[1:])
        s_ref[g] = jnp.where(slots, stat_ref[0], block)


def result_kernel(scale, r_ref, hi_ref, lo_ref, local_ref, grad_hbm, point_ref, grad_ref, sems):
    channels, x_local = grad_ref.shape[:2]
    y_local = SUBLANES // 2
    rows = channels * SUBLANES
    tile = (channels, SUBLANES, LANES)
    values = r_ref[...].reshape(tile)
    turned = pltpu.roll(values, y_local, 1)
    sign = jnp.where(iota(tile, 2) % 2 == 0, 1.0, -1.0)
    upper = iota(tile, 1) < y_local
    halves = [
        jnp.where(upper, values, sign * turned).reshape(rows, LANES),
        jnp.where(upper, turned, sign * values).reshape(rows, LANES),
    ]
    highs = [half.astype(BF16).astype(F32) for half in halves]
    parts = [*highs, *(half - high for half, high in zip(halves, highs))]
    count = len(parts)
    width = LANES // count
    places = width // (2 * HL)
    parts = [part if k == 0 else pltpu.roll(part, k * width, 1) for k, part in enumerate(parts)]
    lane = iota((rows, LANES), 1) // width
    group = 2 * HL
    zeros = jnp.zeros((group, LANES), BF16)

    def rows_of(ref, part, first):
        blocks = []
        for k in range(places):
            at = part % 2 * LANES + (first + k) * group
            row = [zeros] * places
            row[k] = ref[at : at + group, :]
            blocks.append(jnp.concatenate(row, axis=1))
        return jnp.concatenate(blocks, axis=0)

    copies = []
    for index in range(x_local // places):
        first = index * places
        left = parts[0]
        for k in range(1, count):
            left = jnp.where(lane == (index + k) % count, parts[k], left)
        left = left.astype(BF16)
        order = [(k - index) % count for k in range(count)]
        right = [rows_of(ref, part, first) for ref in (hi_ref, lo_ref) for part in order]
        block = dot(jnp.concatenate([left, left], axis=1), jnp.concatenate(right, axis=0))
        for k in range(places):
            part = block[:, k * LANES : (k + 1) * LANES]
            grad_ref[:, first + k] = part.reshape(tile) + local_ref[:, first + k]
        at = (slice(None), pl.ds(first, places))
        copies.append(pltpu.make_async_copy(grad_ref.at[at], grad_hbm.at[at], sems.at[index]))
        copies[-1].start()
    point = jnp.zeros(point_ref.shape, F32)
    for y in range(y_local):
        taken = r_ref[pl.ds(y, channels, stride=SUBLANES), :]
        point += from_slots(taken, slot_place(channels, x_local, y))
    point_ref[...] = point * scale
    for copy in copies:
        copy.wait()


def call(kernel, out_shape, name, vmem=16, **options):
    params = pltpu.CompilerParams(vmem_limit_bytes=vmem << 20)
    return pl.pallas_call(
        kernel, out_shape=out_shape, name=name, compiler_params=params, **options
    )


def held(count):
    return [pl.BlockSpec(memory_space=pltpu.VMEM)] * count


def to_tiles(array):
    lead, (rows, depth) = array.shape[:-2], array.shape[-2:]
    split_up = array.reshape(lead + (rows, depth // LANES, LANES))
    return jnp.swapaxes(split_up, -3, -2).reshape(lead + (SUBLANES, LANES))


def from_tiles(array, rows, depth):
    lead = array.shape[:-2]
    split_up = array.reshape(lead + (depth // LANES, rows, LANES))
    return jnp.swapaxes(split_up, -3, -2).reshape(lead + (rows, depth))


def transposed(inputs, pre_act, grad_out, point_weight, mode_weight):
    channels, x_local, y_local, depth = inputs.shape
    kx_local, ky_local, _, kz_count, pairs = mode_weight.shape
    x_devices = lax.axis_size("gx")
    y_devices = lax.axis_size("gy")
    devices = x_devices * y_devices
    hh_count = kz_count // HL
    cells = x_local * x_devices * y_local * y_devices * depth
    scale = 1.0 / math.sqrt(cells)
    axes = ("gx", "gy")
    rows = channels * SUBLANES

    def struct(shape, kind=F32):
        return jax.ShapeDtypeStruct(shape, kind)

    def exchange(chunks):
        return lax.all_to_all(chunks, axes, 0, 0)

    z_high, z_low = split_table(depth_table(depth, kz_count, x_local))
    tx = split_table(x_table(x_devices, x_local, kx_local))
    ty = split_table(y_table(y_devices, y_local, ky_local, hh_count))
    tyi = split_table(y_inverse_table(y_devices, y_local, ky_local, hh_count))
    spread = spread_table(channels)

    field_shape = (channels, x_local, SUBLANES, LANES)
    later = (z_high.T, z_low.T, *tx, *ty, *tyi, mode_weight)
    chunks, g_high, g_low, *later = call(
        functools.partial(grid_kernel, len(later)),
        (
            struct((channels, 2, SUBLANES, LANES)),
            struct((x_local, rows, LANES), BF16),
            struct((x_local, rows, LANES), BF16),
            *(struct(array.shape, array.dtype) for array in later),
        ),
        "grid",
        vmem=24,
        in_specs=[pl.BlockSpec(memory_space=pltpu.HBM)] * (3 + len(later)),
        out_specs=held(3 + len(later)),
        scratch_shapes=[
            *([pltpu.VMEM(field_shape, BF16)] * 3),
            pltpu.SemaphoreType.DMA((3, x_local)),
            pltpu.SemaphoreType.DMA((len(later),)),
        ],
    )(
        *(
            pltpu.with_memory_space_constraint(array, pltpu.HBM)
            for array in (
                to_tiles(inputs),
                to_tiles(pre_act),
                to_tiles(grad_out),
                *later,
            )
        )
    )
    z_turned, tx, ty, tyi, mode_weight = later[:2], later[2:4], later[4:6], later[6:8], later[8]
    planes = exchange(chunks)
    mode_rows_count = ky_local * 2 * hh_count
    chunks, stats = call(
        plane_kernel,
        (
            struct((x_devices, y_devices, mode_rows_count, LANES)),
            struct((2, SUBLANES, LANES)),
        ),
        "plane",
        in_specs=held(5),
        out_specs=held(2),
    )(planes, *tx, *ty)
    local, bias_grad = call(
        functools.partial(local_kernel, scale),
        (struct(field_shape), struct((1, channels))),
        "local",
        in_specs=held(4),
        out_specs=held(2),
    )(point_weight, g_high, g_low, stats)
    modes = exchange(chunks.reshape(devices, mode_rows_count, LANES))
    modes = modes.reshape(devices * mode_rows_count, LANES)
    chunks = call(
        functools.partial(back_kernel, cells, channels),
        struct((devices * SUBLANES, LANES)),
        "back",
        in_specs=held(2),
        out_specs=held(1)[0],
    )(modes, mode_weight)
    back = exchange(chunks.reshape(devices, SUBLANES, LANES))
    block = (kx_local, 1, 2, kz_count, pairs)
    mode_grad = call(
        functools.partial(outer_kernel, cells),
        struct(mode_weight.shape),
        "outer",
        grid=(ky_local,),
        in_specs=held(2),
        out_specs=pl.BlockSpec(block, lambda k: (0, k, 0, 0, 0)),
    )(modes, spread)
    chunks = call(
        inverse_kernel,
        struct((x_devices, y_devices, SUBLANES, LANES)),
        "inverse",
        in_specs=held(6),
        out_specs=held(1)[0],
    )(back, stats, *tyi, *tx)
    near = exchange(chunks.reshape(devices, SUBLANES, LANES))
    grad, point_grad = call(
        functools.partial(result_kernel, scale),
        (struct(field_shape), struct((channels, channels))),
        "result",
        in_specs=held(4),
        out_specs=(pl.BlockSpec(memory_space=pltpu.HBM), held(1)[0]),
        scratch_shapes=[pltpu.VMEM(field_shape, F32), pltpu.SemaphoreType.DMA((x_local,))],
    )(near.reshape(rows, LANES), *z_turned, local)
    return (from_tiles(grad, y_local, depth), point_grad, bias_grad[0], mode_grad)


def one_channel_each(inputs, mode_weight):
    channels, x_local, y_local, depth = inputs.shape
    kx_local, ky_local, _, kz_count, _ = mode_weight.shape
    return (
        channels == lax.axis_size("gx") * lax.axis_size("gy")
        and LANES % channels == 0
        and depth == 2 * LANES
        and y_local * 2 == SUBLANES
        and kz_count == 2 * HL
        and ky_local * 2 == SUBLANES
        and x_local * 2 * HL == LANES
        and kx_local == x_local
        and x_local * y_local == channels
    )


def shards(inputs, pre_act, grad_out, point_weight, mode_weight):
    plan = transposed if one_channel_each(inputs, mode_weight) else partial_sums
    return plan(inputs, pre_act, grad_out, point_weight, mode_weight)


def solution(mesh):
    return jax.shard_map(
        shards,
        mesh=mesh,
        in_specs=(
            P(None, "gx", "gy", None),
            P(None, "gx", "gy", None),
            P(None, "gx", "gy", None),
            P(),
            P("gx", "gy", None, None, None),
        ),
        out_specs=(P(None, "gx", "gy", None), P(), P(), P("gx", "gy", None, None, None)),
        check_vma=False,
    )
```

```python
import functools
import math

import jax
import jax.numpy as jnp
import numpy as np
from jax import lax
from jax.experimental import pallas as pl
from jax.experimental.pallas import tpu as pltpu
from jax.sharding import PartitionSpec as P

HIGHEST_PRECISION = lax.Precision.HIGHEST
ROOT_HALF = 0.7071067811865476
NORMAL_PEAK = 0.3989422804014327


def gelu_slope(pre_act):
    value = pre_act.astype(jnp.float32)
    return (
        0.5 * (1.0 + jax.scipy.special.erf(value * ROOT_HALF))
        + value * jnp.exp(-0.5 * value * value) * NORMAL_PEAK
    )


def phases(length, modes, wrapped, index, first, count):
    if wrapped:
        frequency = jnp.where(index < modes // 2, index, index + (length - modes))
    else:
        frequency = index
    places = first + jnp.arange(count, dtype=jnp.int32)
    turns = frequency[:, None] * places[None, :] % length
    angle = turns.astype(jnp.float32) * (2.0 * math.pi / length)
    return (jnp.cos(angle), jnp.sin(angle))


def transform(cos_table, sin_table, data, sign):
    real_part = data[..., 0, :]
    imag_part = data[..., 1, :]

    def apply(table, values):
        return jnp.tensordot(table, values, axes=1, precision=HIGHEST_PRECISION)

    if sign < 0:
        out_real = apply(cos_table, real_part) + apply(sin_table, imag_part)
        out_imag = apply(cos_table, imag_part) - apply(sin_table, real_part)
    else:
        out_real = apply(cos_table, real_part) - apply(sin_table, imag_part)
        out_imag = apply(cos_table, imag_part) + apply(sin_table, real_part)
    return jnp.stack([out_real, out_imag], axis=-2)


def depth_forward(field, kz_count):
    channels = field.shape[0]
    depth = field.shape[-1]
    cos_z, sin_z = phases(depth, kz_count, False, jnp.arange(kz_count, dtype=jnp.int32), 0, depth)
    real_part = jnp.einsum("cabz,kz->abkc", field, cos_z, precision=HIGHEST_PRECISION)
    imag_part = -jnp.einsum("cabz,kz->abkc", field, sin_z, precision=HIGHEST_PRECISION)
    lead = real_part.shape[:2]
    return jnp.stack(
        [
            real_part.reshape(lead + (kz_count * channels,)),
            imag_part.reshape(lead + (kz_count * channels,)),
        ],
        axis=2,
    )


def depth_inverse(spectrum, kz_count, channels, depth):
    lead = spectrum.shape[:2]
    split = spectrum.reshape(lead + (2, kz_count, channels))
    cos_z, sin_z = phases(depth, kz_count, False, jnp.arange(kz_count, dtype=jnp.int32), 0, depth)
    return jnp.einsum(
        "abkc,kz->cabz", split[:, :, 0], cos_z, precision=HIGHEST_PRECISION
    ) - jnp.einsum("abkc,kz->cabz", split[:, :, 1], sin_z, precision=HIGHEST_PRECISION)


def mode_work(spectrum_in, spectrum_grad, weight, cells):
    rows_a, rows_b, _, kz_count, _ = weight.shape
    channels = spectrum_in.shape[-1] // kz_count
    factor = (
        jnp.where(jnp.arange(kz_count, dtype=jnp.int32) == 0, 1.0, 2.0).astype(jnp.float32) / cells
    )
    shape = (rows_a, rows_b, 2, kz_count, channels)
    given = spectrum_in.reshape(shape)
    scaled = spectrum_grad.reshape(shape) * factor[:, None]
    mixing = weight.reshape(shape + (channels,))
    in_real = given[:, :, 0]
    in_imag = given[:, :, 1]
    grad_real = scaled[:, :, 0]
    grad_imag = scaled[:, :, 1]
    mix_real = mixing[:, :, 0]
    mix_imag = mixing[:, :, 1]

    def outer(left, right):
        return jnp.einsum("abki,abko->abkio", left, right, precision=HIGHEST_PRECISION)

    def mixed(values, matrix):
        return jnp.einsum("abko,abkio->abki", values, matrix, precision=HIGHEST_PRECISION)

    result_real = outer(in_real, grad_real) + outer(in_imag, grad_imag)
    result_imag = outer(in_real, grad_imag) - outer(in_imag, grad_real)
    mode_grad = jnp.stack([result_real, result_imag], axis=2).reshape(
        rows_a, rows_b, 2, kz_count, channels * channels
    )
    back_real = mixed(grad_real, mix_real) + mixed(grad_imag, mix_imag)
    back_imag = mixed(grad_imag, mix_real) - mixed(grad_real, mix_imag)
    back_spectrum = jnp.stack([back_real, back_imag], axis=2).reshape(
        rows_a, rows_b, 2, kz_count * channels
    )
    return (mode_grad, back_spectrum)


def joined_rows(main, extra):
    count = main.shape[0]
    return jnp.concatenate([main.reshape(count, -1), extra.reshape(count, -1)], axis=1)


def split_rows(result, main_shape, extra_shape):
    main_size = 1
    for item in main_shape[1:]:
        main_size = main_size * item
    main = result[:, :main_size].reshape(main_shape)
    extra = result[:, main_size:].reshape(extra_shape)
    return (main, extra)


def partial_sums(inputs, pre_act, grad_out, point_weight, mode_weight):
    channels, x_local, y_local, depth = inputs.shape
    kx_local, ky_local, _, kz_count, _ = mode_weight.shape
    x_devices = lax.axis_size("gx")
    y_devices = lax.axis_size("gy")
    x_length = x_local * x_devices
    y_length = y_local * y_devices
    kx_count = kx_local * x_devices
    ky_count = ky_local * y_devices
    cells = x_length * y_length * depth
    scale = 1.0 / math.sqrt(cells)
    x_offset = lax.axis_index("gx") * x_local
    y_offset = lax.axis_index("gy") * y_local
    width = kz_count * channels
    pair_width = 2 * width
    stat_count = channels * channels + channels
    mode_count = kx_count * ky_count
    field_in = inputs.astype(jnp.float32)
    pre_grad = grad_out.astype(jnp.float32) * gelu_slope(pre_act)
    weight_sum = jnp.einsum("ixyz,oxyz->io", field_in, pre_grad, precision=HIGHEST_PRECISION)
    bias_sum = jnp.sum(pre_grad, axis=(1, 2, 3))
    extra_cols = (stat_count + mode_count - 1) // mode_count
    stat_flat = jnp.concatenate([weight_sum.reshape(-1), bias_sum])
    grid = jnp.pad(stat_flat, (0, mode_count * extra_cols - stat_count)).reshape(
        kx_count, ky_count, extra_cols
    )
    spectra = jnp.stack(
        [depth_forward(field_in, kz_count), depth_forward(pre_grad, kz_count)], axis=2
    )
    along_y = jnp.swapaxes(spectra, 0, 1)
    grid_y = jnp.swapaxes(grid, 0, 1)
    cos_y, sin_y = phases(
        y_length,
        ky_count,
        True,
        jnp.arange(lax.axis_size("gy") * ky_local, dtype=jnp.int32),
        y_offset,
        y_local,
    )
    partial_y, extra_y = split_rows(
        lax.psum_scatter(
            joined_rows(transform(cos_y, sin_y, along_y, -1), grid_y),
            "gy",
            scatter_dimension=0,
            tiled=True,
        ),
        (ky_local, x_local, 2, 2, width),
        (ky_local, kx_count, extra_cols),
    )
    along_x = jnp.swapaxes(partial_y, 0, 1)
    extra_along = jnp.swapaxes(extra_y, 0, 1)
    cos_x, sin_x = phases(
        x_length,
        kx_count,
        True,
        jnp.arange(lax.axis_size("gx") * kx_local, dtype=jnp.int32),
        x_offset,
        x_local,
    )
    owned, owned_extra = split_rows(
        lax.psum_scatter(
            joined_rows(transform(cos_x, sin_x, along_x, -1), extra_along),
            "gx",
            scatter_dimension=0,
            tiled=True,
        ),
        (kx_local, ky_local, 2, 2, width),
        (kx_local, ky_local, extra_cols),
    )
    mode_grad, back_spectrum = mode_work(owned[:, :, 0], owned[:, :, 1], mode_weight, cells)
    back_joined = jnp.concatenate(
        [back_spectrum.reshape(kx_local, ky_local, pair_width), owned_extra], axis=2
    )
    piece = lax.all_gather(back_joined, "gx", axis=0, tiled=True)
    kx_index = jnp.arange(piece.shape[0], dtype=jnp.int32)
    cos_x, sin_x = phases(x_length, kx_count, True, kx_index, x_offset, x_local)
    main = piece[:, :, :pair_width].reshape(piece.shape[0], piece.shape[1], 2, width)
    near = transform(cos_x.T, sin_x.T, main, 1)
    near_stats = piece[:, :, pair_width:]
    side_cols = (kx_count * extra_cols + x_local - 1) // x_local
    side_flat = jnp.swapaxes(near_stats, 0, 1).reshape(ky_local, kx_count * extra_cols)
    side = jnp.swapaxes(side_flat.reshape(ky_local, x_local, side_cols), 0, 1)
    near_joined = jnp.concatenate([near.reshape(x_local, ky_local, pair_width), side], axis=2)
    piece = lax.all_gather(near_joined, "gy", axis=1, tiled=True)
    ky_index = jnp.arange(piece.shape[1], dtype=jnp.int32)
    cos_y, sin_y = phases(y_length, ky_count, True, ky_index, y_offset, y_local)
    main = piece[:, :, :pair_width].reshape(piece.shape[0], piece.shape[1], 2, width)
    moved = jnp.swapaxes(transform(cos_y.T, sin_y.T, jnp.swapaxes(main, 0, 1), 1), 0, 1)
    far_stats = piece[:, :, pair_width:]
    stats_rows = jnp.swapaxes(far_stats, 0, 1).reshape(ky_count, x_local * side_cols)
    stats_grid = jnp.swapaxes(stats_rows.reshape(ky_count, kx_count, extra_cols), 0, 1)
    stat_values = stats_grid.reshape(-1)[:stat_count]
    point_grad = stat_values[: channels * channels].reshape(channels, channels)
    bias_grad = stat_values[channels * channels :]
    local = jnp.einsum("io,oxyz->ixyz", point_weight, pre_grad, precision=HIGHEST_PRECISION)
    input_grad = local + depth_inverse(moved, kz_count, channels, depth)
    return (input_grad, point_grad * scale, bias_grad * scale, mode_grad)


LANES = 128
SUBLANES = 8
HL = 8
BF16 = jnp.bfloat16
F32 = jnp.float32


def split_table(table):
    high = table.astype(np.float32).astype(BF16)
    low = (table - high.astype(np.float64)).astype(np.float32).astype(BF16)
    return (high, low)


def split(values):
    high = values.astype(BF16)
    return (high, (values - high.astype(F32)).astype(BF16))


def dot(left, right):
    return jnp.dot(left, right, preferred_element_type=F32)


def dot_rows(left, right):
    return lax.dot_general(left, right, (((1,), (1,)), ((), ())), preferred_element_type=F32)


def product(left, right):
    left = jnp.concatenate([left[0], left[1], left[0]], axis=1)
    return dot(left, jnp.concatenate([right[0], right[0], right[1]], axis=0))


def product_rows(left, right):
    left = jnp.concatenate([left[0], left[1], left[0]], axis=1)
    return dot_rows(left, jnp.concatenate([right[0], right[0], right[1]], axis=1))


def iota(shape, axis):
    return lax.broadcasted_iota(jnp.int32, shape, axis)


def wave(length, modes):
    index = np.arange(modes)
    frequency = np.where(index < modes // 2, index, index + (length - modes))
    turns = frequency[:, None] * np.arange(length)[None, :] % length
    angle = turns * (2.0 * math.pi / length)
    return (np.cos(angle), np.sin(angle))


def depth_table(depth, kz_count, x_local):
    h = np.arange(kz_count)
    angle = (h[None, :] * np.arange(LANES)[:, None] % depth) * (2.0 * math.pi / depth)
    both = np.stack([np.cos(angle), -np.sin(angle)], axis=1)
    both = both.reshape(LANES, 2, kz_count // HL, 1, HL).transpose(0, 2, 3, 1, 4)
    return np.broadcast_to(both, (LANES, kz_count // HL, x_local, 2, HL)).reshape(LANES, -1)


def x_table(x_devices, x_local, kx_local):
    cos_x, sin_x = wave(x_devices * x_local, x_devices * kx_local)
    mix = np.array([[cos_x, -sin_x], [sin_x, cos_x]])
    mix = mix.reshape(2, 2, x_devices, kx_local, x_devices, x_local)
    full = np.einsum("pqakbx,hj->bxphaqkj", mix, np.eye(HL))
    size = x_devices * x_local * 2 * HL
    return full.reshape(size, -1)


def y_table(y_devices, y_local, ky_local, hh_count):
    pair = wave(y_devices * y_local, y_devices * ky_local)
    shape = (y_devices, ky_local, y_devices, y_local)
    parts = [
        np.einsum("akby,fg,hi->akgibfhy", t.reshape(shape), np.eye(2), np.eye(hh_count)).reshape(
            y_devices * ky_local * 2 * hh_count, -1
        )
        for t in pair
    ]
    return np.concatenate(parts, axis=1)


def y_inverse_table(y_devices, y_local, ky_local, hh_count):
    pair = wave(y_devices * y_local, y_devices * ky_local)
    shape = (y_devices, ky_local, y_devices, y_local)
    parts = [
        np.einsum("akby,hi->biyakh", t.reshape(shape), np.eye(hh_count)).reshape(
            y_devices * y_local * hh_count, -1
        )
        for t in pair
    ]
    return np.concatenate(parts, axis=1)


def spread_table(channels):
    left = np.repeat(np.eye(channels), channels, axis=1)
    right = np.tile(np.eye(channels), (1, LANES // channels))
    one = np.zeros((2 * channels, channels * channels + LANES))
    one[:channels, : channels * channels] = left
    one[channels:, channels * channels :] = right
    return np.concatenate([one, one], axis=0).astype(BF16)


def slot_mask(y_local):
    shape = (SUBLANES, LANES)
    return (iota(shape, 0) < y_local) & (iota(shape, 1) % (2 * HL) == HL)


def only_x(table, x):
    group = 2 * HL
    zeros = jnp.zeros((LANES, table.shape[1]), table.dtype)
    blocks = []
    for start in range(0, table.shape[0], LANES):
        at = start + x * group
        blocks += [zeros[: x * group], table[at : at + group], zeros[(x + 1) * group :]]
    return jnp.concatenate([block for block in blocks if block.shape[0] > 0], axis=0)


def grid_kernel(count, *refs):
    fields_hbm, refs = refs[:3], refs[3:]
    later_hbm, refs = refs[:count], refs[count:]
    s_ref, ghi_ref, glo_ref = refs[:3]
    later, refs = refs[3 : 3 + count], refs[3 + count :]
    in_ref, pre_ref, out_grad_ref, near_sems, far_sems = refs
    hi_ref, lo_ref = later[:2]
    channels, x_local = in_ref.shape[:2]
    y_local = SUBLANES // 2
    rows = channels * SUBLANES
    group = max(x_local // 4, 1)
    parts = []
    later_copies = [
        pltpu.make_async_copy(source, target, far_sems.at[index])
        for index, (source, target) in enumerate(zip(later_hbm, later))
    ]
    for x in range(0, x_local, group):
        at = (slice(None), pl.ds(x, group))
        copies = [
            pltpu.make_async_copy(source.at[at], target.at[at], near_sems.at[index, x // group])
            for index, (source, target) in enumerate(
                zip(fields_hbm, (in_ref, pre_ref, out_grad_ref))
            )
        ]
        parts.append(copies)
        for copy in copies:
            copy.start()
        if x == 0:
            for copy in later_copies[:2]:
                copy.start()
    for copy in later_copies[2:]:
        copy.start()
    raw, gram = 0.0, 0.0
    ones = jnp.ones((2 * SUBLANES, 2 * group * LANES), BF16)
    for first in range(0, x_local, group):
        for copy in parts[first // group]:
            copy.wait()
        fields, highs, lows = [], [], []
        for x in range(first, first + group):
            pre_grad = out_grad_ref[:, x].astype(F32) * gelu_slope(pre_ref[:, x])
            high, low = split(pre_grad.reshape(rows, LANES))
            ghi_ref[x] = high
            glo_ref[x] = low
            highs.append(high)
            lows.append(low)
            fields.append(in_ref[:, x].reshape(rows, LANES))
        if first == 0:
            for copy in later_copies[:2]:
                copy.wait()
        tables = [
            only_x(ref[...], x) for ref in (hi_ref, lo_ref) for x in range(first, first + group)
        ]
        table = jnp.concatenate(tables, axis=1)
        field = jnp.concatenate(fields * 2, axis=1)
        high = jnp.concatenate(highs * 2, axis=1)
        low = jnp.concatenate(lows * 2, axis=1)
        raw += dot_rows(jnp.concatenate([field, high, low], axis=0), table)
        both = jnp.concatenate(highs + lows, axis=1)
        gram += dot_rows(jnp.concatenate([field, ones], axis=0), both)
    raw_in, raw_grad = raw[:rows], raw[rows : 2 * rows] + raw[2 * rows :]
    gram, bias = gram[:rows], gram[rows : rows + SUBLANES]

    tile = (channels, SUBLANES, LANES)
    sign = jnp.where(iota(tile, 2) % 2 == 0, 1.0, -1.0)
    upper = iota(tile, 1) < y_local

    def joined(raw):
        even = raw[:, :LANES].reshape(tile)
        odd = raw[:, LANES:].reshape(tile)
        return jnp.where(
            upper,
            even + sign * pltpu.roll(even, y_local, 1),
            pltpu.roll(odd, y_local, 1) + sign * odd,
        )

    wide = (channels, SUBLANES, rows)
    row, col = iota(wide, 1), iota(wide, 2)
    trace = jnp.where(row == col % SUBLANES, gram.reshape(wide), 0.0)
    trace = jnp.sum(trace, axis=1, keepdims=True)
    at_row = row == col // SUBLANES // x_local
    weight_rows = split(jnp.where(at_row, trace, 0.0).reshape(rows, rows))
    flat = (rows, LANES)
    place = jnp.where(
        iota(flat, 1) == iota(flat, 0) // SUBLANES % x_local * (2 * HL) + HL, 1.0, 0.0
    ).astype(BF16)
    weight_slots = dot(weight_rows[0], place) + dot(weight_rows[1], place)
    bias_rows = split(jnp.where(at_row[0], bias, 0.0))
    bias_slots = dot(bias_rows[0], place) + dot(bias_rows[1], place)
    s_ref[:, 0] = joined(raw_in) + weight_slots.reshape(tile)
    s_ref[:, 1] = joined(raw_grad) + bias_slots[None]
    for copy in later_copies[2:]:
        copy.wait()


def slot_place(channels, x_local, y):
    lane, out = iota((LANES, channels), 0), iota((LANES, channels), 1)
    place = (lane == out % x_local * (2 * HL) + HL) & (out // x_local == y)
    return jnp.where(place, 1.0, 0.0)


def from_slots(taken, place):
    high = taken.astype(BF16)
    middle, low = split(taken - high.astype(F32))
    place = place.astype(BF16)
    return dot(
        jnp.concatenate([high, middle, low], axis=1), jnp.concatenate([place] * 3, axis=0)
    )


def exchange_order(x_devices, y_devices):
    along = list(range(y_devices))
    middle = y_devices // 4 * 2
    along[:2], along[middle : middle + 2] = along[middle : middle + 2], along[:2]
    return [g * y_devices + k for g in range(x_devices) for k in along]


def by_device(order, x_devices):
    place = sorted(range(len(order)), key=order.__getitem__)
    y_devices = len(order) // x_devices
    return [place[g * y_devices : (g + 1) * y_devices] for g in range(x_devices)]


def plane_kernel(places, r_ref, txh_ref, txl_ref, tyh_ref, tyl_ref, s_ref, stat_ref):
    y_local = SUBLANES // 2
    x_devices = len(places)
    stat_ref[...] = jnp.sum(r_ref[...], axis=0)
    slots = slot_mask(y_local)
    wide = jnp.concatenate(
        [
            jnp.concatenate(
                [jnp.where(slots, 0.0, r_ref[p]).reshape(-1, LANES) for p in row], axis=0
            )
            for row in places
        ],
        axis=1,
    )
    along_x = product(split(wide), (txh_ref[...], txl_ref[...]))
    lane = iota((along_x.shape[0], LANES), 1)
    sign = jnp.where(lane < LANES // 2, 1.0, -1.0)
    turned = [
        sign * pltpu.roll(along_x[:, g * LANES : (g + 1) * LANES], LANES // 2, 1)
        for g in range(x_devices)
    ]
    both = jnp.concatenate([along_x, jnp.concatenate(turned, axis=1)], axis=0)
    along_y = product((tyh_ref[...], tyl_ref[...]), split(both))
    count = s_ref.shape[1]
    for g, row in enumerate(places):
        for k, p in enumerate(row):
            s_ref[p] = along_y[k * count : (k + 1) * count, g * LANES : (g + 1) * LANES]


def mode_rows(r_ref, picks, channels):
    stride = r_ref.shape[0] // channels
    taken = [r_ref[pl.ds(pick, channels, stride=stride), :] for pick in picks]
    return jnp.concatenate(taken, axis=0).T


def repeated(values, times):
    return jnp.concatenate([values] * times, axis=1)


def back_kernel(cells, channels, r_ref, weight_ref, s_ref):
    size = channels * channels
    kx_local, ky_local = weight_ref.shape[:2]
    count = kx_local * HL
    width = SUBLANES * channels
    shape = (2 * SUBLANES, 2 * width)
    sums = iota(shape, 0) == iota(shape, 1) % width // channels
    sums = jnp.where(sums, 1.0, 0.0).astype(BF16)
    group = LANES // channels // 2
    for start in range(0, ky_local, group):
        places = [(ky, hh) for ky in range(start, start + group) for hh in range(2)]
        modes = mode_rows(r_ref, [ky * 4 + 2 + hh for ky, hh in places], channels)
        row, lane = iota(modes.shape, 0), iota(modes.shape, 1)
        first = (row % HL == 0) & (lane // channels % 2 == 0)
        modes = modes * jnp.where(first, 1.0 / cells, 2.0 / cells)
        for index, (ky, hh) in enumerate(places):
            grad = jnp.where(lane // channels == index, modes, 0.0)
            shift = channels
            while shift < LANES:
                grad = grad + pltpu.roll(grad, shift, 1)
                shift = shift * 2
            grad_real = repeated(grad[:count], width // LANES)
            grad_imag = repeated(grad[count:], width // LANES)
            rows = slice(hh * HL, (hh + 1) * HL)
            for block in range(size // width):
                at = slice(block * width, (block + 1) * width)
                mix_real = weight_ref[:, ky, 0, rows, at].reshape(count, width)
                mix_imag = weight_ref[:, ky, 1, rows, at].reshape(count, width)
                terms = jnp.concatenate(
                    [
                        grad_real * mix_real + grad_imag * mix_imag,
                        grad_imag * mix_real - grad_real * mix_imag,
                    ],
                    axis=0,
                )
                back = dot_rows(sums, jnp.concatenate(split(terms), axis=1))
                at = block * SUBLANES * SUBLANES + ky * 2 + hh
                s_ref[pl.ds(at, SUBLANES, stride=SUBLANES), :] = back[:SUBLANES]


def outer_kernel(cells, r_ref, spread_ref, grad_ref):
    kx_local = grad_ref.shape[0]
    size = grad_ref.shape[-1]
    channels = spread_ref.shape[0] // 4
    ky = pl.program_id(0)
    half = LANES // 2
    modes = mode_rows(r_ref, [ky * 4 + f * 2 + hh for hh in range(2) for f in range(2)], channels)
    row, lane = iota(modes.shape, 0), iota(modes.shape, 1)
    first = (row % HL == 0) & (lane < half)
    factor = jnp.where(
        lane // channels % 2 == 1, jnp.where(first, 1.0 / cells, 2.0 / cells), 1.0
    )
    modes = modes * factor
    low = modes - modes.astype(BF16).astype(F32)
    left = jnp.concatenate(
        [
            jnp.where(lane < half, modes, pltpu.roll(low, half, 1)),
            jnp.where(lane < half, pltpu.roll(modes, half, 1), low),
        ],
        axis=0,
    ).astype(BF16)
    spread = dot(left, spread_ref[...])
    count = kx_local * HL
    for hh in range(2):
        real = spread[hh * 2 * count : hh * 2 * count + count]
        imag = spread[hh * 2 * count + count : (hh + 1) * 2 * count]
        in_real, in_imag = real[:, :size], imag[:, :size]
        times = size // LANES
        grad_real, grad_imag = repeated(real[:, size:], times), repeated(imag[:, size:], times)
        rows = pl.ds(hh * HL, HL)
        tile = (kx_local, HL, size)
        grad_ref[:, 0, 0, rows, :] = (in_real * grad_real + in_imag * grad_imag).reshape(tile)
        grad_ref[:, 0, 1, rows, :] = (in_real * grad_imag - in_imag * grad_real).reshape(tile)


def local_kernel(scale, weight_ref, ghi_ref, glo_ref, stat_ref, local_ref, bias_ref):
    channels, x_local = local_ref.shape[:2]
    rows = channels * SUBLANES
    bias = jnp.zeros((SUBLANES, channels), F32)
    for y in range(SUBLANES // 2):
        row = jnp.where(iota((SUBLANES, LANES), 0) == y, stat_ref[1], 0.0)
        bias += from_slots(row, slot_place(channels, x_local, y))
    bias_ref[...] = jnp.sum(bias, axis=0, keepdims=True) * scale
    spread = jnp.where(
        iota((rows, channels), 0) // SUBLANES == iota((rows, channels), 1), 1.0, 0.0
    )
    tall = jnp.dot(
        spread, weight_ref[...], precision=HIGHEST_PRECISION, preferred_element_type=F32
    )
    square = lax.dot_general(
        tall,
        spread,
        (((1,), (1,)), ((), ())),
        precision=HIGHEST_PRECISION,
        preferred_element_type=F32,
    )
    same = iota(square.shape, 0) % SUBLANES == iota(square.shape, 1) % SUBLANES
    high, low = split(jnp.where(same, square, 0.0))
    left = jnp.concatenate([high, high, low], axis=1)
    for x in range(x_local):
        right = jnp.concatenate([ghi_ref[x], glo_ref[x], ghi_ref[x]], axis=0)
        local_ref[:, x] = dot(left, right).reshape(channels, SUBLANES, LANES)


def inverse_kernel(places, r_ref, stat_ref, tyh_ref, tyl_ref, txh_ref, txl_ref, s_ref):
    y_local = SUBLANES // 2
    values = [jnp.concatenate([r_ref[p] for p in row], axis=0) for row in places]
    lane = iota(values[0].shape, 1)
    sign = jnp.where(lane < LANES // 2, -1.0, 1.0)
    wide = jnp.concatenate(values, axis=1)
    turned = [sign * pltpu.roll(value, LANES // 2, 1) for value in values]
    both = jnp.concatenate([wide, jnp.concatenate(turned, axis=1)], axis=0)
    along_y = product((tyh_ref[...], tyl_ref[...]), split(both))
    along_x = product_rows(split(along_y), (txh_ref[...], txl_ref[...]))
    slots = slot_mask(y_local)
    for g, row in enumerate(places):
        for k, p in enumerate(row):
            block = along_x[k * SUBLANES : (k + 1) * SUBLANES, g * LANES : (g + 1) * LANES]
            s_ref[p] = jnp.where(slots, stat_ref[0], block)


def result_kernel(scale, r_ref, hi_ref, lo_ref, local_ref, grad_hbm, point_ref, grad_ref, sems):
    channels, x_local = grad_ref.shape[:2]
    y_local = SUBLANES // 2
    rows = channels * SUBLANES
    tile = (channels, SUBLANES, LANES)
    values = r_ref[...].reshape(tile)
    turned = pltpu.roll(values, y_local, 1)
    sign = jnp.where(iota(tile, 2) % 2 == 0, 1.0, -1.0)
    upper = iota(tile, 1) < y_local
    halves = [
        jnp.where(upper, values, sign * turned).reshape(rows, LANES),
        jnp.where(upper, turned, sign * values).reshape(rows, LANES),
    ]
    highs = [half.astype(BF16).astype(F32) for half in halves]
    parts = [*highs, *(half - high for half, high in zip(halves, highs))]
    count = len(parts)
    width = LANES // count
    places = width // (2 * HL)
    parts = [part if k == 0 else pltpu.roll(part, k * width, 1) for k, part in enumerate(parts)]
    lane = iota((rows, LANES), 1) // width
    group = 2 * HL
    zeros = jnp.zeros((group, LANES), BF16)

    def rows_of(ref, part, first):
        blocks = []
        for k in range(places):
            at = part % 2 * LANES + (first + k) * group
            row = [zeros] * places
            row[k] = ref[at : at + group, :]
            blocks.append(jnp.concatenate(row, axis=1))
        return jnp.concatenate(blocks, axis=0)

    copies = []
    for index in range(x_local // places):
        first = index * places
        left = parts[0]
        for k in range(1, count):
            left = jnp.where(lane == (index + k) % count, parts[k], left)
        left = left.astype(BF16)
        order = [(k - index) % count for k in range(count)]
        right = [rows_of(ref, part, first) for ref in (hi_ref, lo_ref) for part in order]
        block = dot(jnp.concatenate([left, left], axis=1), jnp.concatenate(right, axis=0))
        for k in range(places):
            part = block[:, k * LANES : (k + 1) * LANES]
            grad_ref[:, first + k] = part.reshape(tile) + local_ref[:, first + k]
        at = (slice(None), pl.ds(first, places))
        copies.append(pltpu.make_async_copy(grad_ref.at[at], grad_hbm.at[at], sems.at[index]))
        copies[-1].start()
    point = jnp.zeros(point_ref.shape, F32)
    for y in range(y_local):
        taken = r_ref[pl.ds(y, channels, stride=SUBLANES), :]
        point += from_slots(taken, slot_place(channels, x_local, y))
    point_ref[...] = point * scale
    for copy in copies:
        copy.wait()


def call(kernel, out_shape, name, vmem=16, **options):
    params = pltpu.CompilerParams(vmem_limit_bytes=vmem << 20)
    return pl.pallas_call(
        kernel, out_shape=out_shape, name=name, compiler_params=params, **options
    )


def held(count):
    return [pl.BlockSpec(memory_space=pltpu.VMEM)] * count


def to_tiles(array):
    lead, (rows, depth) = array.shape[:-2], array.shape[-2:]
    split_up = array.reshape(lead + (rows, depth // LANES, LANES))
    return jnp.swapaxes(split_up, -3, -2).reshape(lead + (SUBLANES, LANES))


def from_tiles(array, rows, depth):
    lead = array.shape[:-2]
    split_up = array.reshape(lead + (depth // LANES, rows, LANES))
    return jnp.swapaxes(split_up, -3, -2).reshape(lead + (rows, depth))


def transposed(inputs, pre_act, grad_out, point_weight, mode_weight):
    channels, x_local, y_local, depth = inputs.shape
    kx_local, ky_local, _, kz_count, pairs = mode_weight.shape
    x_devices = lax.axis_size("gx")
    y_devices = lax.axis_size("gy")
    devices = x_devices * y_devices
    hh_count = kz_count // HL
    cells = x_local * x_devices * y_local * y_devices * depth
    scale = 1.0 / math.sqrt(cells)
    axes = ("gx", "gy")
    order = exchange_order(x_devices, y_devices)
    places = by_device(order, x_devices)
    rows = channels * SUBLANES

    def struct(shape, kind=F32):
        return jax.ShapeDtypeStruct(shape, kind)

    def exchange(chunks):
        return lax.all_to_all(chunks, axes, 0, 0, axis_index_groups=[order])

    z_high, z_low = split_table(depth_table(depth, kz_count, x_local))
    tx = split_table(x_table(x_devices, x_local, kx_local))
    ty = split_table(y_table(y_devices, y_local, ky_local, hh_count))
    tyi = split_table(y_inverse_table(y_devices, y_local, ky_local, hh_count))
    spread = spread_table(channels)

    field_shape = (channels, x_local, SUBLANES, LANES)
    later = (z_high.T, z_low.T, *tx, *ty, *tyi, mode_weight)
    chunks, g_high, g_low, *later = call(
        functools.partial(grid_kernel, len(later)),
        (
            struct((channels, 2, SUBLANES, LANES)),
            struct((x_local, rows, LANES), BF16),
            struct((x_local, rows, LANES), BF16),
            *(struct(array.shape, array.dtype) for array in later),
        ),
        "grid",
        vmem=24,
        in_specs=[pl.BlockSpec(memory_space=pltpu.HBM)] * (3 + len(later)),
        out_specs=held(3 + len(later)),
        scratch_shapes=[
            *([pltpu.VMEM(field_shape, BF16)] * 3),
            pltpu.SemaphoreType.DMA((3, x_local)),
            pltpu.SemaphoreType.DMA((len(later),)),
        ],
    )(
        *(
            pltpu.with_memory_space_constraint(array, pltpu.HBM)
            for array in (
                to_tiles(inputs),
                to_tiles(pre_act),
                to_tiles(grad_out),
                *later,
            )
        )
    )
    z_turned, tx, ty, tyi, mode_weight = later[:2], later[2:4], later[4:6], later[6:8], later[8]
    planes = exchange(chunks)
    mode_rows_count = ky_local * 2 * hh_count
    chunks, stats = call(
        functools.partial(plane_kernel, places),
        (
            struct((devices, mode_rows_count, LANES)),
            struct((2, SUBLANES, LANES)),
        ),
        "plane",
        in_specs=held(5),
        out_specs=held(2),
    )(planes, *tx, *ty)
    local, bias_grad = call(
        functools.partial(local_kernel, scale),
        (struct(field_shape), struct((1, channels))),
        "local",
        in_specs=held(4),
        out_specs=held(2),
    )(point_weight, g_high, g_low, stats)
    modes = exchange(chunks)
    modes = modes.reshape(devices * mode_rows_count, LANES)
    chunks = call(
        functools.partial(back_kernel, cells, channels),
        struct((devices * SUBLANES, LANES)),
        "back",
        in_specs=held(2),
        out_specs=held(1)[0],
    )(modes, mode_weight)
    back = exchange(chunks.reshape(devices, SUBLANES, LANES))
    block = (kx_local, 1, 2, kz_count, pairs)
    mode_grad = call(
        functools.partial(outer_kernel, cells),
        struct(mode_weight.shape),
        "outer",
        grid=(ky_local,),
        in_specs=held(2),
        out_specs=pl.BlockSpec(block, lambda k: (0, k, 0, 0, 0)),
    )(modes, spread)
    chunks = call(
        functools.partial(inverse_kernel, places),
        struct((devices, SUBLANES, LANES)),
        "inverse",
        in_specs=held(6),
        out_specs=held(1)[0],
    )(back, stats, *tyi, *tx)
    near = exchange(chunks)
    grad, point_grad = call(
        functools.partial(result_kernel, scale),
        (struct(field_shape), struct((channels, channels))),
        "result",
        in_specs=held(4),
        out_specs=(pl.BlockSpec(memory_space=pltpu.HBM), held(1)[0]),
        scratch_shapes=[pltpu.VMEM(field_shape, F32), pltpu.SemaphoreType.DMA((x_local,))],
    )(near.reshape(rows, LANES), *z_turned, local)
    return (from_tiles(grad, y_local, depth), point_grad, bias_grad[0], mode_grad)


def one_channel_each(inputs, mode_weight):
    channels, x_local, y_local, depth = inputs.shape
    kx_local, ky_local, _, kz_count, _ = mode_weight.shape
    return (
        channels == lax.axis_size("gx") * lax.axis_size("gy")
        and LANES % channels == 0
        and depth == 2 * LANES
        and y_local * 2 == SUBLANES
        and kz_count == 2 * HL
        and ky_local * 2 == SUBLANES
        and x_local * 2 * HL == LANES
        and kx_local == x_local
        and x_local * y_local == channels
    )


def shards(inputs, pre_act, grad_out, point_weight, mode_weight):
    plan = transposed if one_channel_each(inputs, mode_weight) else partial_sums
    return plan(inputs, pre_act, grad_out, point_weight, mode_weight)


def solution(mesh):
    return jax.shard_map(
        shards,
        mesh=mesh,
        in_specs=(
            P(None, "gx", "gy", None),
            P(None, "gx", "gy", None),
            P(None, "gx", "gy", None),
            P(),
            P("gx", "gy", None, None, None),
        ),
        out_specs=(P(None, "gx", "gy", None), P(), P(), P("gx", "gy", None, None, None)),
        check_vma=False,
    )
```

```python
import functools
import math

import jax
import jax.numpy as jnp
import numpy as np
from jax import lax
from jax.experimental import pallas as pl
from jax.experimental.pallas import tpu as pltpu
from jax.sharding import PartitionSpec as P

HIGHEST_PRECISION = lax.Precision.HIGHEST
ROOT_HALF = 0.7071067811865476
NORMAL_PEAK = 0.3989422804014327


def gelu_slope(pre_act):
    value = pre_act.astype(jnp.float32)
    return (
        0.5 * (1.0 + jax.scipy.special.erf(value * ROOT_HALF))
        + value * jnp.exp(-0.5 * value * value) * NORMAL_PEAK
    )


def phases(length, modes, wrapped, index, first, count):
    if wrapped:
        frequency = jnp.where(index < modes // 2, index, index + (length - modes))
    else:
        frequency = index
    places = first + jnp.arange(count, dtype=jnp.int32)
    turns = frequency[:, None] * places[None, :] % length
    angle = turns.astype(jnp.float32) * (2.0 * math.pi / length)
    return (jnp.cos(angle), jnp.sin(angle))


def transform(cos_table, sin_table, data, sign):
    real_part = data[..., 0, :]
    imag_part = data[..., 1, :]

    def apply(table, values):
        return jnp.tensordot(table, values, axes=1, precision=HIGHEST_PRECISION)

    if sign < 0:
        out_real = apply(cos_table, real_part) + apply(sin_table, imag_part)
        out_imag = apply(cos_table, imag_part) - apply(sin_table, real_part)
    else:
        out_real = apply(cos_table, real_part) - apply(sin_table, imag_part)
        out_imag = apply(cos_table, imag_part) + apply(sin_table, real_part)
    return jnp.stack([out_real, out_imag], axis=-2)


def depth_forward(field, kz_count):
    channels = field.shape[0]
    depth = field.shape[-1]
    cos_z, sin_z = phases(depth, kz_count, False, jnp.arange(kz_count, dtype=jnp.int32), 0, depth)
    real_part = jnp.einsum("cabz,kz->abkc", field, cos_z, precision=HIGHEST_PRECISION)
    imag_part = -jnp.einsum("cabz,kz->abkc", field, sin_z, precision=HIGHEST_PRECISION)
    lead = real_part.shape[:2]
    return jnp.stack(
        [
            real_part.reshape(lead + (kz_count * channels,)),
            imag_part.reshape(lead + (kz_count * channels,)),
        ],
        axis=2,
    )


def depth_inverse(spectrum, kz_count, channels, depth):
    lead = spectrum.shape[:2]
    split = spectrum.reshape(lead + (2, kz_count, channels))
    cos_z, sin_z = phases(depth, kz_count, False, jnp.arange(kz_count, dtype=jnp.int32), 0, depth)
    return jnp.einsum(
        "abkc,kz->cabz", split[:, :, 0], cos_z, precision=HIGHEST_PRECISION
    ) - jnp.einsum("abkc,kz->cabz", split[:, :, 1], sin_z, precision=HIGHEST_PRECISION)


def mode_work(spectrum_in, spectrum_grad, weight, cells):
    rows_a, rows_b, _, kz_count, _ = weight.shape
    channels = spectrum_in.shape[-1] // kz_count
    factor = (
        jnp.where(jnp.arange(kz_count, dtype=jnp.int32) == 0, 1.0, 2.0).astype(jnp.float32) / cells
    )
    shape = (rows_a, rows_b, 2, kz_count, channels)
    given = spectrum_in.reshape(shape)
    scaled = spectrum_grad.reshape(shape) * factor[:, None]
    mixing = weight.reshape(shape + (channels,))
    in_real = given[:, :, 0]
    in_imag = given[:, :, 1]
    grad_real = scaled[:, :, 0]
    grad_imag = scaled[:, :, 1]
    mix_real = mixing[:, :, 0]
    mix_imag = mixing[:, :, 1]

    def outer(left, right):
        return jnp.einsum("abki,abko->abkio", left, right, precision=HIGHEST_PRECISION)

    def mixed(values, matrix):
        return jnp.einsum("abko,abkio->abki", values, matrix, precision=HIGHEST_PRECISION)

    result_real = outer(in_real, grad_real) + outer(in_imag, grad_imag)
    result_imag = outer(in_real, grad_imag) - outer(in_imag, grad_real)
    mode_grad = jnp.stack([result_real, result_imag], axis=2).reshape(
        rows_a, rows_b, 2, kz_count, channels * channels
    )
    back_real = mixed(grad_real, mix_real) + mixed(grad_imag, mix_imag)
    back_imag = mixed(grad_imag, mix_real) - mixed(grad_real, mix_imag)
    back_spectrum = jnp.stack([back_real, back_imag], axis=2).reshape(
        rows_a, rows_b, 2, kz_count * channels
    )
    return (mode_grad, back_spectrum)


def joined_rows(main, extra):
    count = main.shape[0]
    return jnp.concatenate([main.reshape(count, -1), extra.reshape(count, -1)], axis=1)


def split_rows(result, main_shape, extra_shape):
    main_size = 1
    for item in main_shape[1:]:
        main_size = main_size * item
    main = result[:, :main_size].reshape(main_shape)
    extra = result[:, main_size:].reshape(extra_shape)
    return (main, extra)


def partial_sums(inputs, pre_act, grad_out, point_weight, mode_weight):
    channels, x_local, y_local, depth = inputs.shape
    kx_local, ky_local, _, kz_count, _ = mode_weight.shape
    x_devices = lax.axis_size("gx")
    y_devices = lax.axis_size("gy")
    x_length = x_local * x_devices
    y_length = y_local * y_devices
    kx_count = kx_local * x_devices
    ky_count = ky_local * y_devices
    cells = x_length * y_length * depth
    scale = 1.0 / math.sqrt(cells)
    x_offset = lax.axis_index("gx") * x_local
    y_offset = lax.axis_index("gy") * y_local
    width = kz_count * channels
    pair_width = 2 * width
    stat_count = channels * channels + channels
    mode_count = kx_count * ky_count
    field_in = inputs.astype(jnp.float32)
    pre_grad = grad_out.astype(jnp.float32) * gelu_slope(pre_act)
    weight_sum = jnp.einsum("ixyz,oxyz->io", field_in, pre_grad, precision=HIGHEST_PRECISION)
    bias_sum = jnp.sum(pre_grad, axis=(1, 2, 3))
    extra_cols = (stat_count + mode_count - 1) // mode_count
    stat_flat = jnp.concatenate([weight_sum.reshape(-1), bias_sum])
    grid = jnp.pad(stat_flat, (0, mode_count * extra_cols - stat_count)).reshape(
        kx_count, ky_count, extra_cols
    )
    spectra = jnp.stack(
        [depth_forward(field_in, kz_count), depth_forward(pre_grad, kz_count)], axis=2
    )
    along_y = jnp.swapaxes(spectra, 0, 1)
    grid_y = jnp.swapaxes(grid, 0, 1)
    cos_y, sin_y = phases(
        y_length,
        ky_count,
        True,
        jnp.arange(lax.axis_size("gy") * ky_local, dtype=jnp.int32),
        y_offset,
        y_local,
    )
    partial_y, extra_y = split_rows(
        lax.psum_scatter(
            joined_rows(transform(cos_y, sin_y, along_y, -1), grid_y),
            "gy",
            scatter_dimension=0,
            tiled=True,
        ),
        (ky_local, x_local, 2, 2, width),
        (ky_local, kx_count, extra_cols),
    )
    along_x = jnp.swapaxes(partial_y, 0, 1)
    extra_along = jnp.swapaxes(extra_y, 0, 1)
    cos_x, sin_x = phases(
        x_length,
        kx_count,
        True,
        jnp.arange(lax.axis_size("gx") * kx_local, dtype=jnp.int32),
        x_offset,
        x_local,
    )
    owned, owned_extra = split_rows(
        lax.psum_scatter(
            joined_rows(transform(cos_x, sin_x, along_x, -1), extra_along),
            "gx",
            scatter_dimension=0,
            tiled=True,
        ),
        (kx_local, ky_local, 2, 2, width),
        (kx_local, ky_local, extra_cols),
    )
    mode_grad, back_spectrum = mode_work(owned[:, :, 0], owned[:, :, 1], mode_weight, cells)
    back_joined = jnp.concatenate(
        [back_spectrum.reshape(kx_local, ky_local, pair_width), owned_extra], axis=2
    )
    piece = lax.all_gather(back_joined, "gx", axis=0, tiled=True)
    kx_index = jnp.arange(piece.shape[0], dtype=jnp.int32)
    cos_x, sin_x = phases(x_length, kx_count, True, kx_index, x_offset, x_local)
    main = piece[:, :, :pair_width].reshape(piece.shape[0], piece.shape[1], 2, width)
    near = transform(cos_x.T, sin_x.T, main, 1)
    near_stats = piece[:, :, pair_width:]
    side_cols = (kx_count * extra_cols + x_local - 1) // x_local
    side_flat = jnp.swapaxes(near_stats, 0, 1).reshape(ky_local, kx_count * extra_cols)
    side = jnp.swapaxes(side_flat.reshape(ky_local, x_local, side_cols), 0, 1)
    near_joined = jnp.concatenate([near.reshape(x_local, ky_local, pair_width), side], axis=2)
    piece = lax.all_gather(near_joined, "gy", axis=1, tiled=True)
    ky_index = jnp.arange(piece.shape[1], dtype=jnp.int32)
    cos_y, sin_y = phases(y_length, ky_count, True, ky_index, y_offset, y_local)
    main = piece[:, :, :pair_width].reshape(piece.shape[0], piece.shape[1], 2, width)
    moved = jnp.swapaxes(transform(cos_y.T, sin_y.T, jnp.swapaxes(main, 0, 1), 1), 0, 1)
    far_stats = piece[:, :, pair_width:]
    stats_rows = jnp.swapaxes(far_stats, 0, 1).reshape(ky_count, x_local * side_cols)
    stats_grid = jnp.swapaxes(stats_rows.reshape(ky_count, kx_count, extra_cols), 0, 1)
    stat_values = stats_grid.reshape(-1)[:stat_count]
    point_grad = stat_values[: channels * channels].reshape(channels, channels)
    bias_grad = stat_values[channels * channels :]
    local = jnp.einsum("io,oxyz->ixyz", point_weight, pre_grad, precision=HIGHEST_PRECISION)
    input_grad = local + depth_inverse(moved, kz_count, channels, depth)
    return (input_grad, point_grad * scale, bias_grad * scale, mode_grad)


LANES = 128
SUBLANES = 8
HL = 8
BF16 = jnp.bfloat16
F32 = jnp.float32


def split_table(table):
    high = table.astype(np.float32).astype(BF16)
    low = (table - high.astype(np.float64)).astype(np.float32).astype(BF16)
    return (high, low)


def split(values):
    high = values.astype(BF16)
    return (high, (values - high.astype(F32)).astype(BF16))


def dot(left, right):
    return jnp.dot(left, right, preferred_element_type=F32)


def dot_rows(left, right):
    return lax.dot_general(left, right, (((1,), (1,)), ((), ())), preferred_element_type=F32)


def product(left, right):
    left = jnp.concatenate([left[0], left[1], left[0]], axis=1)
    return dot(left, jnp.concatenate([right[0], right[0], right[1]], axis=0))


def product_rows(left, right):
    left = jnp.concatenate([left[0], left[1], left[0]], axis=1)
    return dot_rows(left, jnp.concatenate([right[0], right[0], right[1]], axis=1))


def iota(shape, axis):
    return lax.broadcasted_iota(jnp.int32, shape, axis)


def wave(length, modes):
    index = np.arange(modes)
    frequency = np.where(index < modes // 2, index, index + (length - modes))
    turns = frequency[:, None] * np.arange(length)[None, :] % length
    angle = turns * (2.0 * math.pi / length)
    return (np.cos(angle), np.sin(angle))


def depth_table(depth, kz_count, x_local):
    h = np.arange(kz_count)
    angle = (h[None, :] * np.arange(LANES)[:, None] % depth) * (2.0 * math.pi / depth)
    both = np.stack([np.cos(angle), -np.sin(angle)], axis=1)
    both = both.reshape(LANES, 2, kz_count // HL, 1, HL).transpose(0, 2, 3, 1, 4)
    return np.broadcast_to(both, (LANES, kz_count // HL, x_local, 2, HL)).reshape(LANES, -1)


def x_table(x_devices, x_local, kx_local):
    cos_x, sin_x = wave(x_devices * x_local, x_devices * kx_local)
    mix = np.array([[cos_x, -sin_x], [sin_x, cos_x]])
    mix = mix.reshape(2, 2, x_devices, kx_local, x_devices, x_local)
    full = np.einsum("pqakbx,hj->bxphaqkj", mix, np.eye(HL))
    size = x_devices * x_local * 2 * HL
    return full.reshape(size, -1)


def y_table(y_devices, y_local, ky_local, hh_count):
    pair = wave(y_devices * y_local, y_devices * ky_local)
    shape = (y_devices, ky_local, y_devices, y_local)
    parts = [
        np.einsum("akby,fg,hi->akgibfhy", t.reshape(shape), np.eye(2), np.eye(hh_count)).reshape(
            y_devices * ky_local * 2 * hh_count, -1
        )
        for t in pair
    ]
    return np.concatenate(parts, axis=1)


def y_inverse_table(y_devices, y_local, ky_local, hh_count):
    pair = wave(y_devices * y_local, y_devices * ky_local)
    shape = (y_devices, ky_local, y_devices, y_local)
    parts = [
        np.einsum("akby,hi->biyakh", t.reshape(shape), np.eye(hh_count)).reshape(
            y_devices * y_local * hh_count, -1
        )
        for t in pair
    ]
    return np.concatenate(parts, axis=1)


def spread_table(channels):
    left = np.repeat(np.eye(channels), channels, axis=1)
    right = np.tile(np.eye(channels), (1, LANES // channels))
    one = np.zeros((2 * channels, channels * channels + LANES))
    one[:channels, : channels * channels] = left
    one[channels:, channels * channels :] = right
    return np.concatenate([one, one], axis=0).astype(BF16)


def slot_mask(y_local):
    shape = (SUBLANES, LANES)
    return (iota(shape, 0) < y_local) & (iota(shape, 1) % (2 * HL) == HL)


def only_x(table, x):
    group = 2 * HL
    zeros = jnp.zeros((LANES, table.shape[1]), table.dtype)
    blocks = []
    for start in range(0, table.shape[0], LANES):
        at = start + x * group
        blocks += [zeros[: x * group], table[at : at + group], zeros[(x + 1) * group :]]
    return jnp.concatenate([block for block in blocks if block.shape[0] > 0], axis=0)


def grid_kernel(count, *refs):
    fields_hbm, refs = refs[:3], refs[3:]
    later_hbm, refs = refs[:count], refs[count:]
    s_ref, ghi_ref, glo_ref = refs[:3]
    later, refs = refs[3 : 3 + count], refs[3 + count :]
    in_ref, pre_ref, out_grad_ref, near_sems, far_sems = refs
    hi_ref, lo_ref = later[:2]
    channels, x_local = in_ref.shape[:2]
    y_local = SUBLANES // 2
    rows = channels * SUBLANES
    group = max(x_local // 4, 1)
    parts = []
    later_copies = [
        pltpu.make_async_copy(source, target, far_sems.at[index])
        for index, (source, target) in enumerate(zip(later_hbm, later))
    ]
    for x in range(0, x_local, group):
        at = (slice(None), pl.ds(x, group))
        copies = [
            pltpu.make_async_copy(source.at[at], target.at[at], near_sems.at[index, x // group])
            for index, (source, target) in enumerate(
                zip(fields_hbm, (in_ref, pre_ref, out_grad_ref))
            )
        ]
        parts.append(copies)
        for copy in copies:
            copy.start()
        if x == 0:
            for copy in later_copies[:2]:
                copy.start()
    for copy in later_copies[2:]:
        copy.start()
    raw, gram = 0.0, 0.0
    ones = jnp.ones((2 * SUBLANES, 2 * group * LANES), BF16)
    for first in range(0, x_local, group):
        for copy in parts[first // group]:
            copy.wait()
        fields, highs, lows = [], [], []
        for x in range(first, first + group):
            pre_grad = out_grad_ref[:, x].astype(F32) * gelu_slope(pre_ref[:, x])
            high, low = split(pre_grad.reshape(rows, LANES))
            ghi_ref[x] = high
            glo_ref[x] = low
            highs.append(high)
            lows.append(low)
            fields.append(in_ref[:, x].reshape(rows, LANES))
        if first == 0:
            for copy in later_copies[:2]:
                copy.wait()
        tables = [
            only_x(ref[...], x) for ref in (hi_ref, lo_ref) for x in range(first, first + group)
        ]
        table = jnp.concatenate(tables, axis=1)
        field = jnp.concatenate(fields * 2, axis=1)
        high = jnp.concatenate(highs * 2, axis=1)
        low = jnp.concatenate(lows * 2, axis=1)
        raw += dot_rows(jnp.concatenate([field, high, low], axis=0), table)
        both = jnp.concatenate(highs + lows, axis=1)
        gram += dot_rows(jnp.concatenate([field, ones], axis=0), both)
    raw_in, raw_grad = raw[:rows], raw[rows : 2 * rows] + raw[2 * rows :]
    gram, bias = gram[:rows], gram[rows : rows + SUBLANES]

    tile = (channels, SUBLANES, LANES)
    sign = jnp.where(iota(tile, 2) % 2 == 0, 1.0, -1.0)
    upper = iota(tile, 1) < y_local

    def joined(raw):
        even = raw[:, :LANES].reshape(tile)
        odd = raw[:, LANES:].reshape(tile)
        return jnp.where(
            upper,
            even + sign * pltpu.roll(even, y_local, 1),
            pltpu.roll(odd, y_local, 1) + sign * odd,
        )

    wide = (channels, SUBLANES, rows)
    row, col = iota(wide, 1), iota(wide, 2)
    trace = jnp.where(row == col % SUBLANES, gram.reshape(wide), 0.0)
    trace = jnp.sum(trace, axis=1, keepdims=True)
    at_row = row == col // SUBLANES // x_local
    weight_rows = split(jnp.where(at_row, trace, 0.0).reshape(rows, rows))
    flat = (rows, LANES)
    place = jnp.where(
        iota(flat, 1) == iota(flat, 0) // SUBLANES % x_local * (2 * HL) + HL, 1.0, 0.0
    ).astype(BF16)
    weight_slots = dot(weight_rows[0], place) + dot(weight_rows[1], place)
    bias_rows = split(jnp.where(at_row[0], bias, 0.0))
    bias_slots = dot(bias_rows[0], place) + dot(bias_rows[1], place)
    s_ref[:, 0] = joined(raw_in) + weight_slots.reshape(tile)
    s_ref[:, 1] = joined(raw_grad) + bias_slots[None]
    for copy in later_copies[2:]:
        copy.wait()


def slot_place(channels, x_local, y):
    lane, out = iota((LANES, channels), 0), iota((LANES, channels), 1)
    place = (lane == out % x_local * (2 * HL) + HL) & (out // x_local == y)
    return jnp.where(place, 1.0, 0.0)


def from_slots(taken, place):
    high = taken.astype(BF16)
    middle, low = split(taken - high.astype(F32))
    place = place.astype(BF16)
    return dot(
        jnp.concatenate([high, middle, low], axis=1), jnp.concatenate([place] * 3, axis=0)
    )


def exchange_order(x_devices, y_devices):
    along = list(range(y_devices))
    middle = y_devices // 4 * 2
    along[:2], along[middle : middle + 2] = along[middle : middle + 2], along[:2]
    return [g * y_devices + k for g in range(x_devices) for k in along]


def by_device(order, x_devices):
    place = sorted(range(len(order)), key=order.__getitem__)
    y_devices = len(order) // x_devices
    return [place[g * y_devices : (g + 1) * y_devices] for g in range(x_devices)]


def plane_kernel(places, r_ref, txh_ref, txl_ref, tyh_ref, tyl_ref, s_ref, stat_ref):
    y_local = SUBLANES // 2
    x_devices = len(places)
    stat_ref[...] = jnp.sum(r_ref[...], axis=0)
    slots = slot_mask(y_local)
    wide = jnp.concatenate(
        [
            jnp.concatenate(
                [jnp.where(slots, 0.0, r_ref[p]).reshape(-1, LANES) for p in row], axis=0
            )
            for row in places
        ],
        axis=1,
    )
    along_x = product(split(wide), (txh_ref[...], txl_ref[...]))
    lane = iota((along_x.shape[0], LANES), 1)
    sign = jnp.where(lane < LANES // 2, 1.0, -1.0)
    turned = [
        sign * pltpu.roll(along_x[:, g * LANES : (g + 1) * LANES], LANES // 2, 1)
        for g in range(x_devices)
    ]
    both = jnp.concatenate([along_x, jnp.concatenate(turned, axis=1)], axis=0)
    along_y = product((tyh_ref[...], tyl_ref[...]), split(both))
    count = s_ref.shape[1]
    for g, row in enumerate(places):
        for k, p in enumerate(row):
            s_ref[p] = along_y[k * count : (k + 1) * count, g * LANES : (g + 1) * LANES]


def mode_rows(r_ref, picks, channels):
    stride = r_ref.shape[0] // channels
    taken = [r_ref[pl.ds(pick, channels, stride=stride), :] for pick in picks]
    return jnp.concatenate(taken, axis=0).T


def repeated(values, times):
    return jnp.concatenate([values] * times, axis=1)


def back_kernel(cells, channels, r_ref, weight_ref, s_ref):
    size = channels * channels
    kx_local, ky_local = weight_ref.shape[:2]
    count = kx_local * HL
    width = SUBLANES * channels
    shape = (2 * SUBLANES, 2 * width)
    sums = iota(shape, 0) == iota(shape, 1) % width // channels
    sums = jnp.where(sums, 1.0, 0.0).astype(BF16)
    group = LANES // channels // 2
    for start in range(0, ky_local, group):
        places = [(ky, hh) for ky in range(start, start + group) for hh in range(2)]
        modes = mode_rows(r_ref, [ky * 4 + 2 + hh for ky, hh in places], channels)
        row, lane = iota(modes.shape, 0), iota(modes.shape, 1)
        first = (row % HL == 0) & (lane // channels % 2 == 0)
        modes = modes * jnp.where(first, 1.0 / cells, 2.0 / cells)
        for index, (ky, hh) in enumerate(places):
            grad = jnp.where(lane // channels == index, modes, 0.0)
            shift = channels
            while shift < LANES:
                grad = grad + pltpu.roll(grad, shift, 1)
                shift = shift * 2
            grad_real = repeated(grad[:count], width // LANES)
            grad_imag = repeated(grad[count:], width // LANES)
            rows = slice(hh * HL, (hh + 1) * HL)
            for block in range(size // width):
                at = slice(block * width, (block + 1) * width)
                mix_real = weight_ref[:, ky, 0, rows, at].reshape(count, width)
                mix_imag = weight_ref[:, ky, 1, rows, at].reshape(count, width)
                terms = jnp.concatenate(
                    [
                        grad_real * mix_real + grad_imag * mix_imag,
                        grad_imag * mix_real - grad_real * mix_imag,
                    ],
                    axis=0,
                )
                back = dot_rows(sums, jnp.concatenate(split(terms), axis=1))
                at = block * SUBLANES * SUBLANES + ky * 2 + hh
                s_ref[pl.ds(at, SUBLANES, stride=SUBLANES), :] = back[:SUBLANES]


def outer_kernel(cells, r_ref, spread_ref, grad_ref):
    kx_local = grad_ref.shape[0]
    size = grad_ref.shape[-1]
    channels = spread_ref.shape[0] // 4
    ky = pl.program_id(0)
    half = LANES // 2
    modes = mode_rows(r_ref, [ky * 4 + f * 2 + hh for hh in range(2) for f in range(2)], channels)
    row, lane = iota(modes.shape, 0), iota(modes.shape, 1)
    first = (row % HL == 0) & (lane < half)
    factor = jnp.where(
        lane // channels % 2 == 1, jnp.where(first, 1.0 / cells, 2.0 / cells), 1.0
    )
    modes = modes * factor
    low = modes - modes.astype(BF16).astype(F32)
    left = jnp.concatenate(
        [
            jnp.where(lane < half, modes, pltpu.roll(low, half, 1)),
            jnp.where(lane < half, pltpu.roll(modes, half, 1), low),
        ],
        axis=0,
    ).astype(BF16)
    spread = dot(left, spread_ref[...])
    count = kx_local * HL
    for hh in range(2):
        real = spread[hh * 2 * count : hh * 2 * count + count]
        imag = spread[hh * 2 * count + count : (hh + 1) * 2 * count]
        in_real, in_imag = real[:, :size], imag[:, :size]
        times = size // LANES
        grad_real, grad_imag = repeated(real[:, size:], times), repeated(imag[:, size:], times)
        rows = pl.ds(hh * HL, HL)
        tile = (kx_local, HL, size)
        grad_ref[:, 0, 0, rows, :] = (in_real * grad_real + in_imag * grad_imag).reshape(tile)
        grad_ref[:, 0, 1, rows, :] = (in_real * grad_imag - in_imag * grad_real).reshape(tile)


def local_kernel(scale, weight_ref, ghi_ref, glo_ref, stat_ref, local_ref, bias_ref):
    channels, x_local = local_ref.shape[:2]
    rows = channels * SUBLANES
    bias = jnp.zeros((SUBLANES, channels), F32)
    for y in range(SUBLANES // 2):
        row = jnp.where(iota((SUBLANES, LANES), 0) == y, stat_ref[1], 0.0)
        bias += from_slots(row, slot_place(channels, x_local, y))
    bias_ref[...] = jnp.sum(bias, axis=0, keepdims=True) * scale
    spread = jnp.where(
        iota((rows, channels), 0) // SUBLANES == iota((rows, channels), 1), 1.0, 0.0
    )
    tall = jnp.dot(
        spread, weight_ref[...], precision=HIGHEST_PRECISION, preferred_element_type=F32
    )
    square = lax.dot_general(
        tall,
        spread,
        (((1,), (1,)), ((), ())),
        precision=HIGHEST_PRECISION,
        preferred_element_type=F32,
    )
    same = iota(square.shape, 0) % SUBLANES == iota(square.shape, 1) % SUBLANES
    high, low = split(jnp.where(same, square, 0.0))
    left = jnp.concatenate([high, high, low], axis=1)
    for x in range(x_local):
        right = jnp.concatenate([ghi_ref[x], glo_ref[x], ghi_ref[x]], axis=0)
        local_ref[:, x] = dot(left, right).reshape(channels, SUBLANES, LANES)


def inverse_kernel(places, r_ref, stat_ref, tyh_ref, tyl_ref, txh_ref, txl_ref, s_ref):
    y_local = SUBLANES // 2
    values = [jnp.concatenate([r_ref[p] for p in row], axis=0) for row in places]
    lane = iota(values[0].shape, 1)
    sign = jnp.where(lane < LANES // 2, -1.0, 1.0)
    wide = jnp.concatenate(values, axis=1)
    turned = [sign * pltpu.roll(value, LANES // 2, 1) for value in values]
    both = jnp.concatenate([wide, jnp.concatenate(turned, axis=1)], axis=0)
    along_y = product((tyh_ref[...], tyl_ref[...]), split(both))
    along_x = product_rows(split(along_y), (txh_ref[...], txl_ref[...]))
    slots = slot_mask(y_local)
    for g, row in enumerate(places):
        for k, p in enumerate(row):
            block = along_x[k * SUBLANES : (k + 1) * SUBLANES, g * LANES : (g + 1) * LANES]
            s_ref[p] = jnp.where(slots, stat_ref[0], block)


def result_kernel(scale, r_ref, hi_ref, lo_ref, local_ref, grad_hbm, point_ref, grad_ref, sems):
    channels, x_local = grad_ref.shape[:2]
    y_local = SUBLANES // 2
    rows = channels * SUBLANES
    tile = (channels, SUBLANES, LANES)
    values = r_ref[...].reshape(tile)
    turned = pltpu.roll(values, y_local, 1)
    sign = jnp.where(iota(tile, 2) % 2 == 0, 1.0, -1.0)
    upper = iota(tile, 1) < y_local
    halves = [
        jnp.where(upper, values, sign * turned).reshape(rows, LANES),
        jnp.where(upper, turned, sign * values).reshape(rows, LANES),
    ]
    highs = [half.astype(BF16).astype(F32) for half in halves]
    parts = [*highs, *(half - high for half, high in zip(halves, highs))]
    count = len(parts)
    width = LANES // count
    places = width // (2 * HL)
    parts = [part if k == 0 else pltpu.roll(part, k * width, 1) for k, part in enumerate(parts)]
    lane = iota((rows, LANES), 1) // width
    group = 2 * HL
    zeros = jnp.zeros((group, LANES), BF16)

    def rows_of(ref, part, first):
        blocks = []
        for k in range(places):
            at = part % 2 * LANES + (first + k) * group
            row = [zeros] * places
            row[k] = ref[at : at + group, :]
            blocks.append(jnp.concatenate(row, axis=1))
        return jnp.concatenate(blocks, axis=0)

    copies = []
    for index in range(x_local // places):
        first = index * places
        left = parts[0]
        for k in range(1, count):
            left = jnp.where(lane == (index + k) % count, parts[k], left)
        left = left.astype(BF16)
        order = [(k - index) % count for k in range(count)]
        right = [rows_of(ref, part, first) for ref in (hi_ref, lo_ref) for part in order]
        block = dot(jnp.concatenate([left, left], axis=1), jnp.concatenate(right, axis=0))
        for k in range(places):
            part = block[:, k * LANES : (k + 1) * LANES]
            x = first + k
            grad_ref[:, x] = part.reshape(tile) + local_ref[:, x]
            copies.append(
                pltpu.make_async_copy(grad_ref.at[:, x], grad_hbm.at[:, x], sems.at[x])
            )
            copies[-1].start()
    point = jnp.zeros(point_ref.shape, F32)
    for y in range(y_local):
        taken = r_ref[pl.ds(y, channels, stride=SUBLANES), :]
        point += from_slots(taken, slot_place(channels, x_local, y))
    point_ref[...] = point * scale
    for copy in copies:
        copy.wait()


def call(kernel, out_shape, name, vmem=16, **options):
    params = pltpu.CompilerParams(vmem_limit_bytes=vmem << 20)
    return pl.pallas_call(
        kernel, out_shape=out_shape, name=name, compiler_params=params, **options
    )


def held(count):
    return [pl.BlockSpec(memory_space=pltpu.VMEM)] * count


def to_tiles(array):
    lead, (rows, depth) = array.shape[:-2], array.shape[-2:]
    split_up = array.reshape(lead + (rows, depth // LANES, LANES))
    return jnp.swapaxes(split_up, -3, -2).reshape(lead + (SUBLANES, LANES))


def from_tiles(array, rows, depth):
    lead = array.shape[:-2]
    split_up = array.reshape(lead + (depth // LANES, rows, LANES))
    return jnp.swapaxes(split_up, -3, -2).reshape(lead + (rows, depth))


def transposed(inputs, pre_act, grad_out, point_weight, mode_weight):
    channels, x_local, y_local, depth = inputs.shape
    kx_local, ky_local, _, kz_count, pairs = mode_weight.shape
    x_devices = lax.axis_size("gx")
    y_devices = lax.axis_size("gy")
    devices = x_devices * y_devices
    hh_count = kz_count // HL
    cells = x_local * x_devices * y_local * y_devices * depth
    scale = 1.0 / math.sqrt(cells)
    axes = ("gx", "gy")
    order = exchange_order(x_devices, y_devices)
    places = by_device(order, x_devices)
    rows = channels * SUBLANES

    def struct(shape, kind=F32):
        return jax.ShapeDtypeStruct(shape, kind)

    def exchange(chunks):
        return lax.all_to_all(chunks, axes, 0, 0, axis_index_groups=[order])

    z_high, z_low = split_table(depth_table(depth, kz_count, x_local))
    tx = split_table(x_table(x_devices, x_local, kx_local))
    ty = split_table(y_table(y_devices, y_local, ky_local, hh_count))
    tyi = split_table(y_inverse_table(y_devices, y_local, ky_local, hh_count))
    spread = spread_table(channels)

    field_shape = (channels, x_local, SUBLANES, LANES)
    later = (z_high.T, z_low.T, *tx, *ty, *tyi, mode_weight)
    chunks, g_high, g_low, *later = call(
        functools.partial(grid_kernel, len(later)),
        (
            struct((channels, 2, SUBLANES, LANES)),
            struct((x_local, rows, LANES), BF16),
            struct((x_local, rows, LANES), BF16),
            *(struct(array.shape, array.dtype) for array in later),
        ),
        "grid",
        vmem=24,
        in_specs=[pl.BlockSpec(memory_space=pltpu.HBM)] * (3 + len(later)),
        out_specs=held(3 + len(later)),
        scratch_shapes=[
            *([pltpu.VMEM(field_shape, BF16)] * 3),
            pltpu.SemaphoreType.DMA((3, x_local)),
            pltpu.SemaphoreType.DMA((len(later),)),
        ],
    )(
        *(
            pltpu.with_memory_space_constraint(array, pltpu.HBM)
            for array in (
                to_tiles(inputs),
                to_tiles(pre_act),
                to_tiles(grad_out),
                *later,
            )
        )
    )
    z_turned, tx, ty, tyi, mode_weight = later[:2], later[2:4], later[4:6], later[6:8], later[8]
    planes = exchange(chunks)
    mode_rows_count = ky_local * 2 * hh_count
    chunks, stats = call(
        functools.partial(plane_kernel, places),
        (
            struct((devices, mode_rows_count, LANES)),
            struct((2, SUBLANES, LANES)),
        ),
        "plane",
        in_specs=held(5),
        out_specs=held(2),
    )(planes, *tx, *ty)
    local, bias_grad = call(
        functools.partial(local_kernel, scale),
        (struct(field_shape), struct((1, channels))),
        "local",
        in_specs=held(4),
        out_specs=held(2),
    )(point_weight, g_high, g_low, stats)
    modes = exchange(chunks)
    modes = modes.reshape(devices * mode_rows_count, LANES)
    chunks = call(
        functools.partial(back_kernel, cells, channels),
        struct((devices * SUBLANES, LANES)),
        "back",
        in_specs=held(2),
        out_specs=held(1)[0],
    )(modes, mode_weight)
    back = exchange(chunks.reshape(devices, SUBLANES, LANES))
    block = (kx_local, 1, 2, kz_count, pairs)
    mode_grad = call(
        functools.partial(outer_kernel, cells),
        struct(mode_weight.shape),
        "outer",
        grid=(ky_local,),
        in_specs=held(2),
        out_specs=pl.BlockSpec(block, lambda k: (0, k, 0, 0, 0)),
    )(modes, spread)
    chunks = call(
        functools.partial(inverse_kernel, places),
        struct((devices, SUBLANES, LANES)),
        "inverse",
        in_specs=held(6),
        out_specs=held(1)[0],
    )(back, stats, *tyi, *tx)
    near = exchange(chunks)
    grad, point_grad = call(
        functools.partial(result_kernel, scale),
        (struct(field_shape), struct((channels, channels))),
        "result",
        in_specs=held(4),
        out_specs=(pl.BlockSpec(memory_space=pltpu.HBM), held(1)[0]),
        scratch_shapes=[pltpu.VMEM(field_shape, F32), pltpu.SemaphoreType.DMA((x_local,))],
    )(near.reshape(rows, LANES), *z_turned, local)
    return (from_tiles(grad, y_local, depth), point_grad, bias_grad[0], mode_grad)


def one_channel_each(inputs, mode_weight):
    channels, x_local, y_local, depth = inputs.shape
    kx_local, ky_local, _, kz_count, _ = mode_weight.shape
    return (
        channels == lax.axis_size("gx") * lax.axis_size("gy")
        and LANES % channels == 0
        and depth == 2 * LANES
        and y_local * 2 == SUBLANES
        and kz_count == 2 * HL
        and ky_local * 2 == SUBLANES
        and x_local * 2 * HL == LANES
        and kx_local == x_local
        and x_local * y_local == channels
    )


def shards(inputs, pre_act, grad_out, point_weight, mode_weight):
    plan = transposed if one_channel_each(inputs, mode_weight) else partial_sums
    return plan(inputs, pre_act, grad_out, point_weight, mode_weight)


def solution(mesh):
    return jax.shard_map(
        shards,
        mesh=mesh,
        in_specs=(
            P(None, "gx", "gy", None),
            P(None, "gx", "gy", None),
            P(None, "gx", "gy", None),
            P(),
            P("gx", "gy", None, None, None),
        ),
        out_specs=(P(None, "gx", "gy", None), P(), P(), P("gx", "gy", None, None, None)),
        check_vma=False,
    )
```
